32 devices in a mesh: groups: 1, tensor: 16 (over z, y, core), replica: 2 (over x).
Axes of the slice: x: 2, y: 2, z: 4, core: 2. Of those that a mesh axis runs over, the one named last changes fastest.
Arguments:
- q_latent: bfloat16 [256, 1536], P(('groups', 'tensor', 'replica')), may hold values from -6 to 6
- q_gain: float32 [1536], replicated, may hold values from 0.25 to 1.75
- q_up: bfloat16 [1536, 12288], P(None, 'tensor'), may hold values from -0.15625 to 0.15625
- w_uk: bfloat16 [64, 128, 512], P('tensor'), may hold values from -0.5 to 0.5
- w_uv: bfloat16 [64, 512, 128], P('tensor'), may hold values from -1 to 1
- w_o: bfloat16 [8192, 7168], P('tensor', 'replica'), may hold values from -0.0625 to 0.0625
- new_kv: bfloat16 [256, 576], P(('groups', 'tensor', 'replica')), may hold values from -6 to 6
- latent_cache: bfloat16 [64, 1024, 576], P(('groups', 'tensor', 'replica')), may hold values from -64 to 64
- cache_len: int32 [64], P(('groups', 'tensor', 'replica')), may hold values from 128 to 1024, as said below
- draft_count: int32 [64], P(('groups', 'tensor', 'replica')), may hold values from 1 to 4, as said below
Outputs:
- attn_out: bfloat16 [256, 7168], P(('groups', 'tensor', 'replica'))
The draws below stay inside these ranges and needn't reach their ends.
Inputs may be any that keep to these rules, and one draw needn't show every extreme that they name: `cache_len`: some request of every draw uses all 1024 slots. The first draft_count rows of a request are in use; some request of every draw uses all 4.
All inputs are finite; a program needn't handle non-finite values.
Results may differ from the reference program's by a relative error of at most 0.024.
The reference program's roundings to bfloat16 on the way count: a program that leaves them out, or rounds other values in their place, can miss the bound.
Values may be sent and summed in bfloat16 or wider, within the bound.
No kernel may reach another device: no remote copies, remote signals or barrier semaphores. Data moves between devices by JAX's collectives and lax.ppermute only.
A program may use at most 64 MiB of HBM per device.

```python
import jax
import jax.numpy as jnp
from jax import lax

D = 7168
HEADS = 64
QLAT = 1536
LATENT = 512
ROPE = 64
NOPE = 128
VDIM = 128
CACHE = 1024
DRAFT = 4
KVW = 576
QKD = 192
REQS = 64
TOKENS = 256
N_TENSOR = 16


def draw_latent_cache(key, part):
    base_key = jax.random.fold_in(jax.random.fold_in(key, 11), 0)
    stored = jax.random.normal(base_key, (REQS, CACHE, KVW), jnp.float32)
    return jnp.clip(stored, -64.0, 64.0).astype(jnp.bfloat16)


def draw_cache_len(key, part):
    length_key, offset_key = jax.random.split(jax.random.fold_in(key, 23))
    lengths = jax.random.randint(length_key, (REQS,), CACHE // 8, CACHE + 1)
    offset = jax.random.randint(offset_key, (), 0, 7)
    filled = jnp.arange(REQS) % 7 == offset
    return jnp.where(filled, CACHE, lengths).astype(jnp.int32)


def draw_draft_count(key, part):
    count_key, offset_key = jax.random.split(jax.random.fold_in(key, 37))
    counts = jax.random.randint(count_key, (REQS,), 1, DRAFT + 1)
    offset = jax.random.randint(offset_key, (), 0, 5)
    filled = jnp.arange(REQS) % 5 == offset
    return jnp.where(filled, DRAFT, counts).astype(jnp.int32)


def shard_levels(rng, extent, shards, least, largest):
    def one(position, parts):
        draws = jax.random.uniform(jax.random.fold_in(jax.random.fold_in(rng, 6), position), (parts,), jnp.float32, least / len(shards), largest / len(shards))
        return jnp.repeat(jnp.exp(draws), extent[position] // parts).reshape((-1,) + (1,) * (len(extent) - position - 1))

    factor_of = one(*shards[0])
    for cut in shards[1:]:
        factor_of = factor_of * one(*cut)
    return factor_of


def bell_draw(rng, shape, width, bound, cuts=(), dtype=jnp.bfloat16):
    values = width * jax.random.normal(rng, shape, jnp.float32)
    if cuts:
        values = values * shard_levels(rng, shape, cuts, -0.22, 0.18)
    return jnp.clip(values, -bound, bound).astype(dtype)


def setup_inputs(seed: int = 0, part: int = 0) -> dict:
    streams_of = jax.random.split(jax.random.key(seed), 11)
    part_keys = jax.random.split(jax.random.fold_in(streams_of[10], part), 11)
    return {
        "q_latent": bell_draw(part_keys[0], (TOKENS, QLAT), 1.0, 6.0, ((0, 32),)),
        "q_gain": jnp.clip(1.0 + 0.15 * jax.random.normal(streams_of[1], (QLAT,), jnp.float32), 0.25, 1.75),
        "q_up": bell_draw(streams_of[2], (QLAT, HEADS * QKD), QLAT ** -0.5, 0.15625, ((1, 16),)),
        "w_uk": bell_draw(streams_of[3], (HEADS, NOPE, LATENT), NOPE ** -0.5, 0.5, ((0, 16),)),
        "w_uv": bell_draw(streams_of[4], (HEADS, LATENT, VDIM), (LATENT // 16) ** -0.5, 1.0, ((0, 16),)),
        "w_o": bell_draw(streams_of[5], (HEADS * VDIM, D), (HEADS * VDIM) ** -0.5, 0.0625, ((0, 16), (1, 2))),
        "new_kv": bell_draw(part_keys[6], (TOKENS, KVW), 1.0, 6.0, ((0, 32),)),
        "latent_cache": draw_latent_cache(jax.random.fold_in(jax.random.fold_in(streams_of[10], part), 71), part),
        "cache_len": draw_cache_len(jax.random.fold_in(jax.random.fold_in(streams_of[10], part), 71), part),
        "draft_count": draw_draft_count(jax.random.fold_in(jax.random.fold_in(streams_of[10], part), 71), part),
    }


rms_eps = 1e-06
rope_base = 50000.0

def normalize(rows_in, gain_row):
    values_f = rows_in.astype(jnp.float32)
    scaled = values_f * lax.rsqrt(lax.optimization_barrier(jnp.mean(values_f * values_f, axis=-1, keepdims=True)) + rms_eps)
    return (scaled * gain_row).astype(jnp.bfloat16)

def rotate(rope_part, positions):
    half_width = rope_part.shape[-1] // 2
    frequency = rope_base ** (-(jnp.arange(half_width).astype(jnp.float32) * 2.0 / rope_part.shape[-1]))
    angles = positions[:, None, None] * frequency
    cosine = jnp.cos(angles)
    sine = jnp.sin(angles)
    widened = rope_part.astype(jnp.float32)
    first_half = widened[..., :half_width]
    second_half = widened[..., half_width:]
    turned = jnp.concatenate([first_half * cosine - second_half * sine, second_half * cosine + first_half * sine], axis=-1)
    return turned.astype(jnp.bfloat16)

def attend(query_rows, new_rows, cache_rows, length, draft_total):
    queries = query_rows.reshape(-1, query_rows.shape[-1])
    contract = (((1,), (1,)), ((), ()))
    score_scale = (NOPE + ROPE) ** (-0.5)
    cache_scores = lax.dot_general(queries, cache_rows, contract, preferred_element_type=jnp.float32) * score_scale
    new_scores = lax.dot_general(queries, new_rows, contract, preferred_element_type=jnp.float32) * score_scale
    row_draft = jnp.arange(queries.shape[0]) // query_rows.shape[1]
    cache_seen = jnp.arange(cache_rows.shape[0]) < length
    new_seen = jnp.arange(new_rows.shape[0])[None, :] <= row_draft[:, None]
    cache_scores = jnp.where(cache_seen[None, :], cache_scores, -jnp.inf)
    new_scores = jnp.where(new_seen, new_scores, -jnp.inf)
    row_peak = jnp.maximum(lax.optimization_barrier(jnp.max(cache_scores, axis=1)), lax.optimization_barrier(jnp.max(new_scores, axis=1)))[:, None]
    cache_exp = jnp.exp(cache_scores - row_peak)
    new_exp = jnp.exp(new_scores - row_peak)
    denominator = lax.optimization_barrier(jnp.sum(cache_exp, axis=1, keepdims=True)) + lax.optimization_barrier(jnp.sum(new_exp, axis=1, keepdims=True))
    cache_weights = (cache_exp / denominator).astype(jnp.bfloat16)
    new_weights = (new_exp / denominator).astype(jnp.bfloat16)
    latent_mix = jnp.dot(cache_weights, cache_rows[:, :LATENT], preferred_element_type=jnp.float32)
    latent_mix = latent_mix + jnp.dot(new_weights, new_rows[:, :LATENT], preferred_element_type=jnp.float32)
    latent_mix = jnp.where((row_draft < draft_total)[:, None], latent_mix, 0.0).astype(jnp.bfloat16)
    return latent_mix.reshape(query_rows.shape[0], query_rows.shape[1], LATENT)

def reference(q_latent, q_gain, q_up, w_uk, w_uv, w_o, new_kv, latent_cache, cache_len, draft_count):
    normed = normalize(q_latent, q_gain)
    query_full = jnp.dot(normed, q_up, preferred_element_type=jnp.float32).astype(jnp.bfloat16)
    query_full = query_full.reshape(TOKENS, HEADS, QKD)
    absorbed = jnp.einsum('thn,hnl->thl', query_full[..., :NOPE].astype(jnp.float32), w_uk.astype(jnp.float32)).astype(jnp.bfloat16)
    row_length = jnp.broadcast_to(cache_len[:, None], (REQS, DRAFT)).reshape(-1)
    positions = (row_length + jnp.arange(TOKENS) % DRAFT).astype(jnp.float32)
    rotated = rotate(query_full[..., NOPE:], positions)
    query = jnp.concatenate([absorbed, rotated], axis=-1)

    def one_request(packed):
        return attend(packed[0], packed[1], packed[2], packed[3], packed[4])
    latent_out = lax.map(one_request, (query.reshape(REQS, DRAFT, HEADS, KVW), new_kv.reshape(REQS, DRAFT, KVW), latent_cache, cache_len, draft_count))
    latent_out = latent_out.reshape(TOKENS, HEADS, LATENT)
    head_values = jnp.einsum('thl,hlv->thv', latent_out.astype(jnp.float32), w_uv.astype(jnp.float32)).astype(jnp.bfloat16)
    group_width = HEADS // N_TENSOR * VDIM
    grouped_values = jnp.swapaxes(head_values.reshape(TOKENS, N_TENSOR, group_width), 0, 1)
    grouped_weights = w_o.reshape(N_TENSOR, group_width, D)

    def add_group(running, pair):
        contribution = jnp.dot(pair[0], pair[1], preferred_element_type=jnp.float32).astype(jnp.bfloat16)
        contribution = lax.optimization_barrier(contribution)
        return (running + contribution.astype(jnp.float32), None)
    running, unused = lax.scan(add_group, jnp.zeros((TOKENS, D), jnp.float32), (grouped_values, grouped_weights))
    return running.astype(jnp.bfloat16)
```

```python
import functools

import jax
import jax.numpy as jnp
from jax import lax
from jax.experimental import pallas as pl
from jax.experimental.pallas import tpu as pltpu
from jax.sharding import PartitionSpec as P

LATENT = 512
ROPE = 64
NOPE = 128
VDIM = 128
QKD = NOPE + ROPE
LANES = 128

rms_eps = 1e-06
rope_base = 50000.0

VMEM = pltpu.MemorySpace.VMEM
SMEM = pltpu.MemorySpace.SMEM
bf16 = jnp.bfloat16
f32 = jnp.float32


def vmem_spec():
    return pl.BlockSpec(memory_space=VMEM)


def smem_spec():
    return pl.BlockSpec(memory_space=SMEM)


def mm(a, b):
    return jnp.dot(a, b, preferred_element_type=f32)


def mm_nt(a, b):
    return lax.dot_general(a, b, (((1,), (1,)), ((), ())), preferred_element_type=f32)


def query_kernel(reqs, drafts, heads, me_ref, x_ref, gain_ref, up_ref, uk_ref, out_ref):
    owners = out_ref.shape[0]
    rows_dev = reqs * drafts
    hd = heads * drafts
    x = x_ref[...].astype(f32)
    scaled = x * lax.rsqrt(jnp.mean(x * x, axis=-1, keepdims=True) + rms_eps)
    normed = (scaled * gain_ref[...]).astype(bf16)
    full = mm(normed, up_ref[...]).astype(bf16)
    count = owners * reqs * hd
    shape = (count, owners * rows_dev)
    n = lax.broadcasted_iota(jnp.int32, shape, 0)
    m = lax.broadcasted_iota(jnp.int32, shape, 1)
    target = n // (reqs * hd)
    local = (n // hd) % reqs * drafts + n % drafts
    source = m // rows_dev
    spread = jnp.where((target == (source ^ me_ref[0])) & (local == m % rows_dev), 1.0, 0.0)
    wide = mm(spread.astype(bf16), full)
    row_head = (lax.broadcasted_iota(jnp.int32, (count, 1), 0) // drafts) % heads
    absorbed = None
    rope = None
    for h in range(heads):
        mine = row_head == h
        nope_h = jnp.where(mine, wide[:, h * QKD : h * QKD + NOPE], 0.0).astype(bf16)
        part = mm(nope_h, uk_ref[h])
        absorbed = part if absorbed is None else absorbed + part
        rope_h = jnp.where(mine, wide[:, h * QKD + NOPE : (h + 1) * QKD], 0.0)
        rope = rope_h if rope is None else rope + rope_h
    chunks = LATENT // LANES
    absorbed = absorbed.reshape(owners, reqs, hd, LATENT)
    rope = rope.reshape(owners, reqs, hd, ROPE)
    for q in range(reqs):
        for c in range(chunks):
            at = (q * chunks + c) * hd
            out_ref[:, at : at + hd, :] = absorbed[:, q, :, c * LANES : (c + 1) * LANES].astype(bf16)
    per = LANES // ROPE
    for b in range(reqs // per):
        at = (reqs * chunks + b) * hd
        both = jnp.concatenate([rope[:, b * per + i] for i in range(per)], axis=-1)
        out_ref[:, at : at + hd, :] = both.astype(bf16)


def attend_kernel(reqs, drafts, heads, len_ref, count_ref, q_ref, cos_ref, sin_ref, new_ref, cache_ref, out_ref):
    owners = q_ref.shape[0]
    hd = heads * drafts
    count = owners * hd
    chunks = LATENT // LANES
    per = LANES // ROPE
    slots = cache_ref.shape[2]
    scale = QKD ** (-0.5)
    rotated = []
    for b in range(reqs // per):
        at = (reqs * chunks + b) * hd
        x = q_ref[:, at : at + hd, :].astype(f32).reshape(count, LANES)
        lane = lax.broadcasted_iota(jnp.int32, x.shape, 1) % ROPE
        half = ROPE // 2
        other = jnp.where(lane < half, pltpu.roll(x, LANES - half, 1), pltpu.roll(x, half, 1))
        x = x.reshape(owners, hd, LANES) * cos_ref[b] + other.reshape(owners, hd, LANES) * sin_ref[b]
        x = x.astype(bf16).reshape(count, LANES)
        rotated += [x[:, i * ROPE : (i + 1) * ROPE] for i in range(per)]
    draft = lax.broadcasted_iota(jnp.int32, (count, 1), 0) % drafts
    new_at = lax.broadcasted_iota(jnp.int32, (count, new_ref.shape[0]), 1)
    slot = lax.broadcasted_iota(jnp.int32, (1, slots), 1)
    for q in range(reqs):
        absorbed = jnp.concatenate(
            [
                q_ref[:, (q * chunks + c) * hd : (q * chunks + c + 1) * hd, :].reshape(count, LANES)
                for c in range(chunks)
            ],
            axis=-1,
        )
        keys = cache_ref[q]
        rows = new_ref[...]
        score = (mm(absorbed, keys[:LATENT]) + mm(rotated[q], keys[LATENT:])) * scale
        fresh = (mm_nt(absorbed, rows[:, :LATENT]) + mm_nt(rotated[q], rows[:, LATENT:])) * scale
        score = jnp.where(slot < len_ref[q], score, -jnp.inf)
        seen = (new_at >= q * drafts) & (new_at - q * drafts <= draft)
        fresh = jnp.where(seen, fresh, -jnp.inf)
        peak = jnp.maximum(
            jnp.max(score, axis=1, keepdims=True), jnp.max(fresh, axis=1, keepdims=True)
        )
        score = jnp.exp(score - peak)
        fresh = jnp.exp(fresh - peak)
        total = jnp.sum(score, axis=1, keepdims=True) + jnp.sum(fresh, axis=1, keepdims=True)
        inverse = 1.0 / total
        mix = mm_nt((score * inverse).astype(bf16), keys[:LATENT])
        mix = mix + mm((fresh * inverse).astype(bf16), rows[:, :LATENT])
        mix = jnp.where(draft < count_ref[q], mix, 0.0).astype(bf16)
        out_ref[:, q * hd : (q + 1) * hd, :] = mix.reshape(owners, hd, LATENT)


def value_kernel(reqs, drafts, heads, latent_ref, uv_ref, out_ref):
    owners = latent_ref.shape[0]
    hd = heads * drafts
    rows = owners * reqs * drafts
    latent = latent_ref[...].reshape(owners * reqs * hd, LATENT)
    shape = (rows, owners * reqs * hd)
    m = lax.broadcasted_iota(jnp.int32, shape, 0)
    n = lax.broadcasted_iota(jnp.int32, shape, 1)
    wanted = (m // drafts) * hd + m % drafts
    for h in range(heads):
        pick = jnp.where(n == wanted + h * drafts, 1.0, 0.0).astype(bf16)
        mine = mm(pick, latent).astype(bf16)
        out_ref[:, h * VDIM : (h + 1) * VDIM] = mm(mine, uv_ref[h]).astype(bf16)


def output_kernel(core_ref, own_ref, other_ref, w_own_ref, w_other_ref, out_ref):
    out_ref[...] = (mm(own_ref[...], w_own_ref[...]) + mm(other_ref[...], w_other_ref[...])).astype(bf16)


def sum_kernel(replicas, pairs, x_ref, out_ref):
    width = x_ref.shape[-1]
    for r in range(replicas):
        for c in range(2):
            total = None
            for p in range(pairs):
                part = x_ref[(r * pairs + p) * 2 + c].astype(f32)
                total = part if total is None else total + part
            at = (r * 2 + c) * width
            out_ref[:, at : at + width] = total.astype(bf16)


def step(x, axis, size, k):
    return lax.ppermute(x, axis, [(i, i ^ k) for i in range(size)])


def shards(q_latent, q_gain, q_up, w_uk, w_uv, w_o, new_kv, latent_cache, cache_len, draft_count):
    rows_dev, qlat = q_latent.shape
    owners = lax.axis_size("tensor")
    replicas = lax.axis_size("replica")
    heads = w_uk.shape[0]
    reqs = cache_len.shape[0]
    drafts = rows_dev // reqs
    hd = heads * drafts
    me = lax.axis_index("tensor")
    core = me % 2

    half = w_o.shape[1] // 2
    away = lax.dynamic_slice_in_dim(w_o, (1 - core) * half, half, axis=1)
    w_other = step(away, "tensor", owners, 1)

    inner = min(4, owners)
    blocks = [q_latent] + [step(q_latent, "tensor", owners, k) for k in range(inner, owners, inner)]
    rows = jnp.stack(blocks)
    size = inner // 2
    rows = rows[:, None]
    while size:
        rows = jnp.concatenate([rows, step(rows, "tensor", owners, size)], axis=1)
        size //= 2
    order = [0]
    size = inner // 2
    while size:
        order = order + [o ^ size for o in order]
        size //= 2
    inverse = [order.index(i) for i in range(inner)]
    rows = jnp.stack([rows[:, i] for i in inverse], axis=1)
    rows = rows.reshape(owners * rows_dev, qlat)

    chunks = LATENT // LANES
    packed = (reqs * chunks + reqs * ROPE // LANES) * hd
    params = pltpu.CompilerParams(vmem_limit_bytes=32 * 1024 * 1024)
    queries = pl.pallas_call(
        functools.partial(query_kernel, reqs, drafts, heads),
        out_shape=jax.ShapeDtypeStruct((owners, packed, LANES), bf16),
        in_specs=[smem_spec()] + [vmem_spec()] * 4,
        out_specs=vmem_spec(),
        compiler_params=params,
        name="query",
    )(me[None].astype(jnp.int32), rows, q_gain[None, :], q_up, w_uk)
    arrived = lax.all_to_all(queries, "tensor", split_axis=0, concat_axis=0, tiled=True)

    frequency = rope_base ** (-(jnp.arange(ROPE // 2).astype(f32) * 2.0 / ROPE))
    positions = (cache_len[:, None] + jnp.arange(drafts)[None, :]).astype(f32)
    angles = positions[:, :, None] * frequency
    per = LANES // ROPE

    def table(first, second):
        lanes = jnp.concatenate([first, second], axis=-1)
        lanes = lanes.reshape(reqs // per, per, drafts, ROPE)
        lanes = jnp.swapaxes(lanes, 1, 2).reshape(reqs // per, 1, drafts, LANES)
        return jnp.broadcast_to(lanes, (reqs // per, heads, drafts, LANES)).reshape(reqs // per, hd, LANES)

    cosine = jnp.cos(angles)
    sine = jnp.sin(angles)
    latent = pl.pallas_call(
        functools.partial(attend_kernel, reqs, drafts, heads),
        out_shape=jax.ShapeDtypeStruct((owners, reqs * hd, LATENT), bf16),
        in_specs=[smem_spec()] * 2 + [vmem_spec()] * 5,
        out_specs=vmem_spec(),
        compiler_params=params,
        name="attend",
    )(cache_len, draft_count, arrived, table(cosine, cosine), table(-sine, sine), new_kv, jnp.swapaxes(latent_cache, 1, 2))
    returned = lax.all_to_all(latent, "tensor", split_axis=0, concat_axis=0, tiled=True)

    values = pl.pallas_call(
        functools.partial(value_kernel, reqs, drafts, heads),
        out_shape=jax.ShapeDtypeStruct((owners * rows_dev, heads * VDIM), bf16),
        in_specs=[vmem_spec()] * 2,
        out_specs=vmem_spec(),
        compiler_params=params,
        name="values",
    )(returned, w_uv)
    own = lax.all_gather(values, "replica", axis=0, tiled=True)
    other = step(own, "tensor", owners, 1)

    total_rows = own.shape[0]
    tile = half
    for t in (256, 128):
        if half % t == 0:
            tile = t
            break
    tiles = half // tile
    place = core if half % LANES == 0 else jnp.zeros_like(core)
    w_own = w_o if half % LANES == 0 else lax.dynamic_slice_in_dim(w_o, core * half, half, axis=1)
    depth = own.shape[1]
    product = pl.pallas_call(
        output_kernel,
        out_shape=jax.ShapeDtypeStruct((total_rows, half), bf16),
        grid_spec=pltpu.PrefetchScalarGridSpec(
            num_scalar_prefetch=1,
            grid=(tiles,),
            in_specs=[
                pl.BlockSpec((total_rows, depth), lambda i, c: (0, 0)),
                pl.BlockSpec((total_rows, depth), lambda i, c: (0, 0)),
                pl.BlockSpec((depth, tile), lambda i, c: (0, c[0] * tiles + i)),
                pl.BlockSpec((depth, tile), lambda i, c: (0, i)),
            ],
            out_specs=pl.BlockSpec((total_rows, tile), lambda i, c: (0, i)),
        ),
        compiler_params=params,
        name="output",
    )(place[None].astype(jnp.int32), own, other, w_own, w_other)
    product = product.reshape(replicas * owners, rows_dev, half)
    placed = lax.all_to_all(product, ("replica", "tensor"), split_axis=0, concat_axis=0, tiled=True)
    return pl.pallas_call(
        functools.partial(sum_kernel, replicas, owners // 2),
        out_shape=jax.ShapeDtypeStruct((rows_dev, replicas * 2 * half), bf16),
        in_specs=[vmem_spec()],
        out_specs=vmem_spec(),
        compiler_params=params,
        name="combine",
    )(placed)


def solution(mesh):
    rows = ("groups", "tensor", "replica")
    return jax.shard_map(
        shards,
        mesh=mesh,
        in_specs=(
            P(rows, None),
            P(),
            P(None, "tensor"),
            P("tensor", None, None),
            P("tensor", None, None),
            P("tensor", "replica"),
            P(rows, None),
            P(rows, None, None),
            P(rows),
            P(rows),
        ),
        out_specs=P(rows, None),
        check_vma=False,
    )
```

```python
import functools

import jax
import jax.numpy as jnp
from jax import lax
from jax.experimental import pallas as pl
from jax.experimental.pallas import tpu as pltpu
from jax.sharding import PartitionSpec as P

LATENT = 512
ROPE = 64
NOPE = 128
VDIM = 128
QKD = NOPE + ROPE
LANES = 128

rms_eps = 1e-06
rope_base = 50000.0

VMEM = pltpu.MemorySpace.VMEM
SMEM = pltpu.MemorySpace.SMEM
bf16 = jnp.bfloat16
f32 = jnp.float32


def vmem_spec():
    return pl.BlockSpec(memory_space=VMEM)


def smem_spec():
    return pl.BlockSpec(memory_space=SMEM)


def mm(a, b):
    return jnp.dot(a, b, preferred_element_type=f32)


def mm_nt(a, b):
    return lax.dot_general(a, b, (((1,), (1,)), ((), ())), preferred_element_type=f32)


def fetch_kernel(place_ref, *refs):
    count = (len(refs) - 1) // 2
    sems = refs[-1]
    copies = []
    for i in range(count):
        source, target = refs[i], refs[count + i]
        width = target.shape[-1]
        if source.shape[-1] != width:
            source = source.at[:, pl.ds(pl.multiple_of(place_ref[0] * width, LANES), width)]
        copies.append(pltpu.make_async_copy(source, target, sems.at[i]))
        copies[-1].start()
    for copy in copies:
        copy.wait()


def fetch(place, arrays, shapes, name):
    moved = sum(2 * 2 * shape[0] * shape[1] for shape in shapes)
    return pl.pallas_call(
        fetch_kernel,
        out_shape=[pltpu.VMEM(shape, bf16) for shape in shapes],
        in_specs=[smem_spec()] + [pl.BlockSpec(memory_space=pltpu.MemorySpace.HBM)] * len(arrays),
        out_specs=[vmem_spec()] * len(arrays),
        scratch_shapes=[pltpu.SemaphoreType.DMA((len(arrays),))],
        compiler_params=pltpu.CompilerParams(vmem_limit_bytes=1024 * 1024),
        cost_estimate=pl.CostEstimate(flops=0, bytes_accessed=moved, transcendentals=0),
        name=name,
    )(place, *arrays)


def query_kernel(reqs, drafts, heads, place_ref, *refs):
    *x_refs, gain_ref, up_ref, uk_ref, out_ref = refs
    owners = out_ref.shape[0]
    rows_dev = reqs * drafts
    hd = heads * drafts
    x = jnp.concatenate([x_ref[...].astype(f32) for x_ref in x_refs], axis=0)
    scaled = x * lax.rsqrt(jnp.mean(x * x, axis=-1, keepdims=True) + rms_eps)
    normed = (scaled * gain_ref[...][None, :]).astype(bf16)
    full = mm(normed, up_ref[...]).astype(bf16)
    count = owners * reqs * hd
    shape = (count, owners * rows_dev)
    n = lax.broadcasted_iota(jnp.int32, shape, 0)
    m = lax.broadcasted_iota(jnp.int32, shape, 1)
    target = n // (reqs * hd)
    local = (n // hd) % reqs * drafts + n % drafts
    block = m // rows_dev
    distance = jnp.zeros_like(block)
    bit = owners // 2
    while bit:
        distance = distance + block % 2 * bit
        block = block // 2
        bit //= 2
    spread = jnp.where((target == (distance ^ place_ref[2])) & (local == m % rows_dev), 1.0, 0.0)
    wide = mm(spread.astype(bf16), full)
    row_head = (lax.broadcasted_iota(jnp.int32, (count, 1), 0) // drafts) % heads
    absorbed = None
    rope = None
    for h in range(heads):
        mine = row_head == h
        nope_h = jnp.where(mine, wide[:, h * QKD : h * QKD + NOPE], 0.0).astype(bf16)
        part = mm(nope_h, uk_ref[h * NOPE : (h + 1) * NOPE])
        absorbed = part if absorbed is None else absorbed + part
        rope_h = jnp.where(mine, wide[:, h * QKD + NOPE : (h + 1) * QKD], 0.0)
        rope = rope_h if rope is None else rope + rope_h
    chunks = LATENT // LANES
    absorbed = absorbed.reshape(owners, reqs, hd, LATENT)
    rope = rope.reshape(owners, reqs, hd, ROPE)
    for q in range(reqs):
        for c in range(chunks):
            at = (q * chunks + c) * hd
            out_ref[:, at : at + hd, :] = absorbed[:, q, :, c * LANES : (c + 1) * LANES].astype(bf16)
    per = LANES // ROPE
    for b in range(reqs // per):
        at = (reqs * chunks + b) * hd
        both = jnp.concatenate([rope[:, b * per + i] for i in range(per)], axis=-1)
        out_ref[:, at : at + hd, :] = both.astype(bf16)


def attend_kernel(reqs, drafts, heads, len_ref, count_ref, q_ref, cos_ref, sin_ref, new_ref, cache_ref, out_ref):
    owners = q_ref.shape[0]
    hd = heads * drafts
    count = owners * hd
    chunks = LATENT // LANES
    per = LANES // ROPE
    slots = cache_ref.shape[2]
    scale = QKD ** (-0.5)
    rotated = []
    for b in range(reqs // per):
        at = (reqs * chunks + b) * hd
        x = q_ref[:, at : at + hd, :].astype(f32).reshape(count, LANES)
        lane = lax.broadcasted_iota(jnp.int32, x.shape, 1) % ROPE
        half = ROPE // 2
        other = jnp.where(lane < half, pltpu.roll(x, LANES - half, 1), pltpu.roll(x, half, 1))
        x = x.reshape(owners, hd, LANES) * cos_ref[b] + other.reshape(owners, hd, LANES) * sin_ref[b]
        x = x.astype(bf16).reshape(count, LANES)
        rotated += [x[:, i * ROPE : (i + 1) * ROPE] for i in range(per)]
    draft = lax.broadcasted_iota(jnp.int32, (count, 1), 0) % drafts
    new_at = lax.broadcasted_iota(jnp.int32, (count, new_ref.shape[0]), 1)
    slot = lax.broadcasted_iota(jnp.int32, (1, slots), 1)
    for q in range(reqs):
        absorbed = jnp.concatenate(
            [
                q_ref[:, (q * chunks + c) * hd : (q * chunks + c + 1) * hd, :].reshape(count, LANES)
                for c in range(chunks)
            ],
            axis=-1,
        )
        keys = cache_ref[q]
        rows = new_ref[...]
        score = (mm(absorbed, keys[:LATENT]) + mm(rotated[q], keys[LATENT:])) * scale
        fresh = (mm_nt(absorbed, rows[:, :LATENT]) + mm_nt(rotated[q], rows[:, LATENT:])) * scale
        score = jnp.where(slot < len_ref[q], score, -jnp.inf)
        seen = (new_at >= q * drafts) & (new_at - q * drafts <= draft)
        fresh = jnp.where(seen, fresh, -jnp.inf)
        peak = jnp.maximum(
            jnp.max(score, axis=1, keepdims=True), jnp.max(fresh, axis=1, keepdims=True)
        )
        score = jnp.exp(score - peak)
        fresh = jnp.exp(fresh - peak)
        total = jnp.sum(score, axis=1, keepdims=True) + jnp.sum(fresh, axis=1, keepdims=True)
        inverse = 1.0 / total
        mix = mm_nt((score * inverse).astype(bf16), keys[:LATENT])
        mix = mix + mm((fresh * inverse).astype(bf16), rows[:, :LATENT])
        mix = jnp.where(draft < count_ref[q], mix, 0.0).astype(bf16)
        out_ref[:, q * hd : (q + 1) * hd, :] = mix.reshape(owners, hd, LATENT)


def value_kernel(reqs, drafts, heads, latent_ref, uv_ref, out_ref):
    owners = latent_ref.shape[0]
    hd = heads * drafts
    rows = owners * reqs * drafts
    latent = latent_ref[...].reshape(owners * reqs * hd, LATENT)
    shape = (rows, owners * reqs * hd)
    m = lax.broadcasted_iota(jnp.int32, shape, 0)
    n = lax.broadcasted_iota(jnp.int32, shape, 1)
    wanted = (m // drafts) * hd + m % drafts
    for h in range(heads):
        pick = jnp.where(n == wanted + h * drafts, 1.0, 0.0).astype(bf16)
        mine = mm(pick, latent).astype(bf16)
        out_ref[:, h * VDIM : (h + 1) * VDIM] = mm(mine, uv_ref[h]).astype(bf16)


def output_kernel(place_ref, *refs):
    *value_refs, w_own_ref, w_other_ref, out_ref = refs
    replicas, rows, half = out_ref.shape
    own = jnp.concatenate([ref[...] for ref in value_refs[:replicas]], axis=0)
    other = jnp.concatenate([ref[...] for ref in value_refs[replicas:]], axis=0)
    tile = 256 if half % 256 == 0 else half
    for at in range(0, half, tile):
        part = mm(own, w_own_ref[:, at : at + tile]) + mm(other, w_other_ref[:, at : at + tile])
        part = part.astype(bf16)
        for k in range(replicas):
            out_ref[place_ref[1] ^ k, :, at : at + tile] = part[k * rows : (k + 1) * rows]


def sum_kernel(replicas, pairs, x_ref, out_ref):
    width = x_ref.shape[-1]
    for r in range(replicas):
        for c in range(2):
            total = None
            for p in range(pairs):
                part = x_ref[(r * pairs + p) * 2 + c].astype(f32)
                total = part if total is None else total + part
            at = (r * 2 + c) * width
            out_ref[:, at : at + width] = total.astype(bf16)


def step(x, axis, size, k):
    return lax.ppermute(x, axis, [(i, i ^ k) for i in range(size)])


def shards(q_latent, q_gain, q_up, w_uk, w_uv, w_o, new_kv, latent_cache, cache_len, draft_count):
    rows_dev, qlat = q_latent.shape
    owners = lax.axis_size("tensor")
    replicas = lax.axis_size("replica")
    heads = w_uk.shape[0]
    reqs = cache_len.shape[0]
    drafts = rows_dev // reqs
    hd = heads * drafts
    me = lax.axis_index("tensor")
    core = me % 2

    half = w_o.shape[1] // 2
    away = lax.dynamic_slice_in_dim(w_o, (1 - core) * half, half, axis=1)
    w_other = step(away, "tensor", owners, 1)

    place = jnp.stack([core, lax.axis_index("replica"), me]).astype(jnp.int32)
    w_uk = w_uk.reshape(heads * NOPE, LATENT)
    up_near, uk_near = fetch(place, (q_up, w_uk), (q_up.shape, w_uk.shape), "near_query")

    rows = q_latent
    bit = owners // 2
    while bit > 2:
        rows = jnp.concatenate([rows, step(rows, "tensor", owners, bit)], axis=0)
        bit //= 2
    parts = [rows]
    while bit:
        parts = parts + [step(part, "tensor", owners, bit) for part in parts]
        bit //= 2

    chunks = LATENT // LANES
    packed = (reqs * chunks + reqs * ROPE // LANES) * hd
    params = pltpu.CompilerParams(vmem_limit_bytes=32 * 1024 * 1024)
    queries = pl.pallas_call(
        functools.partial(query_kernel, reqs, drafts, heads),
        out_shape=jax.ShapeDtypeStruct((owners, packed, LANES), bf16),
        in_specs=[smem_spec()] + [vmem_spec()] * (len(parts) + 3),
        out_specs=vmem_spec(),
        compiler_params=params,
        name="query",
    )(place, *parts, q_gain, up_near, uk_near)
    arrived = lax.all_to_all(queries, "tensor", split_axis=0, concat_axis=0, tiled=True)

    frequency = rope_base ** (-(jnp.arange(ROPE // 2).astype(f32) * 2.0 / ROPE))
    positions = (cache_len[:, None] + jnp.arange(drafts)[None, :]).astype(f32)
    angles = positions[:, :, None] * frequency
    per = LANES // ROPE

    def table(first, second):
        lanes = jnp.concatenate([first, second], axis=-1)
        lanes = lanes.reshape(reqs // per, per, drafts, ROPE)
        lanes = jnp.swapaxes(lanes, 1, 2).reshape(reqs // per, 1, drafts, LANES)
        return jnp.broadcast_to(lanes, (reqs // per, heads, drafts, LANES)).reshape(reqs // per, hd, LANES)

    cosine = jnp.cos(angles)
    sine = jnp.sin(angles)
    latent = pl.pallas_call(
        functools.partial(attend_kernel, reqs, drafts, heads),
        out_shape=jax.ShapeDtypeStruct((owners, reqs * hd, LATENT), bf16),
        in_specs=[smem_spec()] * 2 + [vmem_spec()] * 5,
        out_specs=vmem_spec(),
        compiler_params=params,
        name="attend",
    )(cache_len, draft_count, arrived, table(cosine, cosine), table(-sine, sine), new_kv, jnp.swapaxes(latent_cache, 1, 2))
    returned = lax.all_to_all(latent, "tensor", split_axis=0, concat_axis=0, tiled=True)

    values = pl.pallas_call(
        functools.partial(value_kernel, reqs, drafts, heads),
        out_shape=jax.ShapeDtypeStruct((owners * rows_dev, heads * VDIM), bf16),
        in_specs=[vmem_spec()] * 2,
        out_specs=vmem_spec(),
        compiler_params=params,
        name="values",
    )(returned, w_uv)
    own = [values] + [step(values, "replica", replicas, k) for k in range(1, replicas)]
    other = [step(piece, "tensor", owners, 1) for piece in own]

    w_own = w_o
    if half % LANES:
        w_own = lax.dynamic_slice_in_dim(w_o, core * half, half, axis=1)
    w_own, w_other = fetch(place, (w_own, w_other), (w_other.shape,) * 2, "near_output")
    product = pl.pallas_call(
        output_kernel,
        out_shape=jax.ShapeDtypeStruct((replicas, owners * rows_dev, half), bf16),
        in_specs=[smem_spec()] + [vmem_spec()] * (2 * replicas + 2),
        out_specs=vmem_spec(),
        compiler_params=params,
        name="output",
    )(place, *own, *other, w_own, w_other)
    product = product.reshape(replicas * owners, rows_dev, half)
    placed = lax.all_to_all(product, ("replica", "tensor"), split_axis=0, concat_axis=0, tiled=True)
    return pl.pallas_call(
        functools.partial(sum_kernel, replicas, owners // 2),
        out_shape=jax.ShapeDtypeStruct((rows_dev, replicas * 2 * half), bf16),
        in_specs=[vmem_spec()],
        out_specs=vmem_spec(),
        compiler_params=params,
        name="combine",
    )(placed)


def solution(mesh):
    rows = ("groups", "tensor", "replica")
    return jax.shard_map(
        shards,
        mesh=mesh,
        in_specs=(
            P(rows, None),
            P(),
            P(None, "tensor"),
            P("tensor", None, None),
            P("tensor", None, None),
            P("tensor", "replica"),
            P(rows, None),
            P(rows, None, None),
            P(rows),
            P(rows),
        ),
        out_specs=P(rows, None),
        check_vma=False,
    )
```

```python
import functools

import jax
import jax.numpy as jnp
from jax import lax
from jax.experimental import pallas as pl
from jax.experimental.pallas import tpu as pltpu
from jax.sharding import PartitionSpec as P


LATENT = 512
ROPE = 64
NOPE = 128
VDIM = 128
QKD = NOPE + ROPE
LANES = 128

rms_eps = 1e-06
rope_base = 50000.0

VMEM = pltpu.MemorySpace.VMEM
SMEM = pltpu.MemorySpace.SMEM
bf16 = jnp.bfloat16
f32 = jnp.float32


def vmem_spec():
    return pl.BlockSpec(memory_space=VMEM)


def smem_spec():
    return pl.BlockSpec(memory_space=SMEM)


def over(x, n):
    return x >> (n.bit_length() - 1) if n & (n - 1) == 0 else x // n


def rest(x, n):
    return x & (n - 1) if n & (n - 1) == 0 else x % n


def mm(a, b):
    return jnp.dot(a, b, preferred_element_type=f32)


def mm_nt(a, b):
    return lax.dot_general(a, b, (((1,), (1,)), ((), ())), preferred_element_type=f32)


def fetch_kernel(*refs):
    count = len(refs) // 2
    copies = [pltpu.make_async_copy(refs[i], refs[count + i], refs[-1].at[i]) for i in range(count)]
    for copy in copies:
        copy.start()
    for copy in copies:
        copy.wait()


def fetch(arrays):
    return pl.pallas_call(
        fetch_kernel,
        out_shape=[pltpu.VMEM(x.shape, x.dtype) for x in arrays],
        in_specs=[pl.BlockSpec(memory_space=pl.ANY)] * len(arrays),
        out_specs=[vmem_spec()] * len(arrays),
        scratch_shapes=[pltpu.SemaphoreType.DMA((len(arrays),))],
        compiler_params=pltpu.CompilerParams(vmem_limit_bytes=1024 * 1024),
        cost_estimate=pl.CostEstimate(
            flops=0, bytes_accessed=sum(4 * x.size for x in arrays), transcendentals=0
        ),
    )(*arrays)


def query_kernel(reqs, drafts, heads, place_ref, *refs):
    *x_refs, gain_ref, up_ref, uk_ref, out_ref = refs
    owners = out_ref.shape[0]
    rows_dev = reqs * drafts
    hd = heads * drafts
    x = jnp.concatenate([x_ref[...] for x_ref in x_refs], axis=0).astype(f32)
    scaled = x * lax.rsqrt(jnp.mean(x * x, axis=-1, keepdims=True) + rms_eps)
    normed = (scaled * gain_ref[...][None, :]).astype(bf16)
    full = mm(normed, up_ref[...]).astype(bf16)
    count = owners * reqs * hd
    shape = (count, owners * rows_dev)
    n = lax.broadcasted_iota(jnp.int32, shape, 0)
    m = lax.broadcasted_iota(jnp.int32, shape, 1)
    target = over(n, reqs * hd)
    local = rest(over(n, hd), reqs) * drafts + rest(n, drafts)
    block = over(m, rows_dev)
    distance = jnp.zeros_like(block)
    bit = owners // 2
    while bit:
        distance = distance + (block & 1) * bit
        block = block >> 1
        bit //= 2
    spread = jnp.where((target == (distance ^ place_ref[2])) & (local == rest(m, rows_dev)), 1.0, 0.0)
    wide = mm(spread.astype(bf16), full)
    row_head = rest(over(lax.broadcasted_iota(jnp.int32, (count, 1), 0), drafts), heads)
    absorbed = None
    rope = None
    for h in range(heads):
        mine = row_head == h
        nope_h = jnp.where(mine, wide[:, h * QKD : h * QKD + NOPE], 0.0).astype(bf16)
        part = mm(nope_h, uk_ref[h * NOPE : (h + 1) * NOPE])
        absorbed = part if absorbed is None else absorbed + part
        rope_h = jnp.where(mine, wide[:, h * QKD + NOPE : (h + 1) * QKD], 0.0)
        rope = rope_h if rope is None else rope + rope_h
    chunks = LATENT // LANES
    absorbed = absorbed.reshape(owners, reqs, hd, LATENT)
    rope = rope.reshape(owners, reqs, hd, ROPE)
    for q in range(reqs):
        for c in range(chunks):
            at = (q * chunks + c) * hd
            out_ref[:, at : at + hd, :] = absorbed[:, q, :, c * LANES : (c + 1) * LANES].astype(bf16)
    per = LANES // ROPE
    for b in range(reqs // per):
        at = (reqs * chunks + b) * hd
        both = jnp.concatenate([rope[:, b * per + i] for i in range(per)], axis=-1)
        out_ref[:, at : at + hd, :] = both.astype(bf16)


def attend_kernel(reqs, drafts, heads, len_ref, count_ref, q_ref, cos_ref, sin_ref, new_ref, cache_ref, out_ref):
    owners = q_ref.shape[0]
    hd = heads * drafts
    count = owners * hd
    chunks = LATENT // LANES
    per = LANES // ROPE
    slots = cache_ref.shape[2]
    scale = QKD ** (-0.5)
    rotated = []
    for b in range(reqs // per):
        at = (reqs * chunks + b) * hd
        x = q_ref[:, at : at + hd, :].astype(f32).reshape(count, LANES)
        lane = rest(lax.broadcasted_iota(jnp.int32, x.shape, 1), ROPE)
        half = ROPE // 2
        other = jnp.where(lane < half, pltpu.roll(x, LANES - half, 1), pltpu.roll(x, half, 1))
        x = x.reshape(owners, hd, LANES) * cos_ref[b] + other.reshape(owners, hd, LANES) * sin_ref[b]
        x = x.astype(bf16).reshape(count, LANES)
        rotated += [x[:, i * ROPE : (i + 1) * ROPE] for i in range(per)]
    draft = rest(lax.broadcasted_iota(jnp.int32, (count, 1), 0), drafts)
    new_at = lax.broadcasted_iota(jnp.int32, (count, new_ref.shape[0]), 1)
    slot = lax.broadcasted_iota(jnp.int32, (1, slots), 1)
    for q in range(reqs):
        absorbed = jnp.concatenate(
            [
                q_ref[:, (q * chunks + c) * hd : (q * chunks + c + 1) * hd, :].reshape(count, LANES)
                for c in range(chunks)
            ],
            axis=-1,
        )
        keys = cache_ref[q]
        rows = new_ref[...]
        score = (mm(absorbed, keys[:LATENT]) + mm(rotated[q], keys[LATENT:])) * scale
        fresh = (mm_nt(absorbed, rows[:, :LATENT]) + mm_nt(rotated[q], rows[:, LATENT:])) * scale
        score = jnp.where(slot < len_ref[q], score, -jnp.inf)
        seen = (new_at >= q * drafts) & (new_at - q * drafts <= draft)
        fresh = jnp.where(seen, fresh, -jnp.inf)
        peak = jnp.maximum(
            jnp.max(score, axis=1, keepdims=True), jnp.max(fresh, axis=1, keepdims=True)
        )
        score = jnp.exp(score - peak)
        fresh = jnp.exp(fresh - peak)
        total = jnp.sum(score, axis=1, keepdims=True) + jnp.sum(fresh, axis=1, keepdims=True)
        inverse = 1.0 / total
        mix = mm_nt((score * inverse).astype(bf16), keys[:LATENT])
        mix = mix + mm((fresh * inverse).astype(bf16), rows[:, :LATENT])
        mix = jnp.where(draft < count_ref[q], mix, 0.0).astype(bf16)
        out_ref[:, q * hd : (q + 1) * hd, :] = mix.reshape(owners, hd, LATENT)


def value_kernel(reqs, drafts, heads, latent_ref, uv_ref, out_ref):
    owners = latent_ref.shape[0]
    hd = heads * drafts
    rows = owners * reqs * drafts
    latent = latent_ref[...].reshape(owners * reqs * hd, LATENT)
    shape = (rows, owners * reqs * hd)
    m = lax.broadcasted_iota(jnp.int32, shape, 0)
    n = lax.broadcasted_iota(jnp.int32, shape, 1)
    wanted = over(m, drafts) * hd + rest(m, drafts)
    for h in range(heads):
        pick = jnp.where(n == wanted + h * drafts, 1.0, 0.0).astype(bf16)
        mine = mm(pick, latent).astype(bf16)
        out_ref[:, h * VDIM : (h + 1) * VDIM] = mm(mine, uv_ref[h]).astype(bf16)


def output_kernel(place_ref, *refs):
    *value_refs, w_own_ref, w_other_ref, out_ref = refs
    replicas, rows, half = out_ref.shape
    own = jnp.concatenate([ref[...] for ref in value_refs[:replicas]], axis=0)
    other = jnp.concatenate([ref[...] for ref in value_refs[replicas:]], axis=0)
    tile = 256 if half % 256 == 0 else half
    start = pl.multiple_of(place_ref[0] * half, LANES) if half % LANES == 0 else 0
    for at in range(0, half, tile):
        part = mm(own, w_own_ref[:, pl.ds(start + at, tile)]) + mm(other, w_other_ref[:, at : at + tile])
        part = part.astype(bf16)
        for k in range(replicas):
            out_ref[place_ref[1] ^ k, :, at : at + tile] = part[k * rows : (k + 1) * rows]


def sum_kernel(replicas, pairs, x_ref, out_ref):
    width = x_ref.shape[-1]
    for r in range(replicas):
        for c in range(2):
            total = None
            for p in range(pairs):
                part = x_ref[(r * pairs + p) * 2 + c].astype(f32)
                total = part if total is None else total + part
            at = (r * 2 + c) * width
            out_ref[:, at : at + width] = total.astype(bf16)


def step(x, axis, size, k):
    return lax.ppermute(x, axis, [(i, i ^ k) for i in range(size)])


def local_step(q_latent, q_gain, q_up, w_uk, w_uv, w_o, new_kv, latent_cache, cache_len, draft_count):
    rows_dev, _ = q_latent.shape
    owners = lax.axis_size("tensor")
    replicas = lax.axis_size("replica")
    heads = w_uk.shape[0]
    reqs = cache_len.shape[0]
    drafts = rows_dev // reqs
    hd = heads * drafts
    me = lax.axis_index("tensor")
    core = me % 2

    place = jnp.stack([core, lax.axis_index("replica"), me]).astype(jnp.int32)
    w_uk = w_uk.reshape(heads * NOPE, LATENT)
    near = fetch((q_up, w_uk, q_latent))

    first = step(q_latent, "tensor", owners, owners // 2)
    first, up_near, uk_near, rows = lax.optimization_barrier((first, *near))
    rows = jnp.concatenate([rows, first], axis=0)
    bit = owners // 4
    while bit > 2:
        rows = jnp.concatenate([rows, step(rows, "tensor", owners, bit)], axis=0)
        bit //= 2
    parts = [rows]
    while bit:
        parts = parts + [step(part, "tensor", owners, bit) for part in parts]
        bit //= 2

    chunks = LATENT // LANES
    packed = (reqs * chunks + reqs * ROPE // LANES) * hd
    params = pltpu.CompilerParams(vmem_limit_bytes=24 * 1024 * 1024)
    queries = pl.pallas_call(
        functools.partial(query_kernel, reqs, drafts, heads),
        out_shape=jax.ShapeDtypeStruct((owners, packed, LANES), bf16),
        in_specs=[smem_spec()] + [vmem_spec()] * (len(parts) + 3),
        out_specs=vmem_spec(),
        compiler_params=params,
        name="query",
    )(place, *parts, q_gain, up_near, uk_near)
    arrived = lax.all_to_all(queries, "tensor", split_axis=0, concat_axis=0, tiled=True)

    half = w_o.shape[1] // 2
    w_away = lax.dynamic_slice_in_dim(w_o, (1 - core) * half, half, axis=1)
    w_other = step(w_away, "tensor", owners, 1)
    arrived, w_other = lax.optimization_barrier((arrived, w_other))
    w_own = w_o if half % LANES == 0 else lax.dynamic_slice_in_dim(w_o, core * half, half, axis=1)

    frequency = rope_base ** (-(jnp.arange(ROPE // 2).astype(f32) * 2.0 / ROPE))
    positions = (cache_len[:, None] + jnp.arange(drafts)[None, :]).astype(f32)
    angles = positions[:, :, None] * frequency
    per = LANES // ROPE

    def table(first, second):
        lanes = jnp.concatenate([first, second], axis=-1)
        lanes = lanes.reshape(reqs // per, per, drafts, ROPE)
        lanes = jnp.swapaxes(lanes, 1, 2).reshape(reqs // per, 1, drafts, LANES)
        return jnp.broadcast_to(lanes, (reqs // per, heads, drafts, LANES)).reshape(reqs // per, hd, LANES)

    cosine = jnp.cos(angles)
    sine = jnp.sin(angles)
    latent = pl.pallas_call(
        functools.partial(attend_kernel, reqs, drafts, heads),
        out_shape=jax.ShapeDtypeStruct((owners, reqs * hd, LATENT), bf16),
        in_specs=[smem_spec()] * 2 + [vmem_spec()] * 5,
        out_specs=vmem_spec(),
        compiler_params=params,
        name="attend",
    )(cache_len, draft_count, arrived, table(cosine, cosine), table(-sine, sine), new_kv, jnp.swapaxes(latent_cache, 1, 2))
    returned = lax.all_to_all(latent, "tensor", split_axis=0, concat_axis=0, tiled=True)

    values = pl.pallas_call(
        functools.partial(value_kernel, reqs, drafts, heads),
        out_shape=jax.ShapeDtypeStruct((owners * rows_dev, heads * VDIM), bf16),
        in_specs=[vmem_spec()] * 2,
        out_specs=vmem_spec(),
        compiler_params=params,
        name="values",
    )(returned, w_uv)
    nearest = step(values, "replica", replicas, 1)
    own = [values, nearest] + [step(values, "replica", replicas, k) for k in range(2, replicas)]
    (w_other,) = fetch((w_other,))
    other = [step(piece, "tensor", owners, 1) for piece in own]

    product = pl.pallas_call(
        output_kernel,
        out_shape=jax.ShapeDtypeStruct((replicas, owners * rows_dev, half), bf16),
        in_specs=[smem_spec()] + [vmem_spec()] * (2 * replicas + 2),
        out_specs=vmem_spec(),
        compiler_params=params,
        name="output",
    )(place, *own, *other, w_own, w_other)
    product = product.reshape(replicas * owners, rows_dev, half)
    placed = lax.all_to_all(product, ("replica", "tensor"), split_axis=0, concat_axis=0, tiled=True)
    return pl.pallas_call(
        functools.partial(sum_kernel, replicas, owners // 2),
        out_shape=jax.ShapeDtypeStruct((rows_dev, replicas * 2 * half), bf16),
        in_specs=[vmem_spec()],
        out_specs=vmem_spec(),
        compiler_params=params,
        name="combine",
    )(placed)


def solution(mesh):
    rows = ("groups", "tensor", "replica")
    return jax.shard_map(
        local_step,
        mesh=mesh,
        in_specs=(
            P(rows, None),
            P(),
            P(None, "tensor"),
            P("tensor", None, None),
            P("tensor", None, None),
            P("tensor", "replica"),
            P(rows, None),
            P(rows, None, None),
            P(rows),
            P(rows),
        ),
        out_specs=P(rows, None),
        check_vma=False,
    )
```

```python
import functools

import jax
import jax.numpy as jnp
from jax import lax
from jax.experimental import pallas as pl
from jax.experimental.pallas import tpu as pltpu
from jax.sharding import PartitionSpec as P


LATENT = 512
ROPE = 64
NOPE = 128
VDIM = 128
QKD = NOPE + ROPE
LANES = 128
UP_PARTS = 4
QUERY_VMEM = 56_000_000
OUTPUT_VMEM = 54_000_000

rms_eps = 1e-06
rope_base = 50000.0

VMEM = pltpu.MemorySpace.VMEM
SMEM = pltpu.MemorySpace.SMEM
bf16 = jnp.bfloat16
f32 = jnp.float32


def vmem_spec():
    return pl.BlockSpec(memory_space=VMEM)


def smem_spec():
    return pl.BlockSpec(memory_space=SMEM)


def over(x, n):
    return x >> (n.bit_length() - 1) if n & (n - 1) == 0 else x // n


def rest(x, n):
    return x & (n - 1) if n & (n - 1) == 0 else x % n


def mm(a, b):
    return jnp.dot(a, b, preferred_element_type=f32)


def mm_nt(a, b):
    return lax.dot_general(a, b, (((1,), (1,)), ((), ())), preferred_element_type=f32)


def query_kernel(reqs, drafts, heads, place_ref, *refs):
    *x_refs, gain_ref, up_hbm, uk_hbm, out_ref, up_ref, uk_ref, sems = refs
    deep = up_ref.shape[0] // UP_PARTS
    copies = [
        pltpu.make_async_copy(up_hbm.at[pl.ds(i * deep, deep)], up_ref.at[pl.ds(i * deep, deep)], sems.at[i])
        for i in range(UP_PARTS)
    ]
    copies.append(pltpu.make_async_copy(uk_hbm, uk_ref, sems.at[UP_PARTS]))
    for copy in copies:
        copy.start()
    owners = out_ref.shape[0]
    rows_dev = reqs * drafts
    hd = heads * drafts
    x = jnp.concatenate([x_ref[...] for x_ref in x_refs], axis=0).astype(f32)
    scaled = x * lax.rsqrt(jnp.mean(x * x, axis=-1, keepdims=True) + rms_eps)
    normed = (scaled * gain_ref[...][None, :]).astype(bf16)
    full = None
    for i in range(UP_PARTS):
        copies[i].wait()
        part = mm(normed[:, i * deep : (i + 1) * deep], up_ref[i * deep : (i + 1) * deep])
        full = part if full is None else full + part
    full = full.astype(bf16)
    count = owners * reqs * hd
    shape = (count, owners * rows_dev)
    n = lax.broadcasted_iota(jnp.int32, shape, 0)
    m = lax.broadcasted_iota(jnp.int32, shape, 1)
    target = over(n, reqs * hd)
    local = rest(over(n, hd), reqs) * drafts + rest(n, drafts)
    block = over(m, rows_dev)
    distance = jnp.zeros_like(block)
    bit = owners // 2
    while bit:
        distance = distance + (block & 1) * bit
        block = block >> 1
        bit //= 2
    spread = jnp.where((target == (distance ^ place_ref[2])) & (local == rest(m, rows_dev)), 1.0, 0.0)
    wide = mm(spread.astype(bf16), full)
    row_head = rest(over(lax.broadcasted_iota(jnp.int32, (count, 1), 0), drafts), heads)
    absorbed = None
    rope = None
    copies[UP_PARTS].wait()
    for h in range(heads):
        mine = row_head == h
        nope_h = jnp.where(mine, wide[:, h * QKD : h * QKD + NOPE], 0.0).astype(bf16)
        part = mm(nope_h, uk_ref[h])
        absorbed = part if absorbed is None else absorbed + part
        rope_h = jnp.where(mine, wide[:, h * QKD + NOPE : (h + 1) * QKD], 0.0)
        rope = rope_h if rope is None else rope + rope_h
    chunks = LATENT // LANES
    absorbed = absorbed.reshape(owners, reqs, hd, LATENT)
    rope = rope.reshape(owners, reqs, hd, ROPE)
    for q in range(reqs):
        for c in range(chunks):
            at = (q * chunks + c) * hd
            out_ref[:, at : at + hd, :] = absorbed[:, q, :, c * LANES : (c + 1) * LANES].astype(bf16)
    per = LANES // ROPE
    for b in range(reqs // per):
        at = (reqs * chunks + b) * hd
        both = jnp.concatenate([rope[:, b * per + i] for i in range(per)], axis=-1)
        out_ref[:, at : at + hd, :] = both.astype(bf16)


def attend_kernel(reqs, drafts, heads, len_ref, count_ref, q_ref, cos_ref, sin_ref, new_ref, cache_ref, out_ref):
    owners = q_ref.shape[0]
    hd = heads * drafts
    count = owners * hd
    chunks = LATENT // LANES
    per = LANES // ROPE
    slots = cache_ref.shape[2]
    scale = QKD ** (-0.5)
    rotated = []
    for b in range(reqs // per):
        at = (reqs * chunks + b) * hd
        x = q_ref[:, at : at + hd, :].astype(f32).reshape(count, LANES)
        lane = rest(lax.broadcasted_iota(jnp.int32, x.shape, 1), ROPE)
        half = ROPE // 2
        other = jnp.where(lane < half, pltpu.roll(x, LANES - half, 1), pltpu.roll(x, half, 1))
        x = x.reshape(owners, hd, LANES) * cos_ref[b] + other.reshape(owners, hd, LANES) * sin_ref[b]
        x = x.astype(bf16).reshape(count, LANES)
        rotated += [x[:, i * ROPE : (i + 1) * ROPE] for i in range(per)]
    draft = rest(lax.broadcasted_iota(jnp.int32, (count, 1), 0), drafts)
    new_at = lax.broadcasted_iota(jnp.int32, (count, new_ref.shape[0]), 1)
    slot = lax.broadcasted_iota(jnp.int32, (1, slots), 1)
    for q in range(reqs):
        absorbed = jnp.concatenate(
            [
                q_ref[:, (q * chunks + c) * hd : (q * chunks + c + 1) * hd, :].reshape(count, LANES)
                for c in range(chunks)
            ],
            axis=-1,
        )
        keys = cache_ref[q]
        rows = new_ref[...]
        score = (mm(absorbed, keys[:LATENT]) + mm(rotated[q], keys[LATENT:])) * scale
        fresh = (mm_nt(absorbed, rows[:, :LATENT]) + mm_nt(rotated[q], rows[:, LATENT:])) * scale
        score = jnp.where(slot < len_ref[q], score, -jnp.inf)
        seen = (new_at >= q * drafts) & (new_at - q * drafts <= draft)
        fresh = jnp.where(seen, fresh, -jnp.inf)
        peak = jnp.maximum(
            jnp.max(score, axis=1, keepdims=True), jnp.max(fresh, axis=1, keepdims=True)
        )
        score = jnp.exp(score - peak)
        fresh = jnp.exp(fresh - peak)
        total = jnp.sum(score, axis=1, keepdims=True) + jnp.sum(fresh, axis=1, keepdims=True)
        inverse = 1.0 / total
        mix = mm_nt((score * inverse).astype(bf16), keys[:LATENT])
        mix = mix + mm((fresh * inverse).astype(bf16), rows[:, :LATENT])
        mix = jnp.where(draft < count_ref[q], mix, 0.0).astype(bf16)
        out_ref[:, q * hd : (q + 1) * hd, :] = mix.reshape(owners, hd, LATENT)


def value_kernel(reqs, drafts, heads, latent_ref, uv_ref, out_ref):
    owners = latent_ref.shape[0]
    hd = heads * drafts
    rows = owners * reqs * drafts
    latent = latent_ref[...].reshape(owners * reqs * hd, LATENT)
    shape = (rows, owners * reqs * hd)
    m = lax.broadcasted_iota(jnp.int32, shape, 0)
    n = lax.broadcasted_iota(jnp.int32, shape, 1)
    wanted = over(m, drafts) * hd + rest(m, drafts)
    for h in range(heads):
        pick = jnp.where(n == wanted + h * drafts, 1.0, 0.0).astype(bf16)
        mine = mm(pick, latent).astype(bf16)
        out_ref[:, h * VDIM : (h + 1) * VDIM] = mm(mine, uv_ref[h]).astype(bf16)


def output_kernel(place_ref, *refs):
    *value_refs, own_hbm, other_hbm, out_ref, own_ref, other_ref, sems = refs
    replicas, rows, half = out_ref.shape
    tile = 256 if half % 256 == 0 else half
    tiles = half // tile
    start = 0
    if own_hbm.shape[1] != half:
        start = pl.multiple_of(place_ref[0] * half, LANES)
    copies = []
    for i in range(tiles):
        to = pl.ds(i * tile, tile)
        own_copy = pltpu.make_async_copy(
            own_hbm.at[:, pl.ds(start + i * tile, tile)], own_ref.at[:, to], sems.at[0, i]
        )
        other_copy = pltpu.make_async_copy(other_hbm.at[:, to], other_ref.at[:, to], sems.at[1, i])
        copies.append((own_copy, other_copy))
        own_copy.start()
        other_copy.start()
    own = jnp.concatenate([ref[...] for ref in value_refs[:replicas]], axis=0)
    other = jnp.concatenate([ref[...] for ref in value_refs[replicas:]], axis=0)
    for i in range(tiles):
        at = slice(i * tile, (i + 1) * tile)
        copies[i][0].wait()
        part = mm(own, own_ref[:, at])
        copies[i][1].wait()
        part = (part + mm(other, other_ref[:, at])).astype(bf16)
        for k in range(replicas):
            out_ref[place_ref[1] ^ k, :, at] = part[k * rows : (k + 1) * rows]


def sum_kernel(replicas, pairs, x_ref, out_ref):
    width = x_ref.shape[-1]
    for r in range(replicas):
        for c in range(2):
            total = None
            for p in range(pairs):
                part = x_ref[(r * pairs + p) * 2 + c].astype(f32)
                total = part if total is None else total + part
            at = (r * 2 + c) * width
            out_ref[:, at : at + width] = total.astype(bf16)


def step(x, axis, size, k):
    return lax.ppermute(x, axis, [(i, i ^ k) for i in range(size)])


def local_step(q_latent, q_gain, q_up, w_uk, w_uv, w_o, new_kv, latent_cache, cache_len, draft_count):
    rows_dev, _ = q_latent.shape
    owners = lax.axis_size("tensor")
    replicas = lax.axis_size("replica")
    heads = w_uk.shape[0]
    reqs = cache_len.shape[0]
    drafts = rows_dev // reqs
    hd = heads * drafts
    me = lax.axis_index("tensor")
    core = me % 2

    place = jnp.stack([core, lax.axis_index("replica"), me]).astype(jnp.int32)

    rows = q_latent
    bit = owners // 2
    while bit > 2:
        rows = jnp.concatenate([rows, step(rows, "tensor", owners, bit)], axis=0)
        bit //= 2
    parts = [rows]
    while bit:
        parts = parts + [step(part, "tensor", owners, bit) for part in parts]
        bit //= 2

    chunks = LATENT // LANES
    packed = (reqs * chunks + reqs * ROPE // LANES) * hd
    params = pltpu.CompilerParams(vmem_limit_bytes=24 * 1024 * 1024)
    queries = pl.pallas_call(
        functools.partial(query_kernel, reqs, drafts, heads),
        out_shape=jax.ShapeDtypeStruct((owners, packed, LANES), bf16),
        in_specs=[smem_spec()] + [vmem_spec()] * (len(parts) + 1) + [pl.BlockSpec(memory_space=pl.ANY)] * 2,
        out_specs=vmem_spec(),
        scratch_shapes=[
            pltpu.VMEM(q_up.shape, bf16),
            pltpu.VMEM(w_uk.shape, bf16),
            pltpu.SemaphoreType.DMA((UP_PARTS + 1,)),
        ],
        compiler_params=pltpu.CompilerParams(vmem_limit_bytes=QUERY_VMEM),
        name="query",
    )(place, *parts, q_gain, q_up, w_uk)
    arrived = lax.all_to_all(queries, "tensor", split_axis=0, concat_axis=0, tiled=True)

    half = w_o.shape[1] // 2
    w_away = lax.dynamic_slice_in_dim(w_o, (1 - core) * half, half, axis=1)
    w_other = step(w_away, "tensor", owners, 1)
    arrived, w_other = lax.optimization_barrier((arrived, w_other))
    w_own = w_o if half % LANES == 0 else lax.dynamic_slice_in_dim(w_o, core * half, half, axis=1)

    frequency = rope_base ** (-(jnp.arange(ROPE // 2).astype(f32) * 2.0 / ROPE))
    positions = (cache_len[:, None] + jnp.arange(drafts)[None, :]).astype(f32)
    angles = positions[:, :, None] * frequency
    per = LANES // ROPE

    def table(first, second):
        lanes = jnp.concatenate([first, second], axis=-1)
        lanes = lanes.reshape(reqs // per, per, drafts, ROPE)
        lanes = jnp.swapaxes(lanes, 1, 2).reshape(reqs // per, 1, drafts, LANES)
        return jnp.broadcast_to(lanes, (reqs // per, heads, drafts, LANES)).reshape(reqs // per, hd, LANES)

    cosine = jnp.cos(angles)
    sine = jnp.sin(angles)
    latent = pl.pallas_call(
        functools.partial(attend_kernel, reqs, drafts, heads),
        out_shape=jax.ShapeDtypeStruct((owners, reqs * hd, LATENT), bf16),
        in_specs=[smem_spec()] * 2 + [vmem_spec()] * 5,
        out_specs=vmem_spec(),
        compiler_params=params,
        name="attend",
    )(cache_len, draft_count, arrived, table(cosine, cosine), table(-sine, sine), new_kv, jnp.swapaxes(latent_cache, 1, 2))
    returned = lax.all_to_all(latent, "tensor", split_axis=0, concat_axis=0, tiled=True)

    values = pl.pallas_call(
        functools.partial(value_kernel, reqs, drafts, heads),
        out_shape=jax.ShapeDtypeStruct((owners * rows_dev, heads * VDIM), bf16),
        in_specs=[vmem_spec()] * 2,
        out_specs=vmem_spec(),
        compiler_params=params,
        name="values",
    )(returned, w_uv)
    own = [values] + [step(values, "replica", replicas, k) for k in range(1, replicas)]
    other = [step(piece, "tensor", owners, 1) for piece in own]

    product = pl.pallas_call(
        output_kernel,
        out_shape=jax.ShapeDtypeStruct((replicas, owners * rows_dev, half), bf16),
        in_specs=[smem_spec()] + [vmem_spec()] * (2 * replicas) + [pl.BlockSpec(memory_space=pl.ANY)] * 2,
        out_specs=vmem_spec(),
        scratch_shapes=[
            pltpu.VMEM(w_other.shape, bf16),
            pltpu.VMEM(w_other.shape, bf16),
            pltpu.SemaphoreType.DMA((2, half // 256 if half % 256 == 0 else 1)),
        ],
        compiler_params=pltpu.CompilerParams(vmem_limit_bytes=OUTPUT_VMEM),
        name="output",
    )(place, *own, *other, w_own, w_other)
    product = product.reshape(replicas * owners, rows_dev, half)
    placed = lax.all_to_all(product, ("replica", "tensor"), split_axis=0, concat_axis=0, tiled=True)
    return pl.pallas_call(
        functools.partial(sum_kernel, replicas, owners // 2),
        out_shape=jax.ShapeDtypeStruct((rows_dev, replicas * 2 * half), bf16),
        in_specs=[vmem_spec()],
        out_specs=vmem_spec(),
        compiler_params=params,
        name="combine",
    )(placed)


def solution(mesh):
    rows = ("groups", "tensor", "replica")
    return jax.shard_map(
        local_step,
        mesh=mesh,
        in_specs=(
            P(rows, None),
            P(),
            P(None, "tensor"),
            P("tensor", None, None),
            P("tensor", None, None),
            P("tensor", "replica"),
            P(rows, None),
            P(rows, None, None),
            P(rows),
            P(rows),
        ),
        out_specs=P(rows, None),
        check_vma=False,
    )
```

```python
import functools

import jax
import jax.numpy as jnp
from jax import lax
from jax.experimental import pallas as pl
from jax.experimental.pallas import tpu as pltpu
from jax.sharding import PartitionSpec as P


LATENT = 512
ROPE = 64
NOPE = 128
VDIM = 128
QKD = NOPE + ROPE
LANES = 128

rms_eps = 1e-06
rope_base = 50000.0

VMEM = pltpu.MemorySpace.VMEM
SMEM = pltpu.MemorySpace.SMEM
bf16 = jnp.bfloat16
f32 = jnp.float32


def vmem_spec():
    return pl.BlockSpec(memory_space=VMEM)


def smem_spec():
    return pl.BlockSpec(memory_space=SMEM)


def over(x, n):
    return x >> (n.bit_length() - 1) if n & (n - 1) == 0 else x // n


def rest(x, n):
    return x & (n - 1) if n & (n - 1) == 0 else x % n


def mm(a, b):
    return jnp.dot(a, b, preferred_element_type=f32)


def mm_nt(a, b):
    return lax.dot_general(a, b, (((1,), (1,)), ((), ())), preferred_element_type=f32)


def join_kernel(first_ref, second_ref, out_ref):
    rows = first_ref.shape[0]
    out_ref[:rows] = first_ref[...]
    out_ref[rows:] = second_ref[...]


def join(first, second):
    return pl.pallas_call(
        join_kernel,
        out_shape=jax.ShapeDtypeStruct((2 * first.shape[0], first.shape[1]), first.dtype),
        in_specs=[vmem_spec()] * 2,
        out_specs=vmem_spec(),
        compiler_params=pltpu.CompilerParams(vmem_limit_bytes=4 * 1024 * 1024),
        cost_estimate=pl.CostEstimate(flops=0, bytes_accessed=8 * first.size, transcendentals=0),
        name="join",
    )(first, second)


def query_kernel(reqs, drafts, heads, place_ref, *refs):
    *x_refs, gain_ref, up_ref, uk_ref, out_ref = refs
    owners = out_ref.shape[0]
    rows_dev = reqs * drafts
    hd = heads * drafts
    x = jnp.concatenate([x_ref[...] for x_ref in x_refs], axis=0).astype(f32)
    scaled = x * lax.rsqrt(jnp.mean(x * x, axis=-1, keepdims=True) + rms_eps)
    normed = (scaled * gain_ref[...][None, :]).astype(bf16)
    full = mm(normed, up_ref[...]).astype(bf16)
    count = owners * reqs * hd
    shape = (count, owners * rows_dev)
    n = lax.broadcasted_iota(jnp.int32, shape, 0)
    m = lax.broadcasted_iota(jnp.int32, shape, 1)
    target = over(n, reqs * hd)
    local = rest(over(n, hd), reqs) * drafts + rest(n, drafts)
    block = over(m, rows_dev)
    distance = jnp.zeros_like(block)
    bit = owners // 2
    while bit:
        distance = distance + (block & 1) * bit
        block = block >> 1
        bit //= 2
    spread = jnp.where((target == (distance ^ place_ref[2])) & (local == rest(m, rows_dev)), 1.0, 0.0)
    wide = mm(spread.astype(bf16), full)
    row_head = rest(over(lax.broadcasted_iota(jnp.int32, (count, 1), 0), drafts), heads)
    absorbed = None
    rope = None
    for h in range(heads):
        mine = row_head == h
        nope_h = jnp.where(mine, wide[:, h * QKD : h * QKD + NOPE], 0.0).astype(bf16)
        part = mm(nope_h, uk_ref[h])
        absorbed = part if absorbed is None else absorbed + part
        rope_h = jnp.where(mine, wide[:, h * QKD + NOPE : (h + 1) * QKD], 0.0)
        rope = rope_h if rope is None else rope + rope_h
    chunks = LATENT // LANES
    absorbed = absorbed.reshape(owners, reqs, hd, LATENT)
    rope = rope.reshape(owners, reqs, hd, ROPE)
    for q in range(reqs):
        for c in range(chunks):
            at = (q * chunks + c) * hd
            out_ref[:, at : at + hd, :] = absorbed[:, q, :, c * LANES : (c + 1) * LANES].astype(bf16)
    per = LANES // ROPE
    for b in range(reqs // per):
        at = (reqs * chunks + b) * hd
        both = jnp.concatenate([rope[:, b * per + i] for i in range(per)], axis=-1)
        out_ref[:, at : at + hd, :] = both.astype(bf16)


def attend_kernel(reqs, drafts, heads, len_ref, count_ref, q_ref, cos_ref, sin_ref, new_ref, cache_ref, out_ref):
    owners = q_ref.shape[0]
    hd = heads * drafts
    count = owners * hd
    chunks = LATENT // LANES
    per = LANES // ROPE
    slots = cache_ref.shape[2]
    scale = QKD ** (-0.5)
    rotated = []
    for b in range(reqs // per):
        at = (reqs * chunks + b) * hd
        x = q_ref[:, at : at + hd, :].astype(f32).reshape(count, LANES)
        lane = rest(lax.broadcasted_iota(jnp.int32, x.shape, 1), ROPE)
        half = ROPE // 2
        other = jnp.where(lane < half, pltpu.roll(x, LANES - half, 1), pltpu.roll(x, half, 1))
        x = x.reshape(owners, hd, LANES) * cos_ref[b] + other.reshape(owners, hd, LANES) * sin_ref[b]
        x = x.astype(bf16).reshape(count, LANES)
        rotated += [x[:, i * ROPE : (i + 1) * ROPE] for i in range(per)]
    draft = rest(lax.broadcasted_iota(jnp.int32, (count, 1), 0), drafts)
    new_at = lax.broadcasted_iota(jnp.int32, (count, new_ref.shape[0]), 1)
    slot = lax.broadcasted_iota(jnp.int32, (1, slots), 1)
    for q in range(reqs):
        absorbed = jnp.concatenate(
            [
                q_ref[:, (q * chunks + c) * hd : (q * chunks + c + 1) * hd, :].reshape(count, LANES)
                for c in range(chunks)
            ],
            axis=-1,
        )
        keys = cache_ref[q]
        rows = new_ref[...]
        score = (mm(absorbed, keys[:LATENT]) + mm(rotated[q], keys[LATENT:])) * scale
        fresh = (mm_nt(absorbed, rows[:, :LATENT]) + mm_nt(rotated[q], rows[:, LATENT:])) * scale
        score = jnp.where(slot < len_ref[q], score, -jnp.inf)
        seen = (new_at >= q * drafts) & (new_at - q * drafts <= draft)
        fresh = jnp.where(seen, fresh, -jnp.inf)
        peak = jnp.maximum(
            jnp.max(score, axis=1, keepdims=True), jnp.max(fresh, axis=1, keepdims=True)
        )
        score = jnp.exp(score - peak)
        fresh = jnp.exp(fresh - peak)
        total = jnp.sum(score, axis=1, keepdims=True) + jnp.sum(fresh, axis=1, keepdims=True)
        inverse = 1.0 / total
        mix = mm_nt((score * inverse).astype(bf16), keys[:LATENT])
        mix = mix + mm((fresh * inverse).astype(bf16), rows[:, :LATENT])
        mix = jnp.where(draft < count_ref[q], mix, 0.0).astype(bf16)
        out_ref[:, q * hd : (q + 1) * hd, :] = mix.reshape(owners, hd, LATENT)


def value_kernel(reqs, drafts, heads, latent_ref, uv_ref, out_ref):
    owners = latent_ref.shape[0]
    hd = heads * drafts
    rows = owners * reqs * drafts
    latent = latent_ref[...].reshape(owners * reqs * hd, LATENT)
    shape = (rows, owners * reqs * hd)
    m = lax.broadcasted_iota(jnp.int32, shape, 0)
    n = lax.broadcasted_iota(jnp.int32, shape, 1)
    wanted = over(m, drafts) * hd + rest(m, drafts)
    for h in range(heads):
        pick = jnp.where(n == wanted + h * drafts, 1.0, 0.0).astype(bf16)
        mine = mm(pick, latent).astype(bf16)
        out_ref[:, h * VDIM : (h + 1) * VDIM] = mm(mine, uv_ref[h]).astype(bf16)


def output_kernel(place_ref, *refs):
    *value_refs, w_own_ref, w_other_ref, out_ref = refs
    replicas, rows, half = out_ref.shape
    own = jnp.concatenate([ref[...] for ref in value_refs[:replicas]], axis=0)
    other = jnp.concatenate([ref[...] for ref in value_refs[replicas:]], axis=0)
    tile = 256 if half % 256 == 0 else half
    start = pl.multiple_of(place_ref[0] * half, LANES) if half % LANES == 0 else 0
    for at in range(0, half, tile):
        part = mm(own, w_own_ref[:, pl.ds(start + at, tile)]) + mm(other, w_other_ref[:, at : at + tile])
        part = part.astype(bf16)
        for k in range(replicas):
            out_ref[place_ref[1] ^ k, :, at : at + tile] = part[k * rows : (k + 1) * rows]


def sum_kernel(replicas, pairs, x_ref, out_ref):
    width = x_ref.shape[-1]
    for r in range(replicas):
        for c in range(2):
            total = None
            for p in range(pairs):
                part = x_ref[(r * pairs + p) * 2 + c].astype(f32)
                total = part if total is None else total + part
            at = (r * 2 + c) * width
            out_ref[:, at : at + width] = total.astype(bf16)


def step(x, axis, size, k):
    return lax.ppermute(x, axis, [(i, i ^ k) for i in range(size)])


def near(x, size):
    return step(x, "tensor", size, 0)


def local_step(q_latent, q_gain, q_up, w_uk, w_uv, w_o, new_kv, latent_cache, cache_len, draft_count):
    rows_dev, _ = q_latent.shape
    owners = lax.axis_size("tensor")
    replicas = lax.axis_size("replica")
    heads = w_uk.shape[0]
    reqs = cache_len.shape[0]
    drafts = rows_dev // reqs
    hd = heads * drafts
    me = lax.axis_index("tensor")
    core = me % 2

    place = jnp.stack([core, lax.axis_index("replica"), me]).astype(jnp.int32)

    rows, gain, q_up, w_uk = (near(x, owners) for x in (q_latent, q_gain, q_up, w_uk))

    bit = owners // 2
    mine = q_latent
    while bit > 2:
        rows = join(rows, step(mine, "tensor", owners, bit))
        mine = rows
        bit //= 2
    parts = [rows]
    while bit:
        parts = parts + [step(part, "tensor", owners, bit) for part in parts]
        bit //= 2

    chunks = LATENT // LANES
    packed = (reqs * chunks + reqs * ROPE // LANES) * hd
    params = pltpu.CompilerParams(vmem_limit_bytes=24 * 1024 * 1024)
    queries = pl.pallas_call(
        functools.partial(query_kernel, reqs, drafts, heads),
        out_shape=jax.ShapeDtypeStruct((owners, packed, LANES), bf16),
        in_specs=[smem_spec()] + [vmem_spec()] * (len(parts) + 3),
        out_specs=vmem_spec(),
        compiler_params=params,
        name="query",
    )(place, *parts, gain, q_up, w_uk)
    arrived = lax.all_to_all(queries, "tensor", split_axis=0, concat_axis=0, tiled=True)

    half = w_o.shape[1] // 2
    w_away = lax.dynamic_slice_in_dim(w_o, (1 - core) * half, half, axis=1)
    w_other = step(w_away, "tensor", owners, 1)
    arrived, w_other = lax.optimization_barrier((arrived, w_other))
    w_own = w_o if half % LANES == 0 else lax.dynamic_slice_in_dim(w_o, core * half, half, axis=1)

    frequency = rope_base ** (-(jnp.arange(ROPE // 2).astype(f32) * 2.0 / ROPE))
    positions = (cache_len[:, None] + jnp.arange(drafts)[None, :]).astype(f32)
    angles = positions[:, :, None] * frequency
    per = LANES // ROPE

    def table(first, second):
        lanes = jnp.concatenate([first, second], axis=-1)
        lanes = lanes.reshape(reqs // per, per, drafts, ROPE)
        lanes = jnp.swapaxes(lanes, 1, 2).reshape(reqs // per, 1, drafts, LANES)
        return jnp.broadcast_to(lanes, (reqs // per, heads, drafts, LANES)).reshape(reqs // per, hd, LANES)

    cosine = jnp.cos(angles)
    sine = jnp.sin(angles)
    latent = pl.pallas_call(
        functools.partial(attend_kernel, reqs, drafts, heads),
        out_shape=jax.ShapeDtypeStruct((owners, reqs * hd, LATENT), bf16),
        in_specs=[smem_spec()] * 2 + [vmem_spec()] * 5,
        out_specs=vmem_spec(),
        compiler_params=params,
        name="attend",
    )(cache_len, draft_count, arrived, table(cosine, cosine), table(-sine, sine), new_kv, jnp.swapaxes(latent_cache, 1, 2))
    returned = lax.all_to_all(latent, "tensor", split_axis=0, concat_axis=0, tiled=True)

    returned, w_own, w_other = lax.optimization_barrier((returned, w_own, w_other))
    w_own, w_other = near(w_own, owners), near(w_other, owners)
    values = pl.pallas_call(
        functools.partial(value_kernel, reqs, drafts, heads),
        out_shape=jax.ShapeDtypeStruct((owners * rows_dev, heads * VDIM), bf16),
        in_specs=[vmem_spec()] * 2,
        out_specs=vmem_spec(),
        compiler_params=params,
        name="values",
    )(returned, w_uv)
    own = [values] + [step(values, "replica", replicas, k) for k in range(1, replicas)]
    other = [step(piece, "tensor", owners, 1) for piece in own]

    product = pl.pallas_call(
        output_kernel,
        out_shape=jax.ShapeDtypeStruct((replicas, owners * rows_dev, half), bf16),
        in_specs=[smem_spec()] + [vmem_spec()] * (2 * replicas + 2),
        out_specs=vmem_spec(),
        compiler_params=params,
        name="output",
    )(place, *own, *other, w_own, w_other)
    product = product.reshape(replicas * owners, rows_dev, half)
    placed = lax.all_to_all(product, ("replica", "tensor"), split_axis=0, concat_axis=0, tiled=True)
    return pl.pallas_call(
        functools.partial(sum_kernel, replicas, owners // 2),
        out_shape=jax.ShapeDtypeStruct((rows_dev, replicas * 2 * half), bf16),
        in_specs=[vmem_spec()],
        out_specs=vmem_spec(),
        compiler_params=params,
        name="combine",
    )(placed)


def solution(mesh):
    rows = ("groups", "tensor", "replica")
    return jax.shard_map(
        local_step,
        mesh=mesh,
        in_specs=(
            P(rows, None),
            P(),
            P(None, "tensor"),
            P("tensor", None, None),
            P("tensor", None, None),
            P("tensor", "replica"),
            P(rows, None),
            P(rows, None, None),
            P(rows),
            P(rows),
        ),
        out_specs=P(rows, None),
        check_vma=False,
    )
```

```python
import functools

import jax
import jax.numpy as jnp
from jax import lax
from jax.experimental import pallas as pl
from jax.experimental.pallas import tpu as pltpu
from jax.sharding import PartitionSpec as P


LATENT = 512
ROPE = 64
NOPE = 128
VDIM = 128
QKD = NOPE + ROPE
LANES = 128

FETCH_VMEM = 53_700_000

rms_eps = 1e-06
rope_base = 50000.0

VMEM = pltpu.MemorySpace.VMEM
SMEM = pltpu.MemorySpace.SMEM
bf16 = jnp.bfloat16
f32 = jnp.float32


def vmem_spec():
    return pl.BlockSpec(memory_space=VMEM)


def smem_spec():
    return pl.BlockSpec(memory_space=SMEM)


def over(x, n):
    return x >> (n.bit_length() - 1) if n & (n - 1) == 0 else x // n


def rest(x, n):
    return x & (n - 1) if n & (n - 1) == 0 else x % n


def mm(a, b):
    return jnp.dot(a, b, preferred_element_type=f32)


def mm_nt(a, b):
    return lax.dot_general(a, b, (((1,), (1,)), ((), ())), preferred_element_type=f32)


def fetch_kernel(*refs):
    count = len(refs) // 2
    copies = [pltpu.make_async_copy(refs[i], refs[count + i], refs[-1].at[i]) for i in range(count)]
    for copy in copies:
        copy.start()
    for copy in copies:
        copy.wait()


def fetch(arrays, limit):
    return pl.pallas_call(
        fetch_kernel,
        out_shape=[pltpu.VMEM(x.shape, x.dtype) for x in arrays],
        in_specs=[pl.BlockSpec(memory_space=pl.ANY)] * len(arrays),
        out_specs=[vmem_spec()] * len(arrays),
        scratch_shapes=[pltpu.SemaphoreType.DMA((len(arrays),))],
        compiler_params=pltpu.CompilerParams(vmem_limit_bytes=limit),
        cost_estimate=pl.CostEstimate(
            flops=0, bytes_accessed=sum(4 * x.size for x in arrays), transcendentals=0
        ),
    )(*arrays)


def query_kernel(reqs, drafts, heads, place_ref, *refs):
    *x_refs, gain_ref, up_ref, uk_ref, out_ref = refs
    owners = out_ref.shape[0]
    rows_dev = reqs * drafts
    hd = heads * drafts
    x = jnp.concatenate([x_ref[...] for x_ref in x_refs], axis=0).astype(f32)
    scaled = x * lax.rsqrt(jnp.mean(x * x, axis=-1, keepdims=True) + rms_eps)
    normed = (scaled * gain_ref[...][None, :]).astype(bf16)
    full = mm(normed, up_ref[...]).astype(bf16)
    count = owners * reqs * hd
    shape = (count, owners * rows_dev)
    n = lax.broadcasted_iota(jnp.int32, shape, 0)
    m = lax.broadcasted_iota(jnp.int32, shape, 1)
    target = over(n, reqs * hd)
    local = rest(over(n, hd), reqs) * drafts + rest(n, drafts)
    block = over(m, rows_dev)
    distance = jnp.zeros_like(block)
    bit = owners // 2
    while bit:
        distance = distance + (block & 1) * bit
        block = block >> 1
        bit //= 2
    spread = jnp.where((target == (distance ^ place_ref[2])) & (local == rest(m, rows_dev)), 1.0, 0.0)
    wide = mm(spread.astype(bf16), full)
    row_head = rest(over(lax.broadcasted_iota(jnp.int32, (count, 1), 0), drafts), heads)
    absorbed = None
    rope = None
    for h in range(heads):
        mine = row_head == h
        nope_h = jnp.where(mine, wide[:, h * QKD : h * QKD + NOPE], 0.0).astype(bf16)
        part = mm(nope_h, uk_ref[h * NOPE : (h + 1) * NOPE])
        absorbed = part if absorbed is None else absorbed + part
        rope_h = jnp.where(mine, wide[:, h * QKD + NOPE : (h + 1) * QKD], 0.0)
        rope = rope_h if rope is None else rope + rope_h
    chunks = LATENT // LANES
    absorbed = absorbed.reshape(owners, reqs, hd, LATENT)
    rope = rope.reshape(owners, reqs, hd, ROPE)
    for q in range(reqs):
        for c in range(chunks):
            at = (q * chunks + c) * hd
            out_ref[:, at : at + hd, :] = absorbed[:, q, :, c * LANES : (c + 1) * LANES].astype(bf16)
    per = LANES // ROPE
    for b in range(reqs // per):
        at = (reqs * chunks + b) * hd
        both = jnp.concatenate([rope[:, b * per + i] for i in range(per)], axis=-1)
        out_ref[:, at : at + hd, :] = both.astype(bf16)


def attend_kernel(reqs, drafts, heads, len_ref, count_ref, q_ref, cos_ref, sin_ref, new_ref, cache_ref, out_ref):
    owners = q_ref.shape[0]
    hd = heads * drafts
    count = owners * hd
    chunks = LATENT // LANES
    per = LANES // ROPE
    slots = cache_ref.shape[2]
    scale = QKD ** (-0.5)
    rotated = []
    for b in range(reqs // per):
        at = (reqs * chunks + b) * hd
        x = q_ref[:, at : at + hd, :].astype(f32).reshape(count, LANES)
        lane = rest(lax.broadcasted_iota(jnp.int32, x.shape, 1), ROPE)
        half = ROPE // 2
        other = jnp.where(lane < half, pltpu.roll(x, LANES - half, 1), pltpu.roll(x, half, 1))
        x = x.reshape(owners, hd, LANES) * cos_ref[b] + other.reshape(owners, hd, LANES) * sin_ref[b]
        x = x.astype(bf16).reshape(count, LANES)
        rotated += [x[:, i * ROPE : (i + 1) * ROPE] for i in range(per)]
    draft = rest(lax.broadcasted_iota(jnp.int32, (count, 1), 0), drafts)
    new_at = lax.broadcasted_iota(jnp.int32, (count, new_ref.shape[0]), 1)
    slot = lax.broadcasted_iota(jnp.int32, (1, slots), 1)
    for q in range(reqs):
        absorbed = jnp.concatenate(
            [
                q_ref[:, (q * chunks + c) * hd : (q * chunks + c + 1) * hd, :].reshape(count, LANES)
                for c in range(chunks)
            ],
            axis=-1,
        )
        keys = cache_ref[q]
        rows = new_ref[...]
        score = (mm(absorbed, keys[:LATENT]) + mm(rotated[q], keys[LATENT:])) * scale
        fresh = (mm_nt(absorbed, rows[:, :LATENT]) + mm_nt(rotated[q], rows[:, LATENT:])) * scale
        score = jnp.where(slot < len_ref[q], score, -jnp.inf)
        seen = (new_at >= q * drafts) & (new_at - q * drafts <= draft)
        fresh = jnp.where(seen, fresh, -jnp.inf)
        peak = jnp.maximum(
            jnp.max(score, axis=1, keepdims=True), jnp.max(fresh, axis=1, keepdims=True)
        )
        score = jnp.exp(score - peak)
        fresh = jnp.exp(fresh - peak)
        total = jnp.sum(score, axis=1, keepdims=True) + jnp.sum(fresh, axis=1, keepdims=True)
        inverse = 1.0 / total
        mix = mm_nt((score * inverse).astype(bf16), keys[:LATENT])
        mix = mix + mm((fresh * inverse).astype(bf16), rows[:, :LATENT])
        mix = jnp.where(draft < count_ref[q], mix, 0.0).astype(bf16)
        out_ref[:, q * hd : (q + 1) * hd, :] = mix.reshape(owners, hd, LATENT)


def value_kernel(reqs, drafts, heads, latent_ref, uv_ref, out_ref):
    owners = latent_ref.shape[0]
    hd = heads * drafts
    rows = owners * reqs * drafts
    latent = latent_ref[...].reshape(owners * reqs * hd, LATENT)
    shape = (rows, owners * reqs * hd)
    m = lax.broadcasted_iota(jnp.int32, shape, 0)
    n = lax.broadcasted_iota(jnp.int32, shape, 1)
    wanted = over(m, drafts) * hd + rest(m, drafts)
    for h in range(heads):
        pick = jnp.where(n == wanted + h * drafts, 1.0, 0.0).astype(bf16)
        mine = mm(pick, latent).astype(bf16)
        out_ref[:, h * VDIM : (h + 1) * VDIM] = mm(mine, uv_ref[h]).astype(bf16)


def output_kernel(place_ref, *refs):
    *value_refs, w_own_ref, w_other_ref, out_ref = refs
    replicas, rows, half = out_ref.shape
    own = jnp.concatenate([ref[...] for ref in value_refs[:replicas]], axis=0)
    other = jnp.concatenate([ref[...] for ref in value_refs[replicas:]], axis=0)
    tile = 256 if half % 256 == 0 else half
    start = pl.multiple_of(place_ref[0] * half, LANES) if half % LANES == 0 else 0
    for at in range(0, half, tile):
        part = mm(own, w_own_ref[:, pl.ds(start + at, tile)]) + mm(other, w_other_ref[:, at : at + tile])
        part = part.astype(bf16)
        for k in range(replicas):
            out_ref[place_ref[1] ^ k, :, at : at + tile] = part[k * rows : (k + 1) * rows]


def sum_kernel(replicas, pairs, x_ref, out_ref):
    width = x_ref.shape[-1]
    for r in range(replicas):
        for c in range(2):
            total = None
            for p in range(pairs):
                part = x_ref[(r * pairs + p) * 2 + c].astype(f32)
                total = part if total is None else total + part
            at = (r * 2 + c) * width
            out_ref[:, at : at + width] = total.astype(bf16)


def step(x, axis, size, k):
    return lax.ppermute(x, axis, [(i, i ^ k) for i in range(size)])


def local_step(q_latent, q_gain, q_up, w_uk, w_uv, w_o, new_kv, latent_cache, cache_len, draft_count):
    rows_dev, _ = q_latent.shape
    owners = lax.axis_size("tensor")
    replicas = lax.axis_size("replica")
    heads = w_uk.shape[0]
    reqs = cache_len.shape[0]
    drafts = rows_dev // reqs
    hd = heads * drafts
    me = lax.axis_index("tensor")
    core = me % 2

    place = jnp.stack([core, lax.axis_index("replica"), me]).astype(jnp.int32)
    w_uk = w_uk.reshape(heads * NOPE, LATENT)
    near = fetch((q_up, w_uk, q_gain, q_latent), FETCH_VMEM)

    first = step(q_latent, "tensor", owners, owners // 2)
    first, q_up, w_uk, gain, rows = lax.optimization_barrier((first, *near))
    rows = jnp.concatenate([rows, first], axis=0)
    bit = owners // 4
    while bit > 2:
        rows = jnp.concatenate([rows, step(rows, "tensor", owners, bit)], axis=0)
        bit //= 2
    parts = [rows]
    while bit:
        parts = parts + [step(part, "tensor", owners, bit) for part in parts]
        bit //= 2

    chunks = LATENT // LANES
    packed = (reqs * chunks + reqs * ROPE // LANES) * hd
    params = pltpu.CompilerParams(vmem_limit_bytes=24 * 1024 * 1024)
    queries = pl.pallas_call(
        functools.partial(query_kernel, reqs, drafts, heads),
        out_shape=jax.ShapeDtypeStruct((owners, packed, LANES), bf16),
        in_specs=[smem_spec()] + [vmem_spec()] * (len(parts) + 3),
        out_specs=vmem_spec(),
        compiler_params=params,
        name="query",
    )(place, *parts, gain, q_up, w_uk)
    arrived = lax.all_to_all(queries, "tensor", split_axis=0, concat_axis=0, tiled=True)

    half = w_o.shape[1] // 2
    w_away = lax.dynamic_slice_in_dim(w_o, (1 - core) * half, half, axis=1)
    w_other = step(w_away, "tensor", owners, 1)
    arrived, w_other = lax.optimization_barrier((arrived, w_other))
    w_own = w_o if half % LANES == 0 else lax.dynamic_slice_in_dim(w_o, core * half, half, axis=1)

    frequency = rope_base ** (-(jnp.arange(ROPE // 2).astype(f32) * 2.0 / ROPE))
    positions = (cache_len[:, None] + jnp.arange(drafts)[None, :]).astype(f32)
    angles = positions[:, :, None] * frequency
    per = LANES // ROPE

    def table(first, second):
        lanes = jnp.concatenate([first, second], axis=-1)
        lanes = lanes.reshape(reqs // per, per, drafts, ROPE)
        lanes = jnp.swapaxes(lanes, 1, 2).reshape(reqs // per, 1, drafts, LANES)
        return jnp.broadcast_to(lanes, (reqs // per, heads, drafts, LANES)).reshape(reqs // per, hd, LANES)

    cosine = jnp.cos(angles)
    sine = jnp.sin(angles)
    latent = pl.pallas_call(
        functools.partial(attend_kernel, reqs, drafts, heads),
        out_shape=jax.ShapeDtypeStruct((owners, reqs * hd, LATENT), bf16),
        in_specs=[smem_spec()] * 2 + [vmem_spec()] * 5,
        out_specs=vmem_spec(),
        compiler_params=params,
        name="attend",
    )(cache_len, draft_count, arrived, table(cosine, cosine), table(-sine, sine), new_kv, jnp.swapaxes(latent_cache, 1, 2))
    returned = lax.all_to_all(latent, "tensor", split_axis=0, concat_axis=0, tiled=True)

    values = pl.pallas_call(
        functools.partial(value_kernel, reqs, drafts, heads),
        out_shape=jax.ShapeDtypeStruct((owners * rows_dev, heads * VDIM), bf16),
        in_specs=[vmem_spec()] * 2,
        out_specs=vmem_spec(),
        compiler_params=params,
        name="values",
    )(returned, w_uv)
    nearest = step(values, "replica", replicas, 1)
    own = [values, nearest] + [step(values, "replica", replicas, k) for k in range(2, replicas)]
    (w_other,) = fetch((w_other,), 1024 * 1024)
    other = [step(piece, "tensor", owners, 1) for piece in own]

    product = pl.pallas_call(
        output_kernel,
        out_shape=jax.ShapeDtypeStruct((replicas, owners * rows_dev, half), bf16),
        in_specs=[smem_spec()] + [vmem_spec()] * (2 * replicas + 2),
        out_specs=vmem_spec(),
        compiler_params=params,
        name="output",
    )(place, *own, *other, w_own, w_other)
    product = product.reshape(replicas * owners, rows_dev, half)
    placed = lax.all_to_all(product, ("replica", "tensor"), split_axis=0, concat_axis=0, tiled=True)
    return pl.pallas_call(
        functools.partial(sum_kernel, replicas, owners // 2),
        out_shape=jax.ShapeDtypeStruct((rows_dev, replicas * 2 * half), bf16),
        in_specs=[vmem_spec()],
        out_specs=vmem_spec(),
        compiler_params=params,
        name="combine",
    )(placed)


def solution(mesh):
    rows = ("groups", "tensor", "replica")
    return jax.shard_map(
        local_step,
        mesh=mesh,
        in_specs=(
            P(rows, None),
            P(),
            P(None, "tensor"),
            P("tensor", None, None),
            P("tensor", None, None),
            P("tensor", "replica"),
            P(rows, None),
            P(rows, None, None),
            P(rows),
            P(rows),
        ),
        out_specs=P(rows, None),
        check_vma=False,
    )
```

```python
import functools

import jax
import jax.numpy as jnp
from jax import lax
from jax.experimental import pallas as pl
from jax.experimental.pallas import tpu as pltpu
from jax.sharding import PartitionSpec as P


LATENT = 512
ROPE = 64
NOPE = 128
VDIM = 128
QKD = NOPE + ROPE
LANES = 128

FETCH_VMEM = 53_700_000

rms_eps = 1e-06
rope_base = 50000.0

VMEM = pltpu.MemorySpace.VMEM
SMEM = pltpu.MemorySpace.SMEM
bf16 = jnp.bfloat16
f32 = jnp.float32


def vmem_spec():
    return pl.BlockSpec(memory_space=VMEM)


def smem_spec():
    return pl.BlockSpec(memory_space=SMEM)


def over(x, n):
    return x >> (n.bit_length() - 1) if n & (n - 1) == 0 else x // n


def rest(x, n):
    return x & (n - 1) if n & (n - 1) == 0 else x % n


def mm(a, b):
    return jnp.dot(a, b, preferred_element_type=f32)


def mm_nt(a, b):
    return lax.dot_general(a, b, (((1,), (1,)), ((), ())), preferred_element_type=f32)


def fetch_kernel(*refs):
    count = len(refs) // 2
    copies = [pltpu.make_async_copy(refs[i], refs[count + i], refs[-1].at[i]) for i in range(count)]
    for copy in copies:
        copy.start()
    for copy in copies:
        copy.wait()


def fetch(arrays, limit):
    return pl.pallas_call(
        fetch_kernel,
        out_shape=[pltpu.VMEM(x.shape, x.dtype) for x in arrays],
        in_specs=[pl.BlockSpec(memory_space=pl.ANY)] * len(arrays),
        out_specs=[vmem_spec()] * len(arrays),
        scratch_shapes=[pltpu.SemaphoreType.DMA((len(arrays),))],
        compiler_params=pltpu.CompilerParams(vmem_limit_bytes=limit),
        cost_estimate=pl.CostEstimate(
            flops=0, bytes_accessed=sum(4 * x.size for x in arrays), transcendentals=0
        ),
    )(*arrays)


def regroup(pieces, groups, size):
    assert groups == 2 and len(pieces) % 2 == 0
    rows = lax.broadcasted_iota(jnp.int32, pieces[0].shape, 0)
    low = rest(over(rows, size), 2) == 0
    total = pieces[0].shape[0]
    width = pieces[0].shape[1]
    firsts, seconds = [], []
    for h in range(0, len(pieces), 2):
        a, b = pieces[h], pieces[h + 1]
        firsts.append(jnp.where(low, a, pltpu.roll(b, size, 0)))
        seconds.append(jnp.where(low, pltpu.roll(a, total - size, 0), b))

    def stack(parts):
        parts = [part.reshape(total // (2 * size), 2 * size, width) for part in parts]
        return jnp.concatenate(parts, axis=1).reshape(total * len(parts), width)

    return [stack(firsts), stack(seconds)]


def query_kernel(reqs, drafts, heads, place_ref, *refs):
    *x_refs, gain_ref, up_ref, uk_ref, out_ref = refs
    owners = out_ref.shape[0]
    hd = heads * drafts
    x = jnp.concatenate([x_ref[...] for x_ref in x_refs], axis=0).astype(f32)
    scaled = x * lax.rsqrt(jnp.mean(x * x, axis=-1, keepdims=True) + rms_eps)
    normed = (scaled * gain_ref[...][None, :]).astype(bf16)
    full = mm(normed, up_ref[...]).astype(bf16)
    absorbed = [mm(full[:, h * QKD : h * QKD + NOPE], uk_ref[h * NOPE : (h + 1) * NOPE]) for h in range(heads)]
    rope = [full[:, h * QKD + NOPE : (h + 1) * QKD].astype(f32) for h in range(heads)]
    absorbed = regroup(absorbed, reqs, drafts)
    rope = regroup(rope, reqs, drafts)
    chunks = LATENT // LANES
    per = LANES // ROPE
    absorbed = [x.reshape(owners, hd, LATENT).astype(bf16) for x in absorbed]
    rope = [
        jnp.concatenate(rope[b * per : (b + 1) * per], axis=-1).reshape(owners, hd, LANES).astype(bf16)
        for b in range(reqs // per)
    ]
    for k in range(owners):
        distance = int(format(k, f"0{owners.bit_length() - 1}b")[::-1], 2)
        target = place_ref[2] ^ distance
        for q in range(reqs):
            for c in range(chunks):
                at = (q * chunks + c) * hd
                out_ref[target, at : at + hd, :] = absorbed[q][k, :, c * LANES : (c + 1) * LANES]
        for b in range(reqs // per):
            at = (reqs * chunks + b) * hd
            out_ref[target, at : at + hd, :] = rope[b][k]


def attend_kernel(reqs, drafts, heads, len_ref, count_ref, q_ref, cos_ref, sin_ref, new_ref, cache_ref, out_ref):
    owners = q_ref.shape[0]
    hd = heads * drafts
    count = owners * hd
    chunks = LATENT // LANES
    per = LANES // ROPE
    slots = cache_ref.shape[2]
    scale = QKD ** (-0.5)
    rotated = []
    for b in range(reqs // per):
        at = (reqs * chunks + b) * hd
        x = q_ref[:, at : at + hd, :].astype(f32).reshape(count, LANES)
        lane = rest(lax.broadcasted_iota(jnp.int32, x.shape, 1), ROPE)
        half = ROPE // 2
        other = jnp.where(lane < half, pltpu.roll(x, LANES - half, 1), pltpu.roll(x, half, 1))
        x = x.reshape(owners, hd, LANES) * cos_ref[b] + other.reshape(owners, hd, LANES) * sin_ref[b]
        x = x.astype(bf16).reshape(count, LANES)
        rotated += [x[:, i * ROPE : (i + 1) * ROPE] for i in range(per)]
    draft = rest(lax.broadcasted_iota(jnp.int32, (count, 1), 0), drafts)
    new_at = lax.broadcasted_iota(jnp.int32, (count, new_ref.shape[0]), 1)
    slot = lax.broadcasted_iota(jnp.int32, (1, slots), 1)
    for q in range(reqs):
        absorbed = jnp.concatenate(
            [
                q_ref[:, (q * chunks + c) * hd : (q * chunks + c + 1) * hd, :].reshape(count, LANES)
                for c in range(chunks)
            ],
            axis=-1,
        )
        keys = cache_ref[q]
        rows = new_ref[...]
        score = (mm(absorbed, keys[:LATENT]) + mm(rotated[q], keys[LATENT:])) * scale
        fresh = (mm_nt(absorbed, rows[:, :LATENT]) + mm_nt(rotated[q], rows[:, LATENT:])) * scale
        score = jnp.where(slot < len_ref[q], score, -jnp.inf)
        seen = (new_at >= q * drafts) & (new_at - q * drafts <= draft)
        fresh = jnp.where(seen, fresh, -jnp.inf)
        peak = jnp.maximum(
            jnp.max(score, axis=1, keepdims=True), jnp.max(fresh, axis=1, keepdims=True)
        )
        score = jnp.exp(score - peak)
        fresh = jnp.exp(fresh - peak)
        total = jnp.sum(score, axis=1, keepdims=True) + jnp.sum(fresh, axis=1, keepdims=True)
        inverse = 1.0 / total
        mix = mm_nt((score * inverse).astype(bf16), keys[:LATENT])
        mix = mix + mm((fresh * inverse).astype(bf16), rows[:, :LATENT])
        mix = jnp.where(draft < count_ref[q], mix, 0.0).astype(bf16)
        out_ref[:, q * hd : (q + 1) * hd, :] = mix.reshape(owners, hd, LATENT)


def value_kernel(drafts, heads, latent_ref, uv_ref, out_ref):
    owners = latent_ref.shape[0]
    hd = heads * drafts
    pair = 2 * drafts
    rows = owners * pair
    low = rest(over(lax.broadcasted_iota(jnp.int32, (rows, LATENT), 0), drafts), 2) == 0
    for h in range(0, heads, 2):
        a = latent_ref[:, h * drafts : h * drafts + pair, :].astype(f32).reshape(rows, LATENT)
        b = latent_ref[:, hd + h * drafts : hd + h * drafts + pair, :].astype(f32).reshape(rows, LATENT)
        first = jnp.where(low, a, pltpu.roll(b, drafts, 0)).astype(bf16)
        second = jnp.where(low, pltpu.roll(a, rows - drafts, 0), b).astype(bf16)
        out_ref[:, h * VDIM : (h + 1) * VDIM] = mm(first, uv_ref[h]).astype(bf16)
        out_ref[:, (h + 1) * VDIM : (h + 2) * VDIM] = mm(second, uv_ref[h + 1]).astype(bf16)


def output_kernel(place_ref, *refs):
    *value_refs, w_own_ref, w_other_ref, out_ref = refs
    replicas, rows, half = out_ref.shape
    own = jnp.concatenate([ref[...] for ref in value_refs[:replicas]], axis=0)
    other = jnp.concatenate([ref[...] for ref in value_refs[replicas:]], axis=0)
    tile = 256 if half % 256 == 0 else half
    start = pl.multiple_of(place_ref[0] * half, LANES) if half % LANES == 0 else 0
    for at in range(0, half, tile):
        part = mm(own, w_own_ref[:, pl.ds(start + at, tile)]) + mm(other, w_other_ref[:, at : at + tile])
        part = part.astype(bf16)
        for k in range(replicas):
            out_ref[place_ref[1] ^ k, :, at : at + tile] = part[k * rows : (k + 1) * rows]


def sum_kernel(replicas, pairs, x_ref, out_ref):
    width = x_ref.shape[-1]
    for r in range(replicas):
        for c in range(2):
            total = None
            for p in range(pairs):
                part = x_ref[(r * pairs + p) * 2 + c].astype(f32)
                total = part if total is None else total + part
            at = (r * 2 + c) * width
            out_ref[:, at : at + width] = total.astype(bf16)


def step(x, axis, size, k):
    return lax.ppermute(x, axis, [(i, i ^ k) for i in range(size)])


def local_step(q_latent, q_gain, q_up, w_uk, w_uv, w_o, new_kv, latent_cache, cache_len, draft_count):
    rows_dev, _ = q_latent.shape
    owners = lax.axis_size("tensor")
    replicas = lax.axis_size("replica")
    heads = w_uk.shape[0]
    reqs = cache_len.shape[0]
    drafts = rows_dev // reqs
    hd = heads * drafts
    me = lax.axis_index("tensor")
    core = me % 2

    place = jnp.stack([core, lax.axis_index("replica"), me]).astype(jnp.int32)
    w_uk = w_uk.reshape(heads * NOPE, LATENT)
    near = fetch((q_up, w_uk, q_gain, q_latent), FETCH_VMEM)

    first = step(q_latent, "tensor", owners, owners // 2)
    first, q_up, w_uk, gain, rows = lax.optimization_barrier((first, *near))
    rows = jnp.concatenate([rows, first], axis=0)
    bit = owners // 4
    while bit > 2:
        rows = jnp.concatenate([rows, step(rows, "tensor", owners, bit)], axis=0)
        bit //= 2
    parts = [rows]
    while bit:
        parts = parts + [step(part, "tensor", owners, bit) for part in parts]
        bit //= 2

    chunks = LATENT // LANES
    packed = (reqs * chunks + reqs * ROPE // LANES) * hd
    params = pltpu.CompilerParams(vmem_limit_bytes=24 * 1024 * 1024)
    queries = pl.pallas_call(
        functools.partial(query_kernel, reqs, drafts, heads),
        out_shape=jax.ShapeDtypeStruct((owners, packed, LANES), bf16),
        in_specs=[smem_spec()] + [vmem_spec()] * (len(parts) + 3),
        out_specs=vmem_spec(),
        compiler_params=params,
        name="query",
    )(place, *parts, gain, q_up, w_uk)
    arrived = lax.all_to_all(queries, "tensor", split_axis=0, concat_axis=0, tiled=True)

    half = w_o.shape[1] // 2
    w_away = lax.dynamic_slice_in_dim(w_o, (1 - core) * half, half, axis=1)
    w_other = step(w_away, "tensor", owners, 1)
    arrived, w_other = lax.optimization_barrier((arrived, w_other))
    w_own = w_o if half % LANES == 0 else lax.dynamic_slice_in_dim(w_o, core * half, half, axis=1)

    frequency = rope_base ** (-(jnp.arange(ROPE // 2).astype(f32) * 2.0 / ROPE))
    positions = (cache_len[:, None] + jnp.arange(drafts)[None, :]).astype(f32)
    angles = positions[:, :, None] * frequency
    per = LANES // ROPE

    def table(first, second):
        lanes = jnp.concatenate([first, second], axis=-1)
        lanes = lanes.reshape(reqs // per, per, drafts, ROPE)
        lanes = jnp.swapaxes(lanes, 1, 2).reshape(reqs // per, 1, drafts, LANES)
        return jnp.broadcast_to(lanes, (reqs // per, heads, drafts, LANES)).reshape(reqs // per, hd, LANES)

    cosine = jnp.cos(angles)
    sine = jnp.sin(angles)
    latent = pl.pallas_call(
        functools.partial(attend_kernel, reqs, drafts, heads),
        out_shape=jax.ShapeDtypeStruct((owners, reqs * hd, LATENT), bf16),
        in_specs=[smem_spec()] * 2 + [vmem_spec()] * 5,
        out_specs=vmem_spec(),
        compiler_params=params,
        name="attend",
    )(cache_len, draft_count, arrived, table(cosine, cosine), table(-sine, sine), new_kv, jnp.swapaxes(latent_cache, 1, 2))
    returned = lax.all_to_all(latent, "tensor", split_axis=0, concat_axis=0, tiled=True)

    values = pl.pallas_call(
        functools.partial(value_kernel, drafts, heads),
        out_shape=jax.ShapeDtypeStruct((owners * rows_dev, heads * VDIM), bf16),
        in_specs=[vmem_spec()] * 2,
        out_specs=vmem_spec(),
        compiler_params=params,
        name="values",
    )(returned, w_uv)
    nearest = step(values, "replica", replicas, 1)
    own = [values, nearest] + [step(values, "replica", replicas, k) for k in range(2, replicas)]
    (w_other,) = fetch((w_other,), 1024 * 1024)
    other = [step(piece, "tensor", owners, 1) for piece in own]

    product = pl.pallas_call(
        output_kernel,
        out_shape=jax.ShapeDtypeStruct((replicas, owners * rows_dev, half), bf16),
        in_specs=[smem_spec()] + [vmem_spec()] * (2 * replicas + 2),
        out_specs=vmem_spec(),
        compiler_params=params,
        name="output",
    )(place, *own, *other, w_own, w_other)
    product = product.reshape(replicas * owners, rows_dev, half)
    placed = lax.all_to_all(product, ("replica", "tensor"), split_axis=0, concat_axis=0, tiled=True)
    return pl.pallas_call(
        functools.partial(sum_kernel, replicas, owners // 2),
        out_shape=jax.ShapeDtypeStruct((rows_dev, replicas * 2 * half), bf16),
        in_specs=[vmem_spec()],
        out_specs=vmem_spec(),
        compiler_params=params,
        name="combine",
    )(placed)


def solution(mesh):
    rows = ("groups", "tensor", "replica")
    return jax.shard_map(
        local_step,
        mesh=mesh,
        in_specs=(
            P(rows, None),
            P(),
            P(None, "tensor"),
            P("tensor", None, None),
            P("tensor", None, None),
            P("tensor", "replica"),
            P(rows, None),
            P(rows, None, None),
            P(rows),
            P(rows),
        ),
        out_specs=P(rows, None),
        check_vma=False,
    )
```

```python
import functools

import jax
import jax.numpy as jnp
from jax import lax
from jax.experimental import pallas as pl
from jax.experimental.pallas import tpu as pltpu
from jax.sharding import PartitionSpec as P


LATENT = 512
ROPE = 64
NOPE = 128
VDIM = 128
QKD = NOPE + ROPE
LANES = 128

FETCH_VMEM = 53_700_000
HALVES_VMEM = 51_000_000

rms_eps = 1e-06
rope_base = 50000.0

VMEM = pltpu.MemorySpace.VMEM
SMEM = pltpu.MemorySpace.SMEM
bf16 = jnp.bfloat16
f32 = jnp.float32


def vmem_spec():
    return pl.BlockSpec(memory_space=VMEM)


def smem_spec():
    return pl.BlockSpec(memory_space=SMEM)


def over(x, n):
    return x >> (n.bit_length() - 1) if n & (n - 1) == 0 else x // n


def rest(x, n):
    return x & (n - 1) if n & (n - 1) == 0 else x % n


def mm(a, b):
    return jnp.dot(a, b, preferred_element_type=f32)


def mm_nt(a, b):
    return lax.dot_general(a, b, (((1,), (1,)), ((), ())), preferred_element_type=f32)


def fetch_kernel(*refs):
    count = len(refs) // 2
    copies = [pltpu.make_async_copy(refs[i], refs[count + i], refs[-1].at[i]) for i in range(count)]
    for copy in copies:
        copy.start()
    for copy in copies:
        copy.wait()


def fetch(arrays, limit):
    return pl.pallas_call(
        fetch_kernel,
        out_shape=[pltpu.VMEM(x.shape, x.dtype) for x in arrays],
        in_specs=[pl.BlockSpec(memory_space=pl.ANY)] * len(arrays),
        out_specs=[vmem_spec()] * len(arrays),
        scratch_shapes=[pltpu.SemaphoreType.DMA((len(arrays),))],
        compiler_params=pltpu.CompilerParams(vmem_limit_bytes=limit),
        cost_estimate=pl.CostEstimate(
            flops=0, bytes_accessed=sum(4 * x.size for x in arrays), transcendentals=0
        ),
    )(*arrays)


def halves_kernel(place_ref, *refs):
    *sources, first, second, sems = refs
    copies = []
    for i, target in enumerate((first, second)):
        source, width = sources[i], target.shape[1]
        if source.shape[1] != width:
            source = source.at[:, pl.ds(pl.multiple_of(place_ref[0] * width, LANES), width)]
        copies.append(pltpu.make_async_copy(source, target, sems.at[i]))
        copies[i].start()
    for copy in copies:
        copy.wait()


def fetch_halves(place, arrays, width):
    depth = arrays[0].shape[0]
    return pl.pallas_call(
        halves_kernel,
        out_shape=[pltpu.VMEM((depth, width), bf16)] * 2,
        in_specs=[smem_spec()] + [pl.BlockSpec(memory_space=pl.ANY)] * 2,
        out_specs=[vmem_spec()] * 2,
        scratch_shapes=[pltpu.SemaphoreType.DMA((2,))],
        compiler_params=pltpu.CompilerParams(vmem_limit_bytes=HALVES_VMEM),
        cost_estimate=pl.CostEstimate(flops=0, bytes_accessed=8 * depth * width, transcendentals=0),
        name="near_output",
    )(place, *arrays)


def regroup(pieces, groups, size):
    assert groups == 2 and len(pieces) % 2 == 0
    rows = lax.broadcasted_iota(jnp.int32, pieces[0].shape, 0)
    low = rest(over(rows, size), 2) == 0
    total = pieces[0].shape[0]
    width = pieces[0].shape[1]
    firsts, seconds = [], []
    for h in range(0, len(pieces), 2):
        a, b = pieces[h], pieces[h + 1]
        firsts.append(jnp.where(low, a, pltpu.roll(b, size, 0)))
        seconds.append(jnp.where(low, pltpu.roll(a, total - size, 0), b))

    def stack(parts):
        parts = [part.reshape(total // (2 * size), 2 * size, width) for part in parts]
        return jnp.concatenate(parts, axis=1).reshape(total * len(parts), width)

    return [stack(firsts), stack(seconds)]


def query_kernel(reqs, drafts, heads, place_ref, *refs):
    *x_refs, gain_ref, up_ref, uk_ref, out_ref = refs
    owners = out_ref.shape[0]
    hd = heads * drafts
    x = jnp.concatenate([x_ref[...] for x_ref in x_refs], axis=0).astype(f32)
    scaled = x * lax.rsqrt(jnp.mean(x * x, axis=-1, keepdims=True) + rms_eps)
    normed = (scaled * gain_ref[...][None, :]).astype(bf16)
    full = mm(normed, up_ref[...]).astype(bf16)
    absorbed = [mm(full[:, h * QKD : h * QKD + NOPE], uk_ref[h * NOPE : (h + 1) * NOPE]) for h in range(heads)]
    rope = [full[:, h * QKD + NOPE : (h + 1) * QKD].astype(f32) for h in range(heads)]
    absorbed = regroup(absorbed, reqs, drafts)
    rope = regroup(rope, reqs, drafts)
    chunks = LATENT // LANES
    per = LANES // ROPE
    absorbed = [x.reshape(owners, hd, LATENT).astype(bf16) for x in absorbed]
    rope = [
        jnp.concatenate(rope[b * per : (b + 1) * per], axis=-1).reshape(owners, hd, LANES).astype(bf16)
        for b in range(reqs // per)
    ]
    for k in range(owners):
        distance = int(format(k, f"0{owners.bit_length() - 1}b")[::-1], 2)
        target = place_ref[2] ^ distance
        for q in range(reqs):
            for c in range(chunks):
                at = (q * chunks + c) * hd
                out_ref[target, at : at + hd, :] = absorbed[q][k, :, c * LANES : (c + 1) * LANES]
        for b in range(reqs // per):
            at = (reqs * chunks + b) * hd
            out_ref[target, at : at + hd, :] = rope[b][k]


def attend_kernel(reqs, drafts, heads, len_ref, count_ref, q_ref, cos_ref, sin_ref, new_ref, cache_ref, out_ref):
    owners = q_ref.shape[0]
    hd = heads * drafts
    count = owners * hd
    chunks = LATENT // LANES
    per = LANES // ROPE
    slots = cache_ref.shape[2]
    scale = QKD ** (-0.5)
    rotated = []
    for b in range(reqs // per):
        at = (reqs * chunks + b) * hd
        x = q_ref[:, at : at + hd, :].astype(f32).reshape(count, LANES)
        lane = rest(lax.broadcasted_iota(jnp.int32, x.shape, 1), ROPE)
        half = ROPE // 2
        other = jnp.where(lane < half, pltpu.roll(x, LANES - half, 1), pltpu.roll(x, half, 1))
        x = x.reshape(owners, hd, LANES) * cos_ref[b] + other.reshape(owners, hd, LANES) * sin_ref[b]
        x = x.astype(bf16).reshape(count, LANES)
        rotated += [x[:, i * ROPE : (i + 1) * ROPE] for i in range(per)]
    draft = rest(lax.broadcasted_iota(jnp.int32, (count, 1), 0), drafts)
    new_at = lax.broadcasted_iota(jnp.int32, (count, new_ref.shape[0]), 1)
    slot = lax.broadcasted_iota(jnp.int32, (1, slots), 1)
    for q in range(reqs):
        absorbed = jnp.concatenate(
            [
                q_ref[:, (q * chunks + c) * hd : (q * chunks + c + 1) * hd, :].reshape(count, LANES)
                for c in range(chunks)
            ],
            axis=-1,
        )
        keys = cache_ref[q]
        rows = new_ref[...]
        score = (mm(absorbed, keys[:LATENT]) + mm(rotated[q], keys[LATENT:])) * scale
        fresh = (mm_nt(absorbed, rows[:, :LATENT]) + mm_nt(rotated[q], rows[:, LATENT:])) * scale
        score = jnp.where(slot < len_ref[q], score, -jnp.inf)
        seen = (new_at >= q * drafts) & (new_at - q * drafts <= draft)
        fresh = jnp.where(seen, fresh, -jnp.inf)
        peak = jnp.maximum(
            jnp.max(score, axis=1, keepdims=True), jnp.max(fresh, axis=1, keepdims=True)
        )
        score = jnp.exp(score - peak)
        fresh = jnp.exp(fresh - peak)
        total = jnp.sum(score, axis=1, keepdims=True) + jnp.sum(fresh, axis=1, keepdims=True)
        inverse = 1.0 / total
        mix = mm_nt((score * inverse).astype(bf16), keys[:LATENT])
        mix = mix + mm((fresh * inverse).astype(bf16), rows[:, :LATENT])
        mix = jnp.where(draft < count_ref[q], mix, 0.0).astype(bf16)
        out_ref[:, q * hd : (q + 1) * hd, :] = mix.reshape(owners, hd, LATENT)


def value_kernel(drafts, heads, latent_ref, uv_ref, out_ref):
    owners = latent_ref.shape[0]
    hd = heads * drafts
    pair = 2 * drafts
    rows = owners * pair
    low = rest(over(lax.broadcasted_iota(jnp.int32, (rows, LATENT), 0), drafts), 2) == 0
    for h in range(0, heads, 2):
        a = latent_ref[:, h * drafts : h * drafts + pair, :].astype(f32).reshape(rows, LATENT)
        b = latent_ref[:, hd + h * drafts : hd + h * drafts + pair, :].astype(f32).reshape(rows, LATENT)
        first = jnp.where(low, a, pltpu.roll(b, drafts, 0)).astype(bf16)
        second = jnp.where(low, pltpu.roll(a, rows - drafts, 0), b).astype(bf16)
        out_ref[:, h * VDIM : (h + 1) * VDIM] = mm(first, uv_ref[h]).astype(bf16)
        out_ref[:, (h + 1) * VDIM : (h + 2) * VDIM] = mm(second, uv_ref[h + 1]).astype(bf16)


def output_kernel(place_ref, *refs):
    *value_refs, w_own_ref, w_other_ref, out_ref = refs
    replicas, rows, half = out_ref.shape
    own = jnp.concatenate([ref[...] for ref in value_refs[:replicas]], axis=0)
    other = jnp.concatenate([ref[...] for ref in value_refs[replicas:]], axis=0)
    tile = 256 if half % 256 == 0 else half
    for at in range(0, half, tile):
        part = mm(own, w_own_ref[:, at : at + tile]) + mm(other, w_other_ref[:, at : at + tile])
        part = part.astype(bf16)
        for k in range(replicas):
            out_ref[place_ref[1] ^ k, :, at : at + tile] = part[k * rows : (k + 1) * rows]


def sum_kernel(replicas, pairs, x_ref, out_ref):
    width = x_ref.shape[-1]
    for r in range(replicas):
        for c in range(2):
            total = None
            for p in range(pairs):
                part = x_ref[(r * pairs + p) * 2 + c].astype(f32)
                total = part if total is None else total + part
            at = (r * 2 + c) * width
            out_ref[:, at : at + width] = total.astype(bf16)


def step(x, axis, size, k):
    return lax.ppermute(x, axis, [(i, i ^ k) for i in range(size)])


def local_step(q_latent, q_gain, q_up, w_uk, w_uv, w_o, new_kv, latent_cache, cache_len, draft_count):
    rows_dev, _ = q_latent.shape
    owners = lax.axis_size("tensor")
    replicas = lax.axis_size("replica")
    heads = w_uk.shape[0]
    reqs = cache_len.shape[0]
    drafts = rows_dev // reqs
    hd = heads * drafts
    me = lax.axis_index("tensor")
    core = me % 2

    place = jnp.stack([core, lax.axis_index("replica"), me]).astype(jnp.int32)
    w_uk = w_uk.reshape(heads * NOPE, LATENT)
    near = fetch((q_up, w_uk, q_gain, q_latent), FETCH_VMEM)

    frequency = rope_base ** (-(jnp.arange(ROPE // 2).astype(f32) * 2.0 / ROPE))
    positions = (cache_len[:, None] + jnp.arange(drafts)[None, :]).astype(f32)
    angles = positions[:, :, None] * frequency
    per = LANES // ROPE

    def table(first, second):
        lanes = jnp.concatenate([first, second], axis=-1)
        lanes = lanes.reshape(reqs // per, per, drafts, ROPE)
        lanes = jnp.swapaxes(lanes, 1, 2).reshape(reqs // per, 1, drafts, LANES)
        return jnp.broadcast_to(lanes, (reqs // per, heads, drafts, LANES)).reshape(reqs // per, hd, LANES)

    cosine = jnp.cos(angles)
    sine = jnp.sin(angles)
    tables = table(cosine, cosine), table(-sine, sine)

    first = step(q_latent, "tensor", owners, owners // 2)
    first, q_up, w_uk, gain, rows, *tables = lax.optimization_barrier((first, *near, *tables))
    rows = jnp.concatenate([rows, first], axis=0)
    bit = owners // 4
    while bit > 2:
        rows = jnp.concatenate([rows, step(rows, "tensor", owners, bit)], axis=0)
        bit //= 2
    parts = [rows]
    while bit:
        parts = parts + [step(part, "tensor", owners, bit) for part in parts]
        bit //= 2

    chunks = LATENT // LANES
    packed = (reqs * chunks + reqs * ROPE // LANES) * hd
    params = pltpu.CompilerParams(vmem_limit_bytes=24 * 1024 * 1024)
    queries = pl.pallas_call(
        functools.partial(query_kernel, reqs, drafts, heads),
        out_shape=jax.ShapeDtypeStruct((owners, packed, LANES), bf16),
        in_specs=[smem_spec()] + [vmem_spec()] * (len(parts) + 3),
        out_specs=vmem_spec(),
        compiler_params=params,
        name="query",
    )(place, *parts, gain, q_up, w_uk)
    arrived = lax.all_to_all(queries, "tensor", split_axis=0, concat_axis=0, tiled=True)

    arrived, w_late = lax.optimization_barrier((arrived, w_o))

    half = w_o.shape[1] // 2
    aligned = half % LANES == 0
    w_own = w_o if aligned else lax.dynamic_slice_in_dim(w_o, core * half, half, axis=1)
    w_away = w_late if aligned else lax.dynamic_slice_in_dim(w_late, (1 - core) * half, half, axis=1)
    w_other = step(w_away, "tensor", owners, 1)

    latent = pl.pallas_call(
        functools.partial(attend_kernel, reqs, drafts, heads),
        out_shape=jax.ShapeDtypeStruct((owners, reqs * hd, LATENT), bf16),
        in_specs=[smem_spec()] * 2 + [vmem_spec()] * 5,
        out_specs=vmem_spec(),
        compiler_params=params,
        name="attend",
    )(cache_len, draft_count, arrived, *tables, new_kv, jnp.swapaxes(latent_cache, 1, 2))
    returned = lax.all_to_all(latent, "tensor", split_axis=0, concat_axis=0, tiled=True)
    returned, w_other = lax.optimization_barrier((returned, w_other))

    values = pl.pallas_call(
        functools.partial(value_kernel, drafts, heads),
        out_shape=jax.ShapeDtypeStruct((owners * rows_dev, heads * VDIM), bf16),
        in_specs=[vmem_spec()] * 2,
        out_specs=vmem_spec(),
        compiler_params=params,
        name="values",
    )(returned, w_uv)
    nearest = step(values, "replica", replicas, 1)
    own = [values, nearest] + [step(values, "replica", replicas, k) for k in range(2, replicas)]
    w_own, w_other = fetch_halves(place, (w_own, w_other), half)
    other = [step(piece, "tensor", owners, 1) for piece in own]

    product = pl.pallas_call(
        output_kernel,
        out_shape=jax.ShapeDtypeStruct((replicas, owners * rows_dev, half), bf16),
        in_specs=[smem_spec()] + [vmem_spec()] * (2 * replicas + 2),
        out_specs=vmem_spec(),
        compiler_params=params,
        name="output",
    )(place, *own, *other, w_own, w_other)
    product = product.reshape(replicas * owners, rows_dev, half)
    placed = lax.all_to_all(product, ("replica", "tensor"), split_axis=0, concat_axis=0, tiled=True)
    return pl.pallas_call(
        functools.partial(sum_kernel, replicas, owners // 2),
        out_shape=jax.ShapeDtypeStruct((rows_dev, replicas * 2 * half), bf16),
        in_specs=[vmem_spec()],
        out_specs=vmem_spec(),
        compiler_params=params,
        name="combine",
    )(placed)


def solution(mesh):
    rows = ("groups", "tensor", "replica")
    return jax.shard_map(
        local_step,
        mesh=mesh,
        in_specs=(
            P(rows, None),
            P(),
            P(None, "tensor"),
            P("tensor", None, None),
            P("tensor", None, None),
            P("tensor", "replica"),
            P(rows, None),
            P(rows, None, None),
            P(rows),
            P(rows),
        ),
        out_specs=P(rows, None),
        check_vma=False,
    )
```

```python
import functools

import jax
import jax.numpy as jnp
from jax import lax
from jax.experimental import pallas as pl
from jax.experimental.pallas import tpu as pltpu
from jax.sharding import PartitionSpec as P


LATENT = 512
ROPE = 64
NOPE = 128
VDIM = 128
QKD = NOPE + ROPE
LANES = 128

FETCH_VMEM = 53_700_000
HALVES_VMEM = 51_000_000

rms_eps = 1e-06
rope_base = 50000.0

VMEM = pltpu.MemorySpace.VMEM
SMEM = pltpu.MemorySpace.SMEM
bf16 = jnp.bfloat16
f32 = jnp.float32


def vmem_spec():
    return pl.BlockSpec(memory_space=VMEM)


def smem_spec():
    return pl.BlockSpec(memory_space=SMEM)


def over(x, n):
    return x >> (n.bit_length() - 1) if n & (n - 1) == 0 else x // n


def rest(x, n):
    return x & (n - 1) if n & (n - 1) == 0 else x % n


def mm(a, b):
    return jnp.dot(a, b, preferred_element_type=f32)


def mm_nt(a, b):
    return lax.dot_general(a, b, (((1,), (1,)), ((), ())), preferred_element_type=f32)


def fetch_kernel(*refs):
    count = len(refs) // 2
    copies = [pltpu.make_async_copy(refs[i], refs[count + i], refs[-1].at[i]) for i in range(count)]
    for copy in copies:
        copy.start()
    for copy in copies:
        copy.wait()


def fetch(arrays, limit):
    return pl.pallas_call(
        fetch_kernel,
        out_shape=[pltpu.VMEM(x.shape, x.dtype) for x in arrays],
        in_specs=[pl.BlockSpec(memory_space=pl.ANY)] * len(arrays),
        out_specs=[vmem_spec()] * len(arrays),
        scratch_shapes=[pltpu.SemaphoreType.DMA((len(arrays),))],
        compiler_params=pltpu.CompilerParams(vmem_limit_bytes=limit),
        cost_estimate=pl.CostEstimate(
            flops=0, bytes_accessed=sum(4 * x.size for x in arrays), transcendentals=0
        ),
    )(*arrays)


def halves_kernel(place_ref, *refs):
    *sources, first, second, sems = refs
    copies = []
    for i, target in enumerate((first, second)):
        source, width = sources[i], target.shape[1]
        if source.shape[1] != width:
            source = source.at[:, pl.ds(pl.multiple_of(place_ref[0] * width, LANES), width)]
        copies.append(pltpu.make_async_copy(source, target, sems.at[i]))
        copies[i].start()
    for copy in copies:
        copy.wait()


def fetch_halves(place, arrays, width):
    depth = arrays[0].shape[0]
    return pl.pallas_call(
        halves_kernel,
        out_shape=[pltpu.VMEM((depth, width), bf16)] * 2,
        in_specs=[smem_spec()] + [pl.BlockSpec(memory_space=pl.ANY)] * 2,
        out_specs=[vmem_spec()] * 2,
        scratch_shapes=[pltpu.SemaphoreType.DMA((2,))],
        compiler_params=pltpu.CompilerParams(vmem_limit_bytes=HALVES_VMEM),
        cost_estimate=pl.CostEstimate(flops=0, bytes_accessed=8 * depth * width, transcendentals=0),
        name="near_output",
    )(place, *arrays)


def regroup(pieces, groups, size):
    assert groups == 2 and len(pieces) % 2 == 0
    rows = lax.broadcasted_iota(jnp.int32, pieces[0].shape, 0)
    low = rest(over(rows, size), 2) == 0
    total = pieces[0].shape[0]
    width = pieces[0].shape[1]
    firsts, seconds = [], []
    for h in range(0, len(pieces), 2):
        a, b = pieces[h], pieces[h + 1]
        firsts.append(jnp.where(low, a, pltpu.roll(b, size, 0)))
        seconds.append(jnp.where(low, pltpu.roll(a, total - size, 0), b))

    def stack(parts):
        parts = [part.reshape(total // (2 * size), 2 * size, width) for part in parts]
        return jnp.concatenate(parts, axis=1).reshape(total * len(parts), width)

    return [stack(firsts), stack(seconds)]


def query_kernel(reqs, drafts, heads, place_ref, *refs):
    *x_refs, gain_ref, up_ref, uk_ref, out_ref = refs
    owners = out_ref.shape[0]
    hd = heads * drafts
    x = jnp.concatenate([x_ref[...] for x_ref in x_refs], axis=0).astype(f32)
    scaled = x * lax.rsqrt(jnp.mean(x * x, axis=-1, keepdims=True) + rms_eps)
    normed = (scaled * gain_ref[...][None, :]).astype(bf16)
    full = mm(normed, up_ref[...]).astype(bf16)
    absorbed = [mm(full[:, h * QKD : h * QKD + NOPE], uk_ref[h * NOPE : (h + 1) * NOPE]) for h in range(heads)]
    rope = [full[:, h * QKD + NOPE : (h + 1) * QKD].astype(f32) for h in range(heads)]
    absorbed = regroup(absorbed, reqs, drafts)
    rope = regroup(rope, reqs, drafts)
    chunks = LATENT // LANES
    per = LANES // ROPE
    absorbed = [x.reshape(owners, hd, LATENT).astype(bf16) for x in absorbed]
    rope = [
        jnp.concatenate(rope[b * per : (b + 1) * per], axis=-1).reshape(owners, hd, LANES).astype(bf16)
        for b in range(reqs // per)
    ]
    for k in range(owners):
        distance = int(format(k, f"0{owners.bit_length() - 1}b")[::-1], 2)
        target = place_ref[2] ^ distance
        for q in range(reqs):
            for c in range(chunks):
                at = (q * chunks + c) * hd
                out_ref[target, at : at + hd, :] = absorbed[q][k, :, c * LANES : (c + 1) * LANES]
        for b in range(reqs // per):
            at = (reqs * chunks + b) * hd
            out_ref[target, at : at + hd, :] = rope[b][k]


def attend_kernel(reqs, drafts, heads, len_ref, count_ref, q_ref, frequency_ref, new_ref, cache_ref, out_ref):
    owners = q_ref.shape[0]
    hd = heads * drafts
    count = owners * hd
    chunks = LATENT // LANES
    per = LANES // ROPE
    slots = cache_ref.shape[2]
    scale = QKD ** (-0.5)
    rotated = []
    for b in range(reqs // per):
        at = (reqs * chunks + b) * hd
        x = q_ref[:, at : at + hd, :].astype(f32).reshape(count, LANES)
        half = ROPE // 2
        low = rest(lax.broadcasted_iota(jnp.int32, x.shape, 1), ROPE) < half
        other = jnp.where(low, pltpu.roll(x, LANES - half, 1), pltpu.roll(x, half, 1))
        lane = lax.broadcasted_iota(jnp.int32, (hd, LANES), 1)
        length = jnp.zeros_like(lane)
        for i in range(per):
            length = jnp.where(over(lane, ROPE) == i, len_ref[b * per + i], length)
        position = length + rest(lax.broadcasted_iota(jnp.int32, (hd, LANES), 0), drafts)
        angle = position.astype(f32) * frequency_ref[...]
        sine = jnp.sin(angle)
        sine = jnp.where(rest(lane, ROPE) < half, -sine, sine)
        x = x.reshape(owners, hd, LANES) * jnp.cos(angle) + other.reshape(owners, hd, LANES) * sine
        x = x.astype(bf16).reshape(count, LANES)
        rotated += [x[:, i * ROPE : (i + 1) * ROPE] for i in range(per)]
    draft = rest(lax.broadcasted_iota(jnp.int32, (count, 1), 0), drafts)
    new_at = lax.broadcasted_iota(jnp.int32, (count, new_ref.shape[0]), 1)
    slot = lax.broadcasted_iota(jnp.int32, (1, slots), 1)
    for q in range(reqs):
        absorbed = jnp.concatenate(
            [
                q_ref[:, (q * chunks + c) * hd : (q * chunks + c + 1) * hd, :].reshape(count, LANES)
                for c in range(chunks)
            ],
            axis=-1,
        )
        keys = cache_ref[q]
        rows = new_ref[...]
        score = (mm(absorbed, keys[:LATENT]) + mm(rotated[q], keys[LATENT:])) * scale
        fresh = (mm_nt(absorbed, rows[:, :LATENT]) + mm_nt(rotated[q], rows[:, LATENT:])) * scale
        score = jnp.where(slot < len_ref[q], score, -jnp.inf)
        seen = (new_at >= q * drafts) & (new_at - q * drafts <= draft)
        fresh = jnp.where(seen, fresh, -jnp.inf)
        peak = jnp.maximum(
            jnp.max(score, axis=1, keepdims=True), jnp.max(fresh, axis=1, keepdims=True)
        )
        score = jnp.exp(score - peak)
        fresh = jnp.exp(fresh - peak)
        total = jnp.sum(score, axis=1, keepdims=True) + jnp.sum(fresh, axis=1, keepdims=True)
        inverse = 1.0 / total
        mix = mm_nt((score * inverse).astype(bf16), keys[:LATENT])
        mix = mix + mm((fresh * inverse).astype(bf16), rows[:, :LATENT])
        mix = jnp.where(draft < count_ref[q], mix, 0.0).astype(bf16)
        out_ref[:, q * hd : (q + 1) * hd, :] = mix.reshape(owners, hd, LATENT)


def value_kernel(drafts, heads, latent_ref, uv_ref, out_ref):
    owners = latent_ref.shape[0]
    hd = heads * drafts
    pair = 2 * drafts
    rows = owners * pair
    low = rest(over(lax.broadcasted_iota(jnp.int32, (rows, LATENT), 0), drafts), 2) == 0
    for h in range(0, heads, 2):
        a = latent_ref[:, h * drafts : h * drafts + pair, :].astype(f32).reshape(rows, LATENT)
        b = latent_ref[:, hd + h * drafts : hd + h * drafts + pair, :].astype(f32).reshape(rows, LATENT)
        first = jnp.where(low, a, pltpu.roll(b, drafts, 0)).astype(bf16)
        second = jnp.where(low, pltpu.roll(a, rows - drafts, 0), b).astype(bf16)
        out_ref[:, h * VDIM : (h + 1) * VDIM] = mm(first, uv_ref[h]).astype(bf16)
        out_ref[:, (h + 1) * VDIM : (h + 2) * VDIM] = mm(second, uv_ref[h + 1]).astype(bf16)


def output_kernel(place_ref, *refs):
    *value_refs, w_own_ref, w_other_ref, out_ref = refs
    replicas, rows, half = out_ref.shape
    own = jnp.concatenate([ref[...] for ref in value_refs[:replicas]], axis=0)
    other = jnp.concatenate([ref[...] for ref in value_refs[replicas:]], axis=0)
    tile = 256 if half % 256 == 0 else half
    for at in range(0, half, tile):
        part = mm(own, w_own_ref[:, at : at + tile]) + mm(other, w_other_ref[:, at : at + tile])
        part = part.astype(bf16)
        for k in range(replicas):
            out_ref[place_ref[1] ^ k, :, at : at + tile] = part[k * rows : (k + 1) * rows]


def sum_kernel(replicas, pairs, x_ref, out_ref):
    width = x_ref.shape[-1]
    for r in range(replicas):
        for c in range(2):
            total = None
            for p in range(pairs):
                part = x_ref[(r * pairs + p) * 2 + c].astype(f32)
                total = part if total is None else total + part
            at = (r * 2 + c) * width
            out_ref[:, at : at + width] = total.astype(bf16)


def step(x, axis, size, k):
    return lax.ppermute(x, axis, [(i, i ^ k) for i in range(size)])


def local_step(q_latent, q_gain, q_up, w_uk, w_uv, w_o, new_kv, latent_cache, cache_len, draft_count):
    rows_dev, _ = q_latent.shape
    owners = lax.axis_size("tensor")
    replicas = lax.axis_size("replica")
    heads = w_uk.shape[0]
    reqs = cache_len.shape[0]
    drafts = rows_dev // reqs
    hd = heads * drafts
    me = lax.axis_index("tensor")
    core = me % 2

    place = jnp.stack([core, lax.axis_index("replica"), me]).astype(jnp.int32)
    w_uk = w_uk.reshape(heads * NOPE, LATENT)
    near = fetch((q_up, w_uk, q_gain, q_latent), FETCH_VMEM)

    lane_pair = jnp.arange(LANES) % (ROPE // 2)
    frequency = (rope_base ** (-(lane_pair.astype(f32) * 2.0 / ROPE)))[None, :]

    first = step(q_latent, "tensor", owners, owners // 2)
    first, q_up, w_uk, gain, rows, frequency = lax.optimization_barrier((first, *near, frequency))
    rows = jnp.concatenate([rows, first], axis=0)
    bit = owners // 4
    while bit > 2:
        rows = jnp.concatenate([rows, step(rows, "tensor", owners, bit)], axis=0)
        bit //= 2
    parts = [rows]
    while bit:
        parts = parts + [step(part, "tensor", owners, bit) for part in parts]
        bit //= 2

    chunks = LATENT // LANES
    packed = (reqs * chunks + reqs * ROPE // LANES) * hd
    params = pltpu.CompilerParams(vmem_limit_bytes=24 * 1024 * 1024)
    queries = pl.pallas_call(
        functools.partial(query_kernel, reqs, drafts, heads),
        out_shape=jax.ShapeDtypeStruct((owners, packed, LANES), bf16),
        in_specs=[smem_spec()] + [vmem_spec()] * (len(parts) + 3),
        out_specs=vmem_spec(),
        compiler_params=params,
        name="query",
    )(place, *parts, gain, q_up, w_uk)
    arrived = lax.all_to_all(queries, "tensor", split_axis=0, concat_axis=0, tiled=True)

    arrived, w_late = lax.optimization_barrier((arrived, w_o))

    half = w_o.shape[1] // 2
    aligned = half % LANES == 0
    w_own = w_o if aligned else lax.dynamic_slice_in_dim(w_o, core * half, half, axis=1)
    w_away = w_late if aligned else lax.dynamic_slice_in_dim(w_late, (1 - core) * half, half, axis=1)
    w_other = step(w_away, "tensor", owners, 1)

    latent = pl.pallas_call(
        functools.partial(attend_kernel, reqs, drafts, heads),
        out_shape=jax.ShapeDtypeStruct((owners, reqs * hd, LATENT), bf16),
        in_specs=[smem_spec()] * 2 + [vmem_spec()] * 4,
        out_specs=vmem_spec(),
        compiler_params=params,
        name="attend",
    )(cache_len, draft_count, arrived, frequency, new_kv, jnp.swapaxes(latent_cache, 1, 2))
    returned = lax.all_to_all(latent, "tensor", split_axis=0, concat_axis=0, tiled=True)
    returned, w_other = lax.optimization_barrier((returned, w_other))

    values = pl.pallas_call(
        functools.partial(value_kernel, drafts, heads),
        out_shape=jax.ShapeDtypeStruct((owners * rows_dev, heads * VDIM), bf16),
        in_specs=[vmem_spec()] * 2,
        out_specs=vmem_spec(),
        compiler_params=params,
        name="values",
    )(returned, w_uv)
    nearest = step(values, "replica", replicas, 1)
    own = [values, nearest] + [step(values, "replica", replicas, k) for k in range(2, replicas)]
    w_own, w_other = fetch_halves(place, (w_own, w_other), half)
    other = [step(piece, "tensor", owners, 1) for piece in own]

    product = pl.pallas_call(
        output_kernel,
        out_shape=jax.ShapeDtypeStruct((replicas, owners * rows_dev, half), bf16),
        in_specs=[smem_spec()] + [vmem_spec()] * (2 * replicas + 2),
        out_specs=vmem_spec(),
        compiler_params=params,
        name="output",
    )(place, *own, *other, w_own, w_other)
    product = product.reshape(replicas * owners, rows_dev, half)
    placed = lax.all_to_all(product, ("replica", "tensor"), split_axis=0, concat_axis=0, tiled=True)
    return pl.pallas_call(
        functools.partial(sum_kernel, replicas, owners // 2),
        out_shape=jax.ShapeDtypeStruct((rows_dev, replicas * 2 * half), bf16),
        in_specs=[vmem_spec()],
        out_specs=vmem_spec(),
        compiler_params=params,
        name="combine",
    )(placed)


def solution(mesh):
    rows = ("groups", "tensor", "replica")
    return jax.shard_map(
        local_step,
        mesh=mesh,
        in_specs=(
            P(rows, None),
            P(),
            P(None, "tensor"),
            P("tensor", None, None),
            P("tensor", None, None),
            P("tensor", "replica"),
            P(rows, None),
            P(rows, None, None),
            P(rows),
            P(rows),
        ),
        out_specs=P(rows, None),
        check_vma=False,
    )
```

```python
import functools

import jax
import jax.numpy as jnp
from jax import lax
from jax.experimental import pallas as pl
from jax.experimental.pallas import tpu as pltpu
from jax.sharding import PartitionSpec as P


LATENT = 512
ROPE = 64
NOPE = 128
VDIM = 128
QKD = NOPE + ROPE
LANES = 128

FETCH_VMEM = 53_700_000
HALVES_VMEM = 51_000_000

rms_eps = 1e-06
rope_base = 50000.0

VMEM = pltpu.MemorySpace.VMEM
SMEM = pltpu.MemorySpace.SMEM
bf16 = jnp.bfloat16
f32 = jnp.float32


def vmem_spec():
    return pl.BlockSpec(memory_space=VMEM)


def smem_spec():
    return pl.BlockSpec(memory_space=SMEM)


def over(x, n):
    return x >> (n.bit_length() - 1) if n & (n - 1) == 0 else x // n


def rest(x, n):
    return x & (n - 1) if n & (n - 1) == 0 else x % n


def mm(a, b):
    return jnp.dot(a, b, preferred_element_type=f32)


def mm_nt(a, b):
    return lax.dot_general(a, b, (((1,), (1,)), ((), ())), preferred_element_type=f32)


def fetch_kernel(*refs):
    count = len(refs) // 2
    copies = [pltpu.make_async_copy(refs[i], refs[count + i], refs[-1].at[i]) for i in range(count)]
    for copy in copies:
        copy.start()
    for copy in copies:
        copy.wait()


def fetch(arrays, limit):
    return pl.pallas_call(
        fetch_kernel,
        out_shape=[pltpu.VMEM(x.shape, x.dtype) for x in arrays],
        in_specs=[pl.BlockSpec(memory_space=pl.ANY)] * len(arrays),
        out_specs=[vmem_spec()] * len(arrays),
        scratch_shapes=[pltpu.SemaphoreType.DMA((len(arrays),))],
        compiler_params=pltpu.CompilerParams(vmem_limit_bytes=limit),
        cost_estimate=pl.CostEstimate(
            flops=0, bytes_accessed=sum(4 * x.size for x in arrays), transcendentals=0
        ),
    )(*arrays)


def halves_kernel(place_ref, *refs):
    *sources, first, second, sems = refs
    copies = []
    for i, target in enumerate((first, second)):
        source, width = sources[i], target.shape[1]
        if source.shape[1] != width:
            source = source.at[:, pl.ds(pl.multiple_of(place_ref[0] * width, LANES), width)]
        copies.append(pltpu.make_async_copy(source, target, sems.at[i]))
        copies[i].start()
    for copy in copies:
        copy.wait()


def fetch_halves(place, arrays, width):
    depth = arrays[0].shape[0]
    return pl.pallas_call(
        halves_kernel,
        out_shape=[pltpu.VMEM((depth, width), bf16)] * 2,
        in_specs=[smem_spec()] + [pl.BlockSpec(memory_space=pl.ANY)] * 2,
        out_specs=[vmem_spec()] * 2,
        scratch_shapes=[pltpu.SemaphoreType.DMA((2,))],
        compiler_params=pltpu.CompilerParams(vmem_limit_bytes=HALVES_VMEM),
        cost_estimate=pl.CostEstimate(flops=0, bytes_accessed=8 * depth * width, transcendentals=0),
        name="near_output",
    )(place, *arrays)


def regroup(pieces, groups, size):
    assert groups == 2 and len(pieces) % 2 == 0
    rows = lax.broadcasted_iota(jnp.int32, pieces[0].shape, 0)
    low = rest(over(rows, size), 2) == 0
    total = pieces[0].shape[0]
    width = pieces[0].shape[1]
    firsts, seconds = [], []
    for h in range(0, len(pieces), 2):
        a, b = pieces[h], pieces[h + 1]
        firsts.append(jnp.where(low, a, pltpu.roll(b, size, 0)))
        seconds.append(jnp.where(low, pltpu.roll(a, total - size, 0), b))

    def stack(parts):
        parts = [part.reshape(total // (2 * size), 2 * size, width) for part in parts]
        return jnp.concatenate(parts, axis=1).reshape(total * len(parts), width)

    return [stack(firsts), stack(seconds)]


def query_kernel(reqs, drafts, heads, place_ref, *refs):
    *x_refs, gain_ref, up_ref, uk_ref, out_ref = refs
    owners = out_ref.shape[0]
    hd = heads * drafts
    x = jnp.concatenate([x_ref[...] for x_ref in x_refs], axis=0).astype(f32)
    scaled = x * lax.rsqrt(jnp.mean(x * x, axis=-1, keepdims=True) + rms_eps)
    normed = (scaled * gain_ref[...][None, :]).astype(bf16)
    full = mm(normed, up_ref[...]).astype(bf16)
    absorbed = [mm(full[:, h * QKD : h * QKD + NOPE], uk_ref[h * NOPE : (h + 1) * NOPE]) for h in range(heads)]
    rope = [full[:, h * QKD + NOPE : (h + 1) * QKD].astype(f32) for h in range(heads)]
    absorbed = regroup(absorbed, reqs, drafts)
    rope = regroup(rope, reqs, drafts)
    chunks = LATENT // LANES
    per = LANES // ROPE
    absorbed = [x.reshape(owners, hd, LATENT).astype(bf16) for x in absorbed]
    rope = [
        jnp.concatenate(rope[b * per : (b + 1) * per], axis=-1).reshape(owners, hd, LANES).astype(bf16)
        for b in range(reqs // per)
    ]
    for k in range(owners):
        distance = int(format(k, f"0{owners.bit_length() - 1}b")[::-1], 2)
        target = place_ref[2] ^ distance
        for q in range(reqs):
            for c in range(chunks):
                at = (q * chunks + c) * hd
                out_ref[target, at : at + hd, :] = absorbed[q][k, :, c * LANES : (c + 1) * LANES]
        for b in range(reqs // per):
            at = (reqs * chunks + b) * hd
            out_ref[target, at : at + hd, :] = rope[b][k]


def attend_kernel(reqs, drafts, heads, len_ref, count_ref, q_ref, frequency_ref, new_ref, cache_ref, out_ref):
    owners = q_ref.shape[0]
    hd = heads * drafts
    count = owners * hd
    chunks = LATENT // LANES
    per = LANES // ROPE
    slots = cache_ref.shape[2]
    scale = QKD ** (-0.5)
    rotated = []
    for b in range(reqs // per):
        at = (reqs * chunks + b) * hd
        x = q_ref[:, at : at + hd, :].astype(f32).reshape(count, LANES)
        half = ROPE // 2
        low = rest(lax.broadcasted_iota(jnp.int32, x.shape, 1), ROPE) < half
        other = jnp.where(low, pltpu.roll(x, LANES - half, 1), pltpu.roll(x, half, 1))
        lane = lax.broadcasted_iota(jnp.int32, (hd, LANES), 1)
        length = jnp.zeros_like(lane)
        for i in range(per):
            length = jnp.where(over(lane, ROPE) == i, len_ref[b * per + i], length)
        position = length + rest(lax.broadcasted_iota(jnp.int32, (hd, LANES), 0), drafts)
        angle = position.astype(f32) * frequency_ref[...]
        sine = jnp.sin(angle)
        sine = jnp.where(rest(lane, ROPE) < half, -sine, sine)
        x = x.reshape(owners, hd, LANES) * jnp.cos(angle) + other.reshape(owners, hd, LANES) * sine
        x = x.astype(bf16).reshape(count, LANES)
        rotated += [x[:, i * ROPE : (i + 1) * ROPE] for i in range(per)]
    draft = rest(lax.broadcasted_iota(jnp.int32, (count, 1), 0), drafts)
    new_at = lax.broadcasted_iota(jnp.int32, (count, new_ref.shape[0]), 1)
    slot = lax.broadcasted_iota(jnp.int32, (1, slots), 1)
    for q in range(reqs):
        absorbed = jnp.concatenate(
            [
                q_ref[:, (q * chunks + c) * hd : (q * chunks + c + 1) * hd, :].reshape(count, LANES)
                for c in range(chunks)
            ],
            axis=-1,
        )
        keys = cache_ref[q]
        rows = new_ref[...]
        score = (mm(absorbed, keys[:LATENT]) + mm(rotated[q], keys[LATENT:])) * scale
        fresh = (mm_nt(absorbed, rows[:, :LATENT]) + mm_nt(rotated[q], rows[:, LATENT:])) * scale
        score = jnp.where(slot < len_ref[q], score, -jnp.inf)
        seen = (new_at >= q * drafts) & (new_at - q * drafts <= draft)
        fresh = jnp.where(seen, fresh, -jnp.inf)
        peak = jnp.maximum(
            jnp.max(score, axis=1, keepdims=True), jnp.max(fresh, axis=1, keepdims=True)
        )
        score = jnp.exp(score - peak)
        fresh = jnp.exp(fresh - peak)
        total = jnp.sum(score, axis=1, keepdims=True) + jnp.sum(fresh, axis=1, keepdims=True)
        inverse = 1.0 / total
        mix = mm_nt((score * inverse).astype(bf16), keys[:LATENT])
        mix = mix + mm((fresh * inverse).astype(bf16), rows[:, :LATENT])
        mix = jnp.where(draft < count_ref[q], mix, 0.0).astype(bf16)
        out_ref[:, q * hd : (q + 1) * hd, :] = mix.reshape(owners, hd, LATENT)


def value_kernel(drafts, heads, latent_ref, uv_ref, out_ref):
    owners = latent_ref.shape[0]
    hd = heads * drafts
    pair = 2 * drafts
    rows = owners * pair
    low = rest(over(lax.broadcasted_iota(jnp.int32, (rows, LATENT), 0), drafts), 2) == 0
    for h in range(0, heads, 2):
        a = latent_ref[:, h * drafts : h * drafts + pair, :].astype(f32).reshape(rows, LATENT)
        b = latent_ref[:, hd + h * drafts : hd + h * drafts + pair, :].astype(f32).reshape(rows, LATENT)
        first = jnp.where(low, a, pltpu.roll(b, drafts, 0)).astype(bf16)
        second = jnp.where(low, pltpu.roll(a, rows - drafts, 0), b).astype(bf16)
        out_ref[:, h * VDIM : (h + 1) * VDIM] = mm(first, uv_ref[h]).astype(bf16)
        out_ref[:, (h + 1) * VDIM : (h + 2) * VDIM] = mm(second, uv_ref[h + 1]).astype(bf16)


def output_kernel(place_ref, *refs):
    *value_refs, w_own_ref, w_other_ref, out_ref = refs
    replicas, rows, half = out_ref.shape
    own = jnp.concatenate([ref[...] for ref in value_refs[:replicas]], axis=0)
    other = jnp.concatenate([ref[...] for ref in value_refs[replicas:]], axis=0)
    tile = 256 if half % 256 == 0 else half
    for at in range(0, half, tile):
        part = mm(own, w_own_ref[:, at : at + tile]) + mm(other, w_other_ref[:, at : at + tile])
        part = part.astype(bf16)
        for k in range(replicas):
            out_ref[place_ref[1] ^ k, :, at : at + tile] = part[k * rows : (k + 1) * rows]


def sum_kernel(replicas, pairs, x_ref, out_ref):
    width = x_ref.shape[-1]
    for r in range(replicas):
        for c in range(2):
            total = None
            for p in range(pairs):
                part = x_ref[(r * pairs + p) * 2 + c].astype(f32)
                total = part if total is None else total + part
            at = (r * 2 + c) * width
            out_ref[:, at : at + width] = total.astype(bf16)


def step(x, axis, size, k):
    return lax.ppermute(x, axis, [(i, i ^ k) for i in range(size)])


def local_step(q_latent, q_gain, q_up, w_uk, w_uv, w_o, new_kv, latent_cache, cache_len, draft_count):
    rows_dev, _ = q_latent.shape
    owners = lax.axis_size("tensor")
    replicas = lax.axis_size("replica")
    heads = w_uk.shape[0]
    reqs = cache_len.shape[0]
    drafts = rows_dev // reqs
    hd = heads * drafts
    me = lax.axis_index("tensor")
    core = me % 2

    place = jnp.stack([core, lax.axis_index("replica"), me]).astype(jnp.int32)
    w_uk = w_uk.reshape(heads * NOPE, LATENT)
    near = fetch((q_up, w_uk, q_gain, q_latent), FETCH_VMEM)

    lane_pair = jnp.arange(LANES) % (ROPE // 2)
    frequency = (rope_base ** (-(lane_pair.astype(f32) * 2.0 / ROPE)))[None, :]

    first = step(q_latent, "tensor", owners, owners // 2)
    first, q_up, w_uk, gain, rows, frequency = lax.optimization_barrier((first, *near, frequency))
    rows = jnp.concatenate([rows, first], axis=0)
    bit = owners // 4
    while bit > 4:
        rows = jnp.concatenate([rows, step(rows, "tensor", owners, bit)], axis=0)
        bit //= 2
    parts = [rows]
    if bit == 4:
        parts = parts + [step(rows, "tensor", owners, k) for k in (4, 2, 6)]
        bit = 1
    while bit:
        parts = parts + [step(part, "tensor", owners, bit) for part in parts]
        bit //= 2

    chunks = LATENT // LANES
    packed = (reqs * chunks + reqs * ROPE // LANES) * hd
    params = pltpu.CompilerParams(vmem_limit_bytes=24 * 1024 * 1024)
    queries = pl.pallas_call(
        functools.partial(query_kernel, reqs, drafts, heads),
        out_shape=jax.ShapeDtypeStruct((owners, packed, LANES), bf16),
        in_specs=[smem_spec()] + [vmem_spec()] * (len(parts) + 3),
        out_specs=vmem_spec(),
        compiler_params=params,
        name="query",
    )(place, *parts, gain, q_up, w_uk)
    arrived = lax.all_to_all(queries, "tensor", split_axis=0, concat_axis=0, tiled=True)

    arrived, w_late = lax.optimization_barrier((arrived, w_o))

    half = w_o.shape[1] // 2
    aligned = half % LANES == 0
    w_own = w_o if aligned else lax.dynamic_slice_in_dim(w_o, core * half, half, axis=1)
    w_away = w_late if aligned else lax.dynamic_slice_in_dim(w_late, (1 - core) * half, half, axis=1)
    w_other = step(w_away, "tensor", owners, 1)

    latent = pl.pallas_call(
        functools.partial(attend_kernel, reqs, drafts, heads),
        out_shape=jax.ShapeDtypeStruct((owners, reqs * hd, LATENT), bf16),
        in_specs=[smem_spec()] * 2 + [vmem_spec()] * 4,
        out_specs=vmem_spec(),
        compiler_params=params,
        name="attend",
    )(cache_len, draft_count, arrived, frequency, new_kv, jnp.swapaxes(latent_cache, 1, 2))
    returned = lax.all_to_all(latent, "tensor", split_axis=0, concat_axis=0, tiled=True)
    returned, w_other = lax.optimization_barrier((returned, w_other))

    values = pl.pallas_call(
        functools.partial(value_kernel, drafts, heads),
        out_shape=jax.ShapeDtypeStruct((owners * rows_dev, heads * VDIM), bf16),
        in_specs=[vmem_spec()] * 2,
        out_specs=vmem_spec(),
        compiler_params=params,
        name="values",
    )(returned, w_uv)
    nearest = step(values, "replica", replicas, 1)
    own = [values, nearest] + [step(values, "replica", replicas, k) for k in range(2, replicas)]
    w_own, w_other = fetch_halves(place, (w_own, w_other), half)
    other = [step(piece, "tensor", owners, 1) for piece in own]

    product = pl.pallas_call(
        output_kernel,
        out_shape=jax.ShapeDtypeStruct((replicas, owners * rows_dev, half), bf16),
        in_specs=[smem_spec()] + [vmem_spec()] * (2 * replicas + 2),
        out_specs=vmem_spec(),
        compiler_params=params,
        name="output",
    )(place, *own, *other, w_own, w_other)
    product = product.reshape(replicas * owners, rows_dev, half)
    placed = lax.all_to_all(product, ("replica", "tensor"), split_axis=0, concat_axis=0, tiled=True)
    return pl.pallas_call(
        functools.partial(sum_kernel, replicas, owners // 2),
        out_shape=jax.ShapeDtypeStruct((rows_dev, replicas * 2 * half), bf16),
        in_specs=[vmem_spec()],
        out_specs=vmem_spec(),
        compiler_params=params,
        name="combine",
    )(placed)


def solution(mesh):
    rows = ("groups", "tensor", "replica")
    return jax.shard_map(
        local_step,
        mesh=mesh,
        in_specs=(
            P(rows, None),
            P(),
            P(None, "tensor"),
            P("tensor", None, None),
            P("tensor", None, None),
            P("tensor", "replica"),
            P(rows, None),
            P(rows, None, None),
            P(rows),
            P(rows),
        ),
        out_specs=P(rows, None),
        check_vma=False,
    )
```

```python
import functools
import math

import jax
import jax.numpy as jnp
from jax import lax
from jax.experimental import pallas as pl
from jax.experimental.pallas import tpu as pltpu
from jax.sharding import PartitionSpec as P


LATENT = 512
ROPE = 64
NOPE = 128
VDIM = 128
QKD = NOPE + ROPE
LANES = 128

FETCH_VMEM = 53_700_000
HALVES_VMEM = 51_000_000

rms_eps = 1e-06
rope_base = 50000.0

VMEM = pltpu.MemorySpace.VMEM
SMEM = pltpu.MemorySpace.SMEM
bf16 = jnp.bfloat16
f32 = jnp.float32


def vmem_spec():
    return pl.BlockSpec(memory_space=VMEM)


def smem_spec():
    return pl.BlockSpec(memory_space=SMEM)


def over(x, n):
    return x >> (n.bit_length() - 1) if n & (n - 1) == 0 else x // n


def rest(x, n):
    return x & (n - 1) if n & (n - 1) == 0 else x % n


def mm(a, b):
    return jnp.dot(a, b, preferred_element_type=f32)


def mm_nt(a, b):
    return lax.dot_general(a, b, (((1,), (1,)), ((), ())), preferred_element_type=f32)


def fetch_kernel(*refs):
    count = len(refs) // 2
    copies = [pltpu.make_async_copy(refs[i], refs[count + i], refs[-1].at[i]) for i in range(count)]
    for copy in copies:
        copy.start()
    for copy in copies:
        copy.wait()


def fetch(arrays, limit):
    return pl.pallas_call(
        fetch_kernel,
        out_shape=[pltpu.VMEM(x.shape, x.dtype) for x in arrays],
        in_specs=[pl.BlockSpec(memory_space=pl.ANY)] * len(arrays),
        out_specs=[vmem_spec()] * len(arrays),
        scratch_shapes=[pltpu.SemaphoreType.DMA((len(arrays),))],
        compiler_params=pltpu.CompilerParams(vmem_limit_bytes=limit),
        cost_estimate=pl.CostEstimate(
            flops=0, bytes_accessed=sum(4 * x.size for x in arrays), transcendentals=0
        ),
    )(*arrays)


def halves_kernel(place_ref, *refs):
    *sources, first, second, sems = refs
    copies = []
    for i, target in enumerate((first, second)):
        source, width = sources[i], target.shape[1]
        if source.shape[1] != width:
            source = source.at[:, pl.ds(pl.multiple_of(place_ref[0] * width, LANES), width)]
        copies.append(pltpu.make_async_copy(source, target, sems.at[i]))
        copies[i].start()
    for copy in copies:
        copy.wait()


def fetch_halves(place, arrays, width):
    depth = arrays[0].shape[0]
    return pl.pallas_call(
        halves_kernel,
        out_shape=[pltpu.VMEM((depth, width), bf16)] * 2,
        in_specs=[smem_spec()] + [pl.BlockSpec(memory_space=pl.ANY)] * 2,
        out_specs=[vmem_spec()] * 2,
        scratch_shapes=[pltpu.SemaphoreType.DMA((2,))],
        compiler_params=pltpu.CompilerParams(vmem_limit_bytes=HALVES_VMEM),
        cost_estimate=pl.CostEstimate(flops=0, bytes_accessed=8 * depth * width, transcendentals=0),
        name="near_output",
    )(place, *arrays)


def regroup(pieces, groups, size):
    assert groups == 2 and len(pieces) % 2 == 0
    rows = lax.broadcasted_iota(jnp.int32, pieces[0].shape, 0)
    low = rest(over(rows, size), 2) == 0
    total = pieces[0].shape[0]
    width = pieces[0].shape[1]
    firsts, seconds = [], []
    for h in range(0, len(pieces), 2):
        a, b = pieces[h], pieces[h + 1]
        firsts.append(jnp.where(low, a, pltpu.roll(b, size, 0)))
        seconds.append(jnp.where(low, pltpu.roll(a, total - size, 0), b))

    def stack(parts):
        parts = [part.reshape(total // (2 * size), 2 * size, width) for part in parts]
        return jnp.concatenate(parts, axis=1).reshape(total * len(parts), width)

    return [stack(firsts), stack(seconds)]


def query_kernel(reqs, drafts, heads, place_ref, *refs):
    *x_refs, gain_ref, up_ref, uk_ref, out_ref = refs
    owners = out_ref.shape[0]
    hd = heads * drafts
    x = jnp.concatenate([x_ref[...] for x_ref in x_refs], axis=0).astype(f32)
    scaled = x * lax.rsqrt(jnp.mean(x * x, axis=-1, keepdims=True) + rms_eps)
    normed = (scaled * gain_ref[...][None, :]).astype(bf16)
    full = mm(normed, up_ref[...]).astype(bf16)
    absorbed = [mm(full[:, h * QKD : h * QKD + NOPE], uk_ref[h * NOPE : (h + 1) * NOPE]) for h in range(heads)]
    rope = [full[:, h * QKD + NOPE : (h + 1) * QKD].astype(f32) for h in range(heads)]
    absorbed = regroup(absorbed, reqs, drafts)
    rope = regroup(rope, reqs, drafts)
    chunks = LATENT // LANES
    per = LANES // ROPE
    absorbed = [x.reshape(owners, hd, LATENT).astype(bf16) for x in absorbed]
    rope = [
        jnp.concatenate(rope[b * per : (b + 1) * per], axis=-1).reshape(owners, hd, LANES).astype(bf16)
        for b in range(reqs // per)
    ]
    for k in range(owners):
        distance = int(format(k, f"0{owners.bit_length() - 1}b")[::-1], 2)
        target = place_ref[2] ^ distance
        for q in range(reqs):
            for c in range(chunks):
                at = (q * chunks + c) * hd
                out_ref[target, at : at + hd, :] = absorbed[q][k, :, c * LANES : (c + 1) * LANES]
        for b in range(reqs // per):
            at = (reqs * chunks + b) * hd
            out_ref[target, at : at + hd, :] = rope[b][k]


def attend_kernel(reqs, drafts, heads, len_ref, count_ref, q_ref, frequency_ref, new_ref, cache_ref, out_ref):
    owners = q_ref.shape[0]
    hd = heads * drafts
    count = owners * hd
    chunks = LATENT // LANES
    per = LANES // ROPE
    slots = cache_ref.shape[2]
    scale = QKD ** (-0.5) * math.log2(math.e)
    rotated = []
    for b in range(reqs // per):
        at = (reqs * chunks + b) * hd
        x = q_ref[:, at : at + hd, :].astype(f32).reshape(count, LANES)
        half = ROPE // 2
        low = rest(lax.broadcasted_iota(jnp.int32, x.shape, 1), ROPE) < half
        other = jnp.where(low, pltpu.roll(x, LANES - half, 1), pltpu.roll(x, half, 1))
        lane = lax.broadcasted_iota(jnp.int32, (hd, LANES), 1)
        length = jnp.zeros_like(lane)
        for i in range(per):
            length = jnp.where(over(lane, ROPE) == i, len_ref[b * per + i], length)
        position = length + rest(lax.broadcasted_iota(jnp.int32, (hd, LANES), 0), drafts)
        angle = position.astype(f32) * frequency_ref[...]
        sine = jnp.sin(angle)
        sine = jnp.where(rest(lane, ROPE) < half, -sine, sine)
        x = x.reshape(owners, hd, LANES) * jnp.cos(angle) + other.reshape(owners, hd, LANES) * sine
        x = x.astype(bf16).reshape(count, LANES)
        rotated += [x[:, i * ROPE : (i + 1) * ROPE] for i in range(per)]
    draft = rest(lax.broadcasted_iota(jnp.int32, (count, 1), 0), drafts)
    new_at = lax.broadcasted_iota(jnp.int32, (count, new_ref.shape[0]), 1)
    slot = lax.broadcasted_iota(jnp.int32, (1, slots), 1)
    for q in range(reqs):
        absorbed = jnp.concatenate(
            [
                q_ref[:, (q * chunks + c) * hd : (q * chunks + c + 1) * hd, :].reshape(count, LANES)
                for c in range(chunks)
            ],
            axis=-1,
        )
        keys = cache_ref[q]
        rows = new_ref[...]
        score = mm(absorbed, keys[:LATENT]) + mm(rotated[q], keys[LATENT:])
        fresh = mm_nt(absorbed, rows[:, :LATENT]) + mm_nt(rotated[q], rows[:, LATENT:])
        score = jnp.where(slot < len_ref[q], score, -jnp.inf)
        seen = (new_at >= q * drafts) & (new_at - q * drafts <= draft)
        fresh = jnp.where(seen, fresh, -jnp.inf)
        peak = jnp.maximum(
            jnp.max(score, axis=1, keepdims=True), jnp.max(fresh, axis=1, keepdims=True)
        )
        score = jnp.exp2((score - peak) * scale)
        fresh = jnp.exp2((fresh - peak) * scale)
        total = jnp.sum(score, axis=1, keepdims=True) + jnp.sum(fresh, axis=1, keepdims=True)
        mix = mm_nt(score.astype(bf16), keys[:LATENT]) + mm(fresh.astype(bf16), rows[:, :LATENT])
        mix = jnp.where(draft < count_ref[q], mix * (1.0 / total), 0.0).astype(bf16)
        out_ref[:, q * hd : (q + 1) * hd, :] = mix.reshape(owners, hd, LATENT)


def value_kernel(drafts, heads, latent_ref, uv_ref, out_ref):
    owners = latent_ref.shape[0]
    hd = heads * drafts
    pair = 2 * drafts
    rows = owners * pair
    low = rest(over(lax.broadcasted_iota(jnp.int32, (rows, LATENT), 0), drafts), 2) == 0
    for h in range(0, heads, 2):
        a = latent_ref[:, h * drafts : h * drafts + pair, :].astype(f32).reshape(rows, LATENT)
        b = latent_ref[:, hd + h * drafts : hd + h * drafts + pair, :].astype(f32).reshape(rows, LATENT)
        first = jnp.where(low, a, pltpu.roll(b, drafts, 0)).astype(bf16)
        second = jnp.where(low, pltpu.roll(a, rows - drafts, 0), b).astype(bf16)
        out_ref[:, h * VDIM : (h + 1) * VDIM] = mm(first, uv_ref[h]).astype(bf16)
        out_ref[:, (h + 1) * VDIM : (h + 2) * VDIM] = mm(second, uv_ref[h + 1]).astype(bf16)


def output_kernel(place_ref, *refs):
    *value_refs, w_own_ref, w_other_ref, out_ref = refs
    replicas, rows, half = out_ref.shape
    own = jnp.concatenate([ref[...] for ref in value_refs[:replicas]], axis=0)
    other = jnp.concatenate([ref[...] for ref in value_refs[replicas:]], axis=0)
    tile = 256 if half % 256 == 0 else half
    for at in range(0, half, tile):
        part = mm(own, w_own_ref[:, at : at + tile]) + mm(other, w_other_ref[:, at : at + tile])
        part = part.astype(bf16)
        for k in range(replicas):
            out_ref[place_ref[1] ^ k, :, at : at + tile] = part[k * rows : (k + 1) * rows]


def sum_kernel(replicas, pairs, x_ref, out_ref):
    width = x_ref.shape[-1]
    for r in range(replicas):
        for c in range(2):
            total = None
            for p in range(pairs):
                part = x_ref[(r * pairs + p) * 2 + c].astype(f32)
                total = part if total is None else total + part
            at = (r * 2 + c) * width
            out_ref[:, at : at + width] = total.astype(bf16)


def step(x, axis, size, k):
    return lax.ppermute(x, axis, [(i, i ^ k) for i in range(size)])


def local_step(q_latent, q_gain, q_up, w_uk, w_uv, w_o, new_kv, latent_cache, cache_len, draft_count):
    rows_dev, _ = q_latent.shape
    owners = lax.axis_size("tensor")
    replicas = lax.axis_size("replica")
    heads = w_uk.shape[0]
    reqs = cache_len.shape[0]
    drafts = rows_dev // reqs
    hd = heads * drafts
    me = lax.axis_index("tensor")
    core = me % 2

    place = jnp.stack([core, lax.axis_index("replica"), me]).astype(jnp.int32)
    w_uk = w_uk.reshape(heads * NOPE, LATENT)
    near = fetch((q_up, w_uk, q_gain, q_latent), FETCH_VMEM)

    lane_pair = jnp.arange(LANES) % (ROPE // 2)
    frequency = (rope_base ** (-(lane_pair.astype(f32) * 2.0 / ROPE)))[None, :]

    first = step(q_latent, "tensor", owners, owners // 2)
    first, q_up, w_uk, gain, rows, frequency = lax.optimization_barrier((first, *near, frequency))
    rows = jnp.concatenate([rows, first], axis=0)
    bit = owners // 4
    while bit > 4:
        rows = jnp.concatenate([rows, step(rows, "tensor", owners, bit)], axis=0)
        bit //= 2
    parts = [rows]
    if bit == 4:
        parts = parts + [step(rows, "tensor", owners, k) for k in (4, 2, 6)]
        bit = 1
    while bit:
        parts = parts + [step(part, "tensor", owners, bit) for part in parts]
        bit //= 2

    chunks = LATENT // LANES
    packed = (reqs * chunks + reqs * ROPE // LANES) * hd
    params = pltpu.CompilerParams(vmem_limit_bytes=24 * 1024 * 1024)
    queries = pl.pallas_call(
        functools.partial(query_kernel, reqs, drafts, heads),
        out_shape=jax.ShapeDtypeStruct((owners, packed, LANES), bf16),
        in_specs=[smem_spec()] + [vmem_spec()] * (len(parts) + 3),
        out_specs=vmem_spec(),
        compiler_params=params,
        name="query",
    )(place, *parts, gain, q_up, w_uk)
    arrived = lax.all_to_all(queries, "tensor", split_axis=0, concat_axis=0, tiled=True)

    arrived, w_late = lax.optimization_barrier((arrived, w_o))

    half = w_o.shape[1] // 2
    aligned = half % LANES == 0
    w_own = w_o if aligned else lax.dynamic_slice_in_dim(w_o, core * half, half, axis=1)
    w_away = w_late if aligned else lax.dynamic_slice_in_dim(w_late, (1 - core) * half, half, axis=1)
    w_other = step(w_away, "tensor", owners, 1)

    latent = pl.pallas_call(
        functools.partial(attend_kernel, reqs, drafts, heads),
        out_shape=jax.ShapeDtypeStruct((owners, reqs * hd, LATENT), bf16),
        in_specs=[smem_spec()] * 2 + [vmem_spec()] * 4,
        out_specs=vmem_spec(),
        compiler_params=params,
        name="attend",
    )(cache_len, draft_count, arrived, frequency, new_kv, jnp.swapaxes(latent_cache, 1, 2))
    returned = lax.all_to_all(latent, "tensor", split_axis=0, concat_axis=0, tiled=True)
    returned, w_other = lax.optimization_barrier((returned, w_other))

    values = pl.pallas_call(
        functools.partial(value_kernel, drafts, heads),
        out_shape=jax.ShapeDtypeStruct((owners * rows_dev, heads * VDIM), bf16),
        in_specs=[vmem_spec()] * 2,
        out_specs=vmem_spec(),
        compiler_params=params,
        name="values",
    )(returned, w_uv)
    nearest = step(values, "replica", replicas, 1)
    own = [values, nearest] + [step(values, "replica", replicas, k) for k in range(2, replicas)]
    w_own, w_other = fetch_halves(place, (w_own, w_other), half)
    other = [step(piece, "tensor", owners, 1) for piece in own]

    product = pl.pallas_call(
        output_kernel,
        out_shape=jax.ShapeDtypeStruct((replicas, owners * rows_dev, half), bf16),
        in_specs=[smem_spec()] + [vmem_spec()] * (2 * replicas + 2),
        out_specs=vmem_spec(),
        compiler_params=params,
        name="output",
    )(place, *own, *other, w_own, w_other)
    product = product.reshape(replicas * owners, rows_dev, half)
    placed = lax.all_to_all(product, ("replica", "tensor"), split_axis=0, concat_axis=0, tiled=True)
    return pl.pallas_call(
        functools.partial(sum_kernel, replicas, owners // 2),
        out_shape=jax.ShapeDtypeStruct((rows_dev, replicas * 2 * half), bf16),
        in_specs=[vmem_spec()],
        out_specs=vmem_spec(),
        compiler_params=params,
        name="combine",
    )(placed)


def solution(mesh):
    rows = ("groups", "tensor", "replica")
    return jax.shard_map(
        local_step,
        mesh=mesh,
        in_specs=(
            P(rows, None),
            P(),
            P(None, "tensor"),
            P("tensor", None, None),
            P("tensor", None, None),
            P("tensor", "replica"),
            P(rows, None),
            P(rows, None, None),
            P(rows),
            P(rows),
        ),
        out_specs=P(rows, None),
        check_vma=False,
    )
```

```python
import functools
import math

import jax
import jax.numpy as jnp
from jax import lax
from jax.experimental import pallas as pl
from jax.experimental.pallas import tpu as pltpu
from jax.sharding import PartitionSpec as P


LATENT = 512
ROPE = 64
NOPE = 128
VDIM = 128
QKD = NOPE + ROPE
LANES = 128

FETCH_VMEM = 53_700_000
HALVES_VMEM = 51_000_000

rms_eps = 1e-06
rope_base = 50000.0

VMEM = pltpu.MemorySpace.VMEM
SMEM = pltpu.MemorySpace.SMEM
bf16 = jnp.bfloat16
f32 = jnp.float32


def vmem_spec():
    return pl.BlockSpec(memory_space=VMEM)


def smem_spec():
    return pl.BlockSpec(memory_space=SMEM)


def over(x, n):
    return x >> (n.bit_length() - 1) if n & (n - 1) == 0 else x // n


def rest(x, n):
    return x & (n - 1) if n & (n - 1) == 0 else x % n


def mm(a, b):
    return jnp.dot(a, b, preferred_element_type=f32)


def mm_nt(a, b):
    return lax.dot_general(a, b, (((1,), (1,)), ((), ())), preferred_element_type=f32)


def fetch_kernel(*refs):
    count = len(refs) // 2
    copies = [pltpu.make_async_copy(refs[i], refs[count + i], refs[-1].at[i]) for i in range(count)]
    for copy in copies:
        copy.start()
    for copy in copies:
        copy.wait()


def fetch(arrays, limit):
    return pl.pallas_call(
        fetch_kernel,
        out_shape=[pltpu.VMEM(x.shape, x.dtype) for x in arrays],
        in_specs=[pl.BlockSpec(memory_space=pl.ANY)] * len(arrays),
        out_specs=[vmem_spec()] * len(arrays),
        scratch_shapes=[pltpu.SemaphoreType.DMA((len(arrays),))],
        compiler_params=pltpu.CompilerParams(vmem_limit_bytes=limit),
        cost_estimate=pl.CostEstimate(
            flops=0, bytes_accessed=sum(4 * x.size for x in arrays), transcendentals=0
        ),
    )(*arrays)


def halves_kernel(place_ref, *refs):
    *sources, first, second, sems = refs
    copies = []
    for i, target in enumerate((first, second)):
        source, width = sources[i], target.shape[1]
        if source.shape[1] != width:
            source = source.at[:, pl.ds(pl.multiple_of(place_ref[0] * width, LANES), width)]
        copies.append(pltpu.make_async_copy(source, target, sems.at[i]))
        copies[i].start()
    for copy in copies:
        copy.wait()


def fetch_halves(place, arrays, width):
    depth = arrays[0].shape[0]
    return pl.pallas_call(
        halves_kernel,
        out_shape=[pltpu.VMEM((depth, width), bf16)] * 2,
        in_specs=[smem_spec()] + [pl.BlockSpec(memory_space=pl.ANY)] * 2,
        out_specs=[vmem_spec()] * 2,
        scratch_shapes=[pltpu.SemaphoreType.DMA((2,))],
        compiler_params=pltpu.CompilerParams(vmem_limit_bytes=HALVES_VMEM),
        cost_estimate=pl.CostEstimate(flops=0, bytes_accessed=8 * depth * width, transcendentals=0),
        name="near_output",
    )(place, *arrays)


def regroup(pieces, groups, size):
    assert groups == 2 and len(pieces) % 2 == 0
    rows = lax.broadcasted_iota(jnp.int32, pieces[0].shape, 0)
    low = rest(over(rows, size), 2) == 0
    total = pieces[0].shape[0]
    width = pieces[0].shape[1]
    firsts, seconds = [], []
    for h in range(0, len(pieces), 2):
        a, b = pieces[h], pieces[h + 1]
        firsts.append(jnp.where(low, a, pltpu.roll(b, size, 0)))
        seconds.append(jnp.where(low, pltpu.roll(a, total - size, 0), b))

    def stack(parts):
        parts = [part.reshape(total // (2 * size), 2 * size, width) for part in parts]
        return jnp.concatenate(parts, axis=1).reshape(total * len(parts), width)

    return [stack(firsts), stack(seconds)]


def query_kernel(reqs, drafts, heads, place_ref, *refs):
    *x_refs, gain_ref, up_ref, uk_ref, out_ref = refs
    owners = out_ref.shape[0]
    hd = heads * drafts
    x = jnp.concatenate([x_ref[...] for x_ref in x_refs], axis=0).astype(f32)
    scaled = x * lax.rsqrt(jnp.mean(x * x, axis=-1, keepdims=True) + rms_eps)
    normed = (scaled * gain_ref[...][None, :]).astype(bf16)
    full = mm(normed, up_ref[...]).astype(bf16)
    absorbed = [mm(full[:, h * QKD : h * QKD + NOPE], uk_ref[h * NOPE : (h + 1) * NOPE]) for h in range(heads)]
    rope = [full[:, h * QKD + NOPE : (h + 1) * QKD].astype(f32) for h in range(heads)]
    absorbed = regroup(absorbed, reqs, drafts)
    rope = regroup(rope, reqs, drafts)
    chunks = LATENT // LANES
    per = LANES // ROPE
    absorbed = [x.reshape(owners, hd, LATENT).astype(bf16) for x in absorbed]
    rope = [
        jnp.concatenate(rope[b * per : (b + 1) * per], axis=-1).reshape(owners, hd, LANES).astype(bf16)
        for b in range(reqs // per)
    ]
    for k in range(owners):
        distance = int(format(k, f"0{owners.bit_length() - 1}b")[::-1], 2)
        target = place_ref[2] ^ distance
        for q in range(reqs):
            for c in range(chunks):
                at = (q * chunks + c) * hd
                out_ref[target, at : at + hd, :] = absorbed[q][k, :, c * LANES : (c + 1) * LANES]
        for b in range(reqs // per):
            at = (reqs * chunks + b) * hd
            out_ref[target, at : at + hd, :] = rope[b][k]


def attend_kernel(reqs, drafts, heads, len_ref, count_ref, q_ref, frequency_ref, new_ref, cache_ref, out_ref):
    owners = q_ref.shape[0]
    hd = heads * drafts
    count = owners * hd
    chunks = LATENT // LANES
    per = LANES // ROPE
    slots = cache_ref.shape[2]
    scale = QKD ** (-0.5) * math.log2(math.e)
    rotated = []
    for b in range(reqs // per):
        at = (reqs * chunks + b) * hd
        x = q_ref[:, at : at + hd, :].astype(f32).reshape(count, LANES)
        half = ROPE // 2
        low = rest(lax.broadcasted_iota(jnp.int32, x.shape, 1), ROPE) < half
        other = jnp.where(low, pltpu.roll(x, LANES - half, 1), pltpu.roll(x, half, 1))
        lane = lax.broadcasted_iota(jnp.int32, (hd, LANES), 1)
        length = jnp.zeros_like(lane)
        for i in range(per):
            length = jnp.where(over(lane, ROPE) == i, len_ref[b * per + i], length)
        position = length + rest(lax.broadcasted_iota(jnp.int32, (hd, LANES), 0), drafts)
        angle = position.astype(f32) * frequency_ref[...]
        sine = jnp.sin(angle)
        sine = jnp.where(rest(lane, ROPE) < half, -sine, sine)
        x = x.reshape(owners, hd, LANES) * jnp.cos(angle) + other.reshape(owners, hd, LANES) * sine
        x = x.astype(bf16).reshape(count, LANES)
        rotated += [x[:, i * ROPE : (i + 1) * ROPE] for i in range(per)]
    draft = rest(lax.broadcasted_iota(jnp.int32, (count, 1), 0), drafts)
    new_at = lax.broadcasted_iota(jnp.int32, (count, new_ref.shape[0]), 1)
    slot = lax.broadcasted_iota(jnp.int32, (1, slots), 1)
    for q in range(reqs):
        absorbed = jnp.concatenate(
            [
                q_ref[:, (q * chunks + c) * hd : (q * chunks + c + 1) * hd, :].reshape(count, LANES)
                for c in range(chunks)
            ],
            axis=-1,
        )
        keys = cache_ref[q]
        rows = new_ref[...]
        score = mm(absorbed, keys[:LATENT]) + mm(rotated[q], keys[LATENT:])
        fresh = mm_nt(absorbed, rows[:, :LATENT]) + mm_nt(rotated[q], rows[:, LATENT:])
        score = jnp.where(slot < len_ref[q], score, -jnp.inf)
        seen = (new_at >= q * drafts) & (new_at - q * drafts <= draft)
        fresh = jnp.where(seen, fresh, -jnp.inf)
        peak = jnp.maximum(
            jnp.max(score, axis=1, keepdims=True), jnp.max(fresh, axis=1, keepdims=True)
        )
        score = jnp.exp2((score - peak) * scale)
        fresh = jnp.exp2((fresh - peak) * scale)
        total = jnp.sum(score, axis=1, keepdims=True) + jnp.sum(fresh, axis=1, keepdims=True)
        mix = mm_nt(score.astype(bf16), keys[:LATENT]) + mm(fresh.astype(bf16), rows[:, :LATENT])
        mix = jnp.where(draft < count_ref[q], mix * (1.0 / total), 0.0).astype(bf16)
        out_ref[:, q * hd : (q + 1) * hd, :] = mix.reshape(owners, hd, LATENT)


def value_kernel(drafts, heads, latent_ref, uv_ref, out_ref):
    owners = latent_ref.shape[0]
    hd = heads * drafts
    pair = 2 * drafts
    rows = owners * pair
    low = rest(over(lax.broadcasted_iota(jnp.int32, (rows, LATENT), 0), drafts), 2) == 0
    for h in range(0, heads, 2):
        a = latent_ref[:, h * drafts : h * drafts + pair, :].astype(f32).reshape(rows, LATENT)
        b = latent_ref[:, hd + h * drafts : hd + h * drafts + pair, :].astype(f32).reshape(rows, LATENT)
        first = jnp.where(low, a, pltpu.roll(b, drafts, 0)).astype(bf16)
        second = jnp.where(low, pltpu.roll(a, rows - drafts, 0), b).astype(bf16)
        out_ref[:, h * VDIM : (h + 1) * VDIM] = mm(first, uv_ref[h]).astype(bf16)
        out_ref[:, (h + 1) * VDIM : (h + 2) * VDIM] = mm(second, uv_ref[h + 1]).astype(bf16)


def output_kernel(done, place_ref, w_own_ref, w_other_ref, *refs):
    ready_refs, value_refs, out_ref = refs[:done], refs[done:-1], refs[-1]
    rows, half = out_ref.shape[1:]
    count = len(value_refs) // 2
    own = jnp.concatenate([ref[...] for ref in value_refs[:count]], axis=0)
    other = jnp.concatenate([ref[...] for ref in value_refs[count:]], axis=0)
    base = place_ref[1] if done else 0
    for k in range(done):
        out_ref[base ^ k] = ready_refs[k][0]
    tile = 256 if half % 256 == 0 else half
    for at in range(0, half, tile):
        part = mm(own, w_own_ref[:, at : at + tile]) + mm(other, w_other_ref[:, at : at + tile])
        part = part.astype(bf16)
        for k in range(count):
            out_ref[base ^ (done + k), :, at : at + tile] = part[k * rows : (k + 1) * rows]


def output_rows(ready, blocks, place, weights, own, other, params):
    operands = [place, *weights, *ready, *own, *other]
    shape = (blocks, own[0].shape[0], weights[0].shape[1])
    return pl.pallas_call(
        functools.partial(output_kernel, len(ready)),
        out_shape=jax.ShapeDtypeStruct(shape, bf16),
        in_specs=[smem_spec()] + [vmem_spec()] * (len(operands) - 1),
        out_specs=vmem_spec(),
        compiler_params=params,
        name="output",
    )(*operands)


def sum_kernel(replicas, pairs, x_ref, out_ref):
    width = x_ref.shape[-1]
    for r in range(replicas):
        for c in range(2):
            total = None
            for p in range(pairs):
                part = x_ref[(r * pairs + p) * 2 + c].astype(f32)
                total = part if total is None else total + part
            at = (r * 2 + c) * width
            out_ref[:, at : at + width] = total.astype(bf16)


def step(x, axis, size, k):
    return lax.ppermute(x, axis, [(i, i ^ k) for i in range(size)])


def local_step(q_latent, q_gain, q_up, w_uk, w_uv, w_o, new_kv, latent_cache, cache_len, draft_count):
    rows_dev, _ = q_latent.shape
    owners = lax.axis_size("tensor")
    replicas = lax.axis_size("replica")
    heads = w_uk.shape[0]
    reqs = cache_len.shape[0]
    drafts = rows_dev // reqs
    hd = heads * drafts
    me = lax.axis_index("tensor")
    core = me % 2

    place = jnp.stack([core, lax.axis_index("replica"), me]).astype(jnp.int32)
    w_uk = w_uk.reshape(heads * NOPE, LATENT)
    near = fetch((q_up, w_uk, q_gain, q_latent), FETCH_VMEM)

    lane_pair = jnp.arange(LANES) % (ROPE // 2)
    frequency = (rope_base ** (-(lane_pair.astype(f32) * 2.0 / ROPE)))[None, :]

    first = step(q_latent, "tensor", owners, owners // 2)
    first, q_up, w_uk, gain, rows, frequency = lax.optimization_barrier((first, *near, frequency))
    rows = jnp.concatenate([rows, first], axis=0)
    bit = owners // 4
    while bit > 4:
        rows = jnp.concatenate([rows, step(rows, "tensor", owners, bit)], axis=0)
        bit //= 2
    parts = [rows]
    if bit == 4:
        parts = parts + [step(rows, "tensor", owners, k) for k in (4, 2, 6)]
        bit = 1
    while bit:
        parts = parts + [step(part, "tensor", owners, bit) for part in parts]
        bit //= 2

    chunks = LATENT // LANES
    packed = (reqs * chunks + reqs * ROPE // LANES) * hd
    params = pltpu.CompilerParams(vmem_limit_bytes=24 * 1024 * 1024)
    queries = pl.pallas_call(
        functools.partial(query_kernel, reqs, drafts, heads),
        out_shape=jax.ShapeDtypeStruct((owners, packed, LANES), bf16),
        in_specs=[smem_spec()] + [vmem_spec()] * (len(parts) + 3),
        out_specs=vmem_spec(),
        compiler_params=params,
        name="query",
    )(place, *parts, gain, q_up, w_uk)
    arrived = lax.all_to_all(queries, "tensor", split_axis=0, concat_axis=0, tiled=True)

    arrived, w_late = lax.optimization_barrier((arrived, w_o))

    half = w_o.shape[1] // 2
    aligned = half % LANES == 0
    w_own = w_o if aligned else lax.dynamic_slice_in_dim(w_o, core * half, half, axis=1)
    w_away = w_late if aligned else lax.dynamic_slice_in_dim(w_late, (1 - core) * half, half, axis=1)
    w_other = step(w_away, "tensor", owners, 1)

    latent = pl.pallas_call(
        functools.partial(attend_kernel, reqs, drafts, heads),
        out_shape=jax.ShapeDtypeStruct((owners, reqs * hd, LATENT), bf16),
        in_specs=[smem_spec()] * 2 + [vmem_spec()] * 4,
        out_specs=vmem_spec(),
        compiler_params=params,
        name="attend",
    )(cache_len, draft_count, arrived, frequency, new_kv, jnp.swapaxes(latent_cache, 1, 2))
    returned = lax.all_to_all(latent, "tensor", split_axis=0, concat_axis=0, tiled=True)
    returned, w_other = lax.optimization_barrier((returned, w_other))

    values = pl.pallas_call(
        functools.partial(value_kernel, drafts, heads),
        out_shape=jax.ShapeDtypeStruct((owners * rows_dev, heads * VDIM), bf16),
        in_specs=[vmem_spec()] * 2,
        out_specs=vmem_spec(),
        compiler_params=params,
        name="values",
    )(returned, w_uv)
    nearest = step(values, "replica", replicas, 1)
    own = [values, nearest] + [step(values, "replica", replicas, k) for k in range(2, replicas)]
    w_own, w_other = fetch_halves(place, (w_own, w_other), half)
    other = [step(piece, "tensor", owners, 1) for piece in own]

    weights = (w_own, w_other)
    product = output_rows((), 1, place, weights, own[:1], other[:1], params)
    if replicas > 1:
        product = output_rows((product,), replicas, place, weights, own[1:], other[1:], params)
    product = product.reshape(replicas * owners, rows_dev, half)
    placed = lax.all_to_all(product, ("replica", "tensor"), split_axis=0, concat_axis=0, tiled=True)
    return pl.pallas_call(
        functools.partial(sum_kernel, replicas, owners // 2),
        out_shape=jax.ShapeDtypeStruct((rows_dev, replicas * 2 * half), bf16),
        in_specs=[vmem_spec()],
        out_specs=vmem_spec(),
        compiler_params=params,
        name="combine",
    )(placed)


def solution(mesh):
    rows = ("groups", "tensor", "replica")
    return jax.shard_map(
        local_step,
        mesh=mesh,
        in_specs=(
            P(rows, None),
            P(),
            P(None, "tensor"),
            P("tensor", None, None),
            P("tensor", None, None),
            P("tensor", "replica"),
            P(rows, None),
            P(rows, None, None),
            P(rows),
            P(rows),
        ),
        out_specs=P(rows, None),
        check_vma=False,
    )
```

```python
import functools
import math

import jax
import jax.numpy as jnp
from jax import lax
from jax.experimental import pallas as pl
from jax.experimental.pallas import tpu as pltpu
from jax.sharding import PartitionSpec as P


LATENT = 512
ROPE = 64
NOPE = 128
VDIM = 128
QKD = NOPE + ROPE
LANES = 128

FETCH_VMEM = 53_700_000
HALVES_VMEM = 51_000_000

rms_eps = 1e-06
rope_base = 50000.0

VMEM = pltpu.MemorySpace.VMEM
SMEM = pltpu.MemorySpace.SMEM
bf16 = jnp.bfloat16
f32 = jnp.float32


def vmem_spec():
    return pl.BlockSpec(memory_space=VMEM)


def smem_spec():
    return pl.BlockSpec(memory_space=SMEM)


def over(x, n):
    return x >> (n.bit_length() - 1) if n & (n - 1) == 0 else x // n


def rest(x, n):
    return x & (n - 1) if n & (n - 1) == 0 else x % n


def mm(a, b):
    return jnp.dot(a, b, preferred_element_type=f32)


def mm_nt(a, b):
    return lax.dot_general(a, b, (((1,), (1,)), ((), ())), preferred_element_type=f32)


def fetch_kernel(*refs):
    count = len(refs) // 2
    copies = [pltpu.make_async_copy(refs[i], refs[count + i], refs[-1].at[i]) for i in range(count)]
    for copy in copies:
        copy.start()
    for copy in copies:
        copy.wait()


def fetch(arrays, limit):
    return pl.pallas_call(
        fetch_kernel,
        out_shape=[pltpu.VMEM(x.shape, x.dtype) for x in arrays],
        in_specs=[pl.BlockSpec(memory_space=pl.ANY)] * len(arrays),
        out_specs=[vmem_spec()] * len(arrays),
        scratch_shapes=[pltpu.SemaphoreType.DMA((len(arrays),))],
        compiler_params=pltpu.CompilerParams(vmem_limit_bytes=limit),
        cost_estimate=pl.CostEstimate(
            flops=0, bytes_accessed=sum(4 * x.size for x in arrays), transcendentals=0
        ),
    )(*arrays)


def halves_kernel(place_ref, *refs):
    *sources, first, second, sems = refs
    copies = []
    for i, target in enumerate((first, second)):
        source, width = sources[i], target.shape[1]
        if source.shape[1] != width:
            source = source.at[:, pl.ds(pl.multiple_of(place_ref[0] * width, LANES), width)]
        copies.append(pltpu.make_async_copy(source, target, sems.at[i]))
        copies[i].start()
    for copy in copies:
        copy.wait()


def fetch_halves(place, arrays, width):
    depth = arrays[0].shape[0]
    return pl.pallas_call(
        halves_kernel,
        out_shape=[pltpu.VMEM((depth, width), bf16)] * 2,
        in_specs=[smem_spec()] + [pl.BlockSpec(memory_space=pl.ANY)] * 2,
        out_specs=[vmem_spec()] * 2,
        scratch_shapes=[pltpu.SemaphoreType.DMA((2,))],
        compiler_params=pltpu.CompilerParams(vmem_limit_bytes=HALVES_VMEM),
        cost_estimate=pl.CostEstimate(flops=0, bytes_accessed=8 * depth * width, transcendentals=0),
        name="near_output",
    )(place, *arrays)


def regroup(pieces, groups, size):
    assert groups == 2 and len(pieces) % 2 == 0
    rows = lax.broadcasted_iota(jnp.int32, pieces[0].shape, 0)
    low = rest(over(rows, size), 2) == 0
    total = pieces[0].shape[0]
    width = pieces[0].shape[1]
    firsts, seconds = [], []
    for h in range(0, len(pieces), 2):
        a, b = pieces[h], pieces[h + 1]
        firsts.append(jnp.where(low, a, pltpu.roll(b, size, 0)))
        seconds.append(jnp.where(low, pltpu.roll(a, total - size, 0), b))

    def stack(parts):
        parts = [part.reshape(total // (2 * size), 2 * size, width) for part in parts]
        return jnp.concatenate(parts, axis=1).reshape(total * len(parts), width)

    return [stack(firsts), stack(seconds)]


def query_kernel(reqs, drafts, heads, place_ref, *refs):
    *x_refs, gain_ref, up_ref, uk_ref, out_ref = refs
    owners = out_ref.shape[0]
    hd = heads * drafts
    x = jnp.concatenate([x_ref[...] for x_ref in x_refs], axis=0).astype(f32)
    scaled = x * lax.rsqrt(jnp.mean(x * x, axis=-1, keepdims=True) + rms_eps)
    normed = (scaled * gain_ref[...][None, :]).astype(bf16)
    full = mm(normed, up_ref[...]).astype(bf16)
    absorbed = [mm(full[:, h * QKD : h * QKD + NOPE], uk_ref[h * NOPE : (h + 1) * NOPE]) for h in range(heads)]
    rope = [full[:, h * QKD + NOPE : (h + 1) * QKD].astype(f32) for h in range(heads)]
    absorbed = regroup(absorbed, reqs, drafts)
    rope = regroup(rope, reqs, drafts)
    chunks = LATENT // LANES
    per = LANES // ROPE
    absorbed = [x.reshape(owners, hd, LATENT).astype(bf16) for x in absorbed]
    rope = [
        jnp.concatenate(rope[b * per : (b + 1) * per], axis=-1).reshape(owners, hd, LANES).astype(bf16)
        for b in range(reqs // per)
    ]
    for k in range(owners):
        distance = int(format(k, f"0{owners.bit_length() - 1}b")[::-1], 2)
        target = place_ref[2] ^ distance
        for q in range(reqs):
            for c in range(chunks):
                at = (q * chunks + c) * hd
                out_ref[target, at : at + hd, :] = absorbed[q][k, :, c * LANES : (c + 1) * LANES]
        for b in range(reqs // per):
            at = (reqs * chunks + b) * hd
            out_ref[target, at : at + hd, :] = rope[b][k]


def attend_kernel(reqs, drafts, heads, len_ref, count_ref, q_ref, frequency_ref, new_ref, cache_ref, out_ref):
    owners = q_ref.shape[0]
    hd = heads * drafts
    count = owners * hd
    chunks = LATENT // LANES
    per = LANES // ROPE
    slots = cache_ref.shape[2]
    scale = QKD ** (-0.5) * math.log2(math.e)
    rotated = []
    for b in range(reqs // per):
        at = (reqs * chunks + b) * hd
        x = q_ref[:, at : at + hd, :].astype(f32).reshape(count, LANES)
        half = ROPE // 2
        low = rest(lax.broadcasted_iota(jnp.int32, x.shape, 1), ROPE) < half
        other = jnp.where(low, pltpu.roll(x, LANES - half, 1), pltpu.roll(x, half, 1))
        lane = lax.broadcasted_iota(jnp.int32, (hd, LANES), 1)
        length = jnp.zeros_like(lane)
        for i in range(per):
            length = jnp.where(over(lane, ROPE) == i, len_ref[b * per + i], length)
        position = length + rest(lax.broadcasted_iota(jnp.int32, (hd, LANES), 0), drafts)
        angle = position.astype(f32) * frequency_ref[...]
        sine = jnp.sin(angle)
        sine = jnp.where(rest(lane, ROPE) < half, -sine, sine)
        x = x.reshape(owners, hd, LANES) * jnp.cos(angle) + other.reshape(owners, hd, LANES) * sine
        x = x.astype(bf16).reshape(count, LANES)
        rotated += [x[:, i * ROPE : (i + 1) * ROPE] for i in range(per)]
    draft = rest(lax.broadcasted_iota(jnp.int32, (count, 1), 0), drafts)
    new_at = lax.broadcasted_iota(jnp.int32, (count, new_ref.shape[0]), 1)
    slot = lax.broadcasted_iota(jnp.int32, (1, slots), 1)
    for q in range(reqs):
        absorbed = jnp.concatenate(
            [
                q_ref[:, (q * chunks + c) * hd : (q * chunks + c + 1) * hd, :].reshape(count, LANES)
                for c in range(chunks)
            ],
            axis=-1,
        )
        keys = cache_ref[q]
        rows = new_ref[...]
        score = mm(absorbed, keys[:LATENT]) + mm(rotated[q], keys[LATENT:])
        fresh = mm_nt(absorbed, rows[:, :LATENT]) + mm_nt(rotated[q], rows[:, LATENT:])
        score = jnp.where(slot < len_ref[q], score, -jnp.inf)
        seen = (new_at >= q * drafts) & (new_at - q * drafts <= draft)
        fresh = jnp.where(seen, fresh, -jnp.inf)
        peak = jnp.maximum(
            jnp.max(score, axis=1, keepdims=True), jnp.max(fresh, axis=1, keepdims=True)
        )
        score = jnp.exp2((score - peak) * scale)
        fresh = jnp.exp2((fresh - peak) * scale)
        total = jnp.sum(score, axis=1, keepdims=True) + jnp.sum(fresh, axis=1, keepdims=True)
        mix = mm_nt(score.astype(bf16), keys[:LATENT]) + mm(fresh.astype(bf16), rows[:, :LATENT])
        mix = jnp.where(draft < count_ref[q], mix * (1.0 / total), 0.0).astype(bf16)
        out_ref[:, q * hd : (q + 1) * hd, :] = mix.reshape(owners, hd, LATENT)


def value_kernel(drafts, heads, latent_ref, uv_ref, out_ref):
    owners = latent_ref.shape[0]
    hd = heads * drafts
    pair = 2 * drafts
    rows = owners * pair
    low = rest(over(lax.broadcasted_iota(jnp.int32, (rows, LATENT), 0), drafts), 2) == 0
    for h in range(0, heads, 2):
        a = latent_ref[:, h * drafts : h * drafts + pair, :].astype(f32).reshape(rows, LATENT)
        b = latent_ref[:, hd + h * drafts : hd + h * drafts + pair, :].astype(f32).reshape(rows, LATENT)
        first = jnp.where(low, a, pltpu.roll(b, drafts, 0)).astype(bf16)
        second = jnp.where(low, pltpu.roll(a, rows - drafts, 0), b).astype(bf16)
        out_ref[:, h * VDIM : (h + 1) * VDIM] = mm(first, uv_ref[h]).astype(bf16)
        out_ref[:, (h + 1) * VDIM : (h + 2) * VDIM] = mm(second, uv_ref[h + 1]).astype(bf16)


def tile_of(width):
    return 256 if width % 256 == 0 else width


def half_product_kernel(count, *refs):
    w_ref, *value_refs, out_ref = refs
    rows = jnp.concatenate([ref[...] for ref in value_refs[:count]], axis=0)
    tile = tile_of(w_ref.shape[1])
    for at in range(0, w_ref.shape[1], tile):
        out_ref[:, at : at + tile] = mm(rows, w_ref[:, at : at + tile])


def half_product(weights, pieces, params):
    return pl.pallas_call(
        functools.partial(half_product_kernel, len(pieces)),
        out_shape=jax.ShapeDtypeStruct((len(pieces) * pieces[0].shape[0], weights.shape[1]), f32),
        in_specs=[vmem_spec()] * (1 + len(pieces)),
        out_specs=vmem_spec(),
        compiler_params=params,
        name="half_product",
    )(weights, *pieces)


def output_kernel(done, place_ref, w_ref, partial_ref, *refs):
    ready_refs, value_refs, out_ref = refs[:done], refs[done:-1], refs[-1]
    rows, half = out_ref.shape[1:]
    other = jnp.concatenate([ref[...] for ref in value_refs], axis=0)
    base = place_ref[1] if done else 0
    for k in range(done):
        out_ref[base ^ k] = ready_refs[k][0]
    tile = tile_of(half)
    for at in range(0, half, tile):
        part = partial_ref[:, at : at + tile] + mm(other, w_ref[:, at : at + tile])
        part = part.astype(bf16)
        for k in range(len(value_refs)):
            out_ref[base ^ (done + k), :, at : at + tile] = part[k * rows : (k + 1) * rows]


def output_rows(ready, blocks, place, weights, partial, other, params):
    operands = [place, weights, partial, *ready, *other]
    shape = (blocks, other[0].shape[0], weights.shape[1])
    return pl.pallas_call(
        functools.partial(output_kernel, len(ready)),
        out_shape=jax.ShapeDtypeStruct(shape, bf16),
        in_specs=[smem_spec()] + [vmem_spec()] * (len(operands) - 1),
        out_specs=vmem_spec(),
        compiler_params=params,
        name="output",
    )(*operands)


def sum_kernel(replicas, pairs, x_ref, out_ref):
    width = x_ref.shape[-1]
    for r in range(replicas):
        for c in range(2):
            total = None
            for p in range(pairs):
                part = x_ref[(r * pairs + p) * 2 + c].astype(f32)
                total = part if total is None else total + part
            at = (r * 2 + c) * width
            out_ref[:, at : at + width] = total.astype(bf16)


def step(x, axis, size, k):
    return lax.ppermute(x, axis, [(i, i ^ k) for i in range(size)])


def local_step(q_latent, q_gain, q_up, w_uk, w_uv, w_o, new_kv, latent_cache, cache_len, draft_count):
    rows_dev, _ = q_latent.shape
    owners = lax.axis_size("tensor")
    replicas = lax.axis_size("replica")
    heads = w_uk.shape[0]
    reqs = cache_len.shape[0]
    drafts = rows_dev // reqs
    hd = heads * drafts
    me = lax.axis_index("tensor")
    core = me % 2

    place = jnp.stack([core, lax.axis_index("replica"), me]).astype(jnp.int32)
    w_uk = w_uk.reshape(heads * NOPE, LATENT)
    near = fetch((q_up, w_uk, q_gain, q_latent), FETCH_VMEM)

    lane_pair = jnp.arange(LANES) % (ROPE // 2)
    frequency = (rope_base ** (-(lane_pair.astype(f32) * 2.0 / ROPE)))[None, :]

    first = step(q_latent, "tensor", owners, owners // 2)
    first, q_up, w_uk, gain, rows, frequency = lax.optimization_barrier((first, *near, frequency))
    rows = jnp.concatenate([rows, first], axis=0)
    bit = owners // 4
    while bit > 4:
        rows = jnp.concatenate([rows, step(rows, "tensor", owners, bit)], axis=0)
        bit //= 2
    parts = [rows]
    if bit == 4:
        parts = parts + [step(rows, "tensor", owners, k) for k in (4, 2, 6)]
        bit = 1
    while bit:
        parts = parts + [step(part, "tensor", owners, bit) for part in parts]
        bit //= 2

    chunks = LATENT // LANES
    packed = (reqs * chunks + reqs * ROPE // LANES) * hd
    params = pltpu.CompilerParams(vmem_limit_bytes=24 * 1024 * 1024)
    queries = pl.pallas_call(
        functools.partial(query_kernel, reqs, drafts, heads),
        out_shape=jax.ShapeDtypeStruct((owners, packed, LANES), bf16),
        in_specs=[smem_spec()] + [vmem_spec()] * (len(parts) + 3),
        out_specs=vmem_spec(),
        compiler_params=params,
        name="query",
    )(place, *parts, gain, q_up, w_uk)
    arrived = lax.all_to_all(queries, "tensor", split_axis=0, concat_axis=0, tiled=True)

    arrived, w_late = lax.optimization_barrier((arrived, w_o))

    half = w_o.shape[1] // 2
    aligned = half % LANES == 0
    w_own = w_o if aligned else lax.dynamic_slice_in_dim(w_o, core * half, half, axis=1)
    w_away = w_late if aligned else lax.dynamic_slice_in_dim(w_late, (1 - core) * half, half, axis=1)
    w_other = step(w_away, "tensor", owners, 1)

    latent = pl.pallas_call(
        functools.partial(attend_kernel, reqs, drafts, heads),
        out_shape=jax.ShapeDtypeStruct((owners, reqs * hd, LATENT), bf16),
        in_specs=[smem_spec()] * 2 + [vmem_spec()] * 4,
        out_specs=vmem_spec(),
        compiler_params=params,
        name="attend",
    )(cache_len, draft_count, arrived, frequency, new_kv, jnp.swapaxes(latent_cache, 1, 2))
    returned = lax.all_to_all(latent, "tensor", split_axis=0, concat_axis=0, tiled=True)
    returned, w_other = lax.optimization_barrier((returned, w_other))

    values = pl.pallas_call(
        functools.partial(value_kernel, drafts, heads),
        out_shape=jax.ShapeDtypeStruct((owners * rows_dev, heads * VDIM), bf16),
        in_specs=[vmem_spec()] * 2,
        out_specs=vmem_spec(),
        compiler_params=params,
        name="values",
    )(returned, w_uv)
    nearest = step(values, "replica", replicas, 1)
    own = [values, nearest] + [step(values, "replica", replicas, k) for k in range(2, replicas)]
    w_own, w_other = fetch_halves(place, (w_own, w_other), half)
    other = [step(own[0], "tensor", owners, 1)]
    product = half_product(w_own, own[:1], params)
    product = output_rows((), 1, place, w_other, product, other, params)
    if replicas > 1:
        other = [step(own[1], "tensor", owners, 1)]
        other = other + [step(piece, "tensor", owners, 1) for piece in own[2:]]
        partial = half_product(w_own, own[1:], params)
        product = output_rows((product,), replicas, place, w_other, partial, other, params)
    product = product.reshape(replicas * owners, rows_dev, half)
    placed = lax.all_to_all(product, ("replica", "tensor"), split_axis=0, concat_axis=0, tiled=True)
    return pl.pallas_call(
        functools.partial(sum_kernel, replicas, owners // 2),
        out_shape=jax.ShapeDtypeStruct((rows_dev, replicas * 2 * half), bf16),
        in_specs=[vmem_spec()],
        out_specs=vmem_spec(),
        compiler_params=params,
        name="combine",
    )(placed)


def solution(mesh):
    rows = ("groups", "tensor", "replica")
    return jax.shard_map(
        local_step,
        mesh=mesh,
        in_specs=(
            P(rows, None),
            P(),
            P(None, "tensor"),
            P("tensor", None, None),
            P("tensor", None, None),
            P("tensor", "replica"),
            P(rows, None),
            P(rows, None, None),
            P(rows),
            P(rows),
        ),
        out_specs=P(rows, None),
        check_vma=False,
    )
```

```python
import functools
import math

import jax
import jax.numpy as jnp
from jax import lax
from jax.experimental import pallas as pl
from jax.experimental.pallas import tpu as pltpu
from jax.sharding import PartitionSpec as P


LATENT = 512
ROPE = 64
NOPE = 128
VDIM = 128
QKD = NOPE + ROPE
LANES = 128

FETCH_VMEM = 53_700_000
HALVES_VMEM = 51_000_000

rms_eps = 1e-06
rope_base = 50000.0

VMEM = pltpu.MemorySpace.VMEM
SMEM = pltpu.MemorySpace.SMEM
bf16 = jnp.bfloat16
f32 = jnp.float32


def vmem_spec():
    return pl.BlockSpec(memory_space=VMEM)


def smem_spec():
    return pl.BlockSpec(memory_space=SMEM)


def over(x, n):
    return x >> (n.bit_length() - 1) if n & (n - 1) == 0 else x // n


def rest(x, n):
    return x & (n - 1) if n & (n - 1) == 0 else x % n


def mm(a, b):
    return jnp.dot(a, b, preferred_element_type=f32)


def mm_nt(a, b):
    return lax.dot_general(a, b, (((1,), (1,)), ((), ())), preferred_element_type=f32)


def fetch_kernel(*refs):
    count = len(refs) // 2
    copies = [pltpu.make_async_copy(refs[i], refs[count + i], refs[-1].at[i]) for i in range(count)]
    for copy in copies:
        copy.start()
    for copy in copies:
        copy.wait()


def fetch(arrays, limit):
    return pl.pallas_call(
        fetch_kernel,
        out_shape=[pltpu.VMEM(x.shape, x.dtype) for x in arrays],
        in_specs=[pl.BlockSpec(memory_space=pl.ANY)] * len(arrays),
        out_specs=[vmem_spec()] * len(arrays),
        scratch_shapes=[pltpu.SemaphoreType.DMA((len(arrays),))],
        compiler_params=pltpu.CompilerParams(vmem_limit_bytes=limit),
        cost_estimate=pl.CostEstimate(
            flops=0, bytes_accessed=sum(4 * x.size for x in arrays), transcendentals=0
        ),
    )(*arrays)


def halves_kernel(place_ref, *refs):
    *sources, first, second, sems = refs
    copies = []
    for i, target in enumerate((first, second)):
        source, width = sources[i], target.shape[1]
        if source.shape[1] != width:
            source = source.at[:, pl.ds(pl.multiple_of(place_ref[0] * width, LANES), width)]
        copies.append(pltpu.make_async_copy(source, target, sems.at[i]))
        copies[i].start()
    for copy in copies:
        copy.wait()


def fetch_halves(place, arrays, width):
    depth = arrays[0].shape[0]
    return pl.pallas_call(
        halves_kernel,
        out_shape=[pltpu.VMEM((depth, width), bf16)] * 2,
        in_specs=[smem_spec()] + [pl.BlockSpec(memory_space=pl.ANY)] * 2,
        out_specs=[vmem_spec()] * 2,
        scratch_shapes=[pltpu.SemaphoreType.DMA((2,))],
        compiler_params=pltpu.CompilerParams(vmem_limit_bytes=HALVES_VMEM),
        cost_estimate=pl.CostEstimate(flops=0, bytes_accessed=8 * depth * width, transcendentals=0),
        name="near_output",
    )(place, *arrays)


def regroup(pieces, groups, size):
    assert groups == 2 and len(pieces) % 2 == 0
    rows = lax.broadcasted_iota(jnp.int32, pieces[0].shape, 0)
    low = rest(over(rows, size), 2) == 0
    total = pieces[0].shape[0]
    width = pieces[0].shape[1]
    firsts, seconds = [], []
    for h in range(0, len(pieces), 2):
        a, b = pieces[h], pieces[h + 1]
        firsts.append(jnp.where(low, a, pltpu.roll(b, size, 0)))
        seconds.append(jnp.where(low, pltpu.roll(a, total - size, 0), b))

    def stack(parts):
        parts = [part.reshape(total // (2 * size), 2 * size, width) for part in parts]
        return jnp.concatenate(parts, axis=1).reshape(total * len(parts), width)

    return [stack(firsts), stack(seconds)]


def query_kernel(reqs, drafts, heads, place_ref, *refs):
    *x_refs, gain_ref, up_ref, uk_ref, out_ref = refs
    owners = out_ref.shape[0]
    hd = heads * drafts
    x = jnp.concatenate([x_ref[...] for x_ref in x_refs], axis=0).astype(f32)
    scaled = x * lax.rsqrt(jnp.mean(x * x, axis=-1, keepdims=True) + rms_eps)
    normed = (scaled * gain_ref[...][None, :]).astype(bf16)
    full = mm(normed, up_ref[...]).astype(bf16)
    absorbed = [mm(full[:, h * QKD : h * QKD + NOPE], uk_ref[h * NOPE : (h + 1) * NOPE]) for h in range(heads)]
    rope = [full[:, h * QKD + NOPE : (h + 1) * QKD].astype(f32) for h in range(heads)]
    absorbed = regroup(absorbed, reqs, drafts)
    rope = regroup(rope, reqs, drafts)
    chunks = LATENT // LANES
    per = LANES // ROPE
    absorbed = [x.reshape(owners, hd, LATENT).astype(bf16) for x in absorbed]
    rope = [
        jnp.concatenate(rope[b * per : (b + 1) * per], axis=-1).reshape(owners, hd, LANES).astype(bf16)
        for b in range(reqs // per)
    ]
    for k in range(owners):
        distance = int(format(k, f"0{owners.bit_length() - 1}b")[::-1], 2)
        target = place_ref[2] ^ distance
        for q in range(reqs):
            for c in range(chunks):
                at = (q * chunks + c) * hd
                out_ref[target, at : at + hd, :] = absorbed[q][k, :, c * LANES : (c + 1) * LANES]
        for b in range(reqs // per):
            at = (reqs * chunks + b) * hd
            out_ref[target, at : at + hd, :] = rope[b][k]


def attend_kernel(reqs, drafts, heads, len_ref, count_ref, q_ref, frequency_ref, new_ref, cache_ref, out_ref):
    owners = q_ref.shape[0]
    hd = heads * drafts
    count = owners * hd
    chunks = LATENT // LANES
    per = LANES // ROPE
    slots = cache_ref.shape[2]
    scale = QKD ** (-0.5) * math.log2(math.e)
    rotated = []
    for b in range(reqs // per):
        at = (reqs * chunks + b) * hd
        x = q_ref[:, at : at + hd, :].astype(f32).reshape(count, LANES)
        half = ROPE // 2
        low = rest(lax.broadcasted_iota(jnp.int32, x.shape, 1), ROPE) < half
        other = jnp.where(low, pltpu.roll(x, LANES - half, 1), pltpu.roll(x, half, 1))
        lane = lax.broadcasted_iota(jnp.int32, (hd, LANES), 1)
        length = jnp.zeros_like(lane)
        for i in range(per):
            length = jnp.where(over(lane, ROPE) == i, len_ref[b * per + i], length)
        position = length + rest(lax.broadcasted_iota(jnp.int32, (hd, LANES), 0), drafts)
        angle = position.astype(f32) * frequency_ref[...]
        sine = jnp.sin(angle)
        sine = jnp.where(rest(lane, ROPE) < half, -sine, sine)
        x = x.reshape(owners, hd, LANES) * jnp.cos(angle) + other.reshape(owners, hd, LANES) * sine
        x = x.astype(bf16).reshape(count, LANES)
        rotated += [x[:, i * ROPE : (i + 1) * ROPE] for i in range(per)]
    draft = rest(lax.broadcasted_iota(jnp.int32, (count, 1), 0), drafts)
    new_at = lax.broadcasted_iota(jnp.int32, (count, new_ref.shape[0]), 1)
    slot = lax.broadcasted_iota(jnp.int32, (1, slots), 1)
    for q in range(reqs):
        absorbed = jnp.concatenate(
            [
                q_ref[:, (q * chunks + c) * hd : (q * chunks + c + 1) * hd, :].reshape(count, LANES)
                for c in range(chunks)
            ],
            axis=-1,
        )
        keys = cache_ref[q]
        rows = new_ref[...]
        score = mm(absorbed, keys[:LATENT]) + mm(rotated[q], keys[LATENT:])
        fresh = mm_nt(absorbed, rows[:, :LATENT]) + mm_nt(rotated[q], rows[:, LATENT:])
        score = jnp.where(slot < len_ref[q], score, -jnp.inf)
        seen = (new_at >= q * drafts) & (new_at - q * drafts <= draft)
        fresh = jnp.where(seen, fresh, -jnp.inf)
        peak = jnp.maximum(
            jnp.max(score, axis=1, keepdims=True), jnp.max(fresh, axis=1, keepdims=True)
        )
        score = jnp.exp2((score - peak) * scale)
        fresh = jnp.exp2((fresh - peak) * scale)
        total = jnp.sum(score, axis=1, keepdims=True) + jnp.sum(fresh, axis=1, keepdims=True)
        mix = mm_nt(score.astype(bf16), keys[:LATENT]) + mm(fresh.astype(bf16), rows[:, :LATENT])
        mix = jnp.where(draft < count_ref[q], mix * (1.0 / total), 0.0).astype(bf16)
        out_ref[:, q * hd : (q + 1) * hd, :] = mix.reshape(owners, hd, LATENT)


def value_kernel(drafts, heads, latent_ref, uv_ref, out_ref):
    owners = latent_ref.shape[0]
    hd = heads * drafts
    pair = 2 * drafts
    rows = owners * pair
    low = rest(over(lax.broadcasted_iota(jnp.int32, (rows, LATENT), 0), drafts), 2) == 0
    for h in range(0, heads, 2):
        a = latent_ref[:, h * drafts : h * drafts + pair, :].astype(f32).reshape(rows, LATENT)
        b = latent_ref[:, hd + h * drafts : hd + h * drafts + pair, :].astype(f32).reshape(rows, LATENT)
        first = jnp.where(low, a, pltpu.roll(b, drafts, 0)).astype(bf16)
        second = jnp.where(low, pltpu.roll(a, rows - drafts, 0), b).astype(bf16)
        out_ref[:, h * VDIM : (h + 1) * VDIM] = mm(first, uv_ref[h]).astype(bf16)
        out_ref[:, (h + 1) * VDIM : (h + 2) * VDIM] = mm(second, uv_ref[h + 1]).astype(bf16)


def tile_of(width):
    return 256 if width % 256 == 0 else width


def half_product_kernel(count, *refs):
    w_ref, *value_refs, out_ref = refs
    rows = jnp.concatenate([ref[...] for ref in value_refs[:count]], axis=0)
    tile = tile_of(w_ref.shape[1])
    for at in range(0, w_ref.shape[1], tile):
        out_ref[:, at : at + tile] = mm(rows, w_ref[:, at : at + tile])


def half_product(weights, pieces, params):
    return pl.pallas_call(
        functools.partial(half_product_kernel, len(pieces)),
        out_shape=jax.ShapeDtypeStruct((len(pieces) * pieces[0].shape[0], weights.shape[1]), f32),
        in_specs=[vmem_spec()] * (1 + len(pieces)),
        out_specs=vmem_spec(),
        compiler_params=params,
        name="half_product",
    )(weights, *pieces)


def output_kernel(done, place_ref, w_ref, partial_ref, *refs):
    ready_refs, value_refs, out_ref = refs[:done], refs[done:-1], refs[-1]
    rows = out_ref.shape[1]
    other = jnp.concatenate([ref[...] for ref in value_refs], axis=0)
    base = place_ref[1] if done else 0
    for k in range(done):
        out_ref[base ^ k] = ready_refs[k][0]
    part = (partial_ref[...] + mm(other, w_ref[...])).astype(bf16)
    for k in range(len(value_refs)):
        out_ref[base ^ (done + k)] = part[k * rows : (k + 1) * rows]


def output_rows(ready, blocks, place, weights, partial, other, params):
    operands = [place, weights, partial, *ready, *other]
    shape = (blocks, other[0].shape[0], weights.shape[1])
    return pl.pallas_call(
        functools.partial(output_kernel, len(ready)),
        out_shape=jax.ShapeDtypeStruct(shape, bf16),
        in_specs=[smem_spec()] + [vmem_spec()] * (len(operands) - 1),
        out_specs=vmem_spec(),
        compiler_params=params,
        name="output",
    )(*operands)


def sum_kernel(replicas, pairs, x_ref, out_ref):
    width = x_ref.shape[-1]
    for r in range(replicas):
        for c in range(2):
            total = None
            for p in range(pairs):
                part = x_ref[(r * pairs + p) * 2 + c].astype(f32)
                total = part if total is None else total + part
            at = (r * 2 + c) * width
            out_ref[:, at : at + width] = total.astype(bf16)


def step(x, axis, size, k):
    return lax.ppermute(x, axis, [(i, i ^ k) for i in range(size)])


def local_step(q_latent, q_gain, q_up, w_uk, w_uv, w_o, new_kv, latent_cache, cache_len, draft_count):
    rows_dev, _ = q_latent.shape
    owners = lax.axis_size("tensor")
    replicas = lax.axis_size("replica")
    heads = w_uk.shape[0]
    reqs = cache_len.shape[0]
    drafts = rows_dev // reqs
    hd = heads * drafts
    me = lax.axis_index("tensor")
    core = me % 2

    place = jnp.stack([core, lax.axis_index("replica"), me]).astype(jnp.int32)
    w_uk = w_uk.reshape(heads * NOPE, LATENT)
    near = fetch((q_up, w_uk, q_gain, q_latent), FETCH_VMEM)

    lane_pair = jnp.arange(LANES) % (ROPE // 2)
    frequency = (rope_base ** (-(lane_pair.astype(f32) * 2.0 / ROPE)))[None, :]

    first = step(q_latent, "tensor", owners, owners // 2)
    first, q_up, w_uk, gain, rows, frequency = lax.optimization_barrier((first, *near, frequency))
    rows = jnp.concatenate([rows, first], axis=0)
    bit = owners // 4
    while bit > 4:
        rows = jnp.concatenate([rows, step(rows, "tensor", owners, bit)], axis=0)
        bit //= 2
    parts = [rows]
    if bit == 4:
        parts = parts + [step(rows, "tensor", owners, k) for k in (4, 2, 6)]
        bit = 1
    while bit:
        parts = parts + [step(part, "tensor", owners, bit) for part in parts]
        bit //= 2

    chunks = LATENT // LANES
    packed = (reqs * chunks + reqs * ROPE // LANES) * hd
    params = pltpu.CompilerParams(vmem_limit_bytes=24 * 1024 * 1024)
    queries = pl.pallas_call(
        functools.partial(query_kernel, reqs, drafts, heads),
        out_shape=jax.ShapeDtypeStruct((owners, packed, LANES), bf16),
        in_specs=[smem_spec()] + [vmem_spec()] * (len(parts) + 3),
        out_specs=vmem_spec(),
        compiler_params=params,
        name="query",
    )(place, *parts, gain, q_up, w_uk)
    arrived = lax.all_to_all(queries, "tensor", split_axis=0, concat_axis=0, tiled=True)

    arrived, w_late = lax.optimization_barrier((arrived, w_o))

    half = w_o.shape[1] // 2
    aligned = half % LANES == 0
    w_own = w_o if aligned else lax.dynamic_slice_in_dim(w_o, core * half, half, axis=1)
    w_away = w_late if aligned else lax.dynamic_slice_in_dim(w_late, (1 - core) * half, half, axis=1)
    w_other = step(w_away, "tensor", owners, 1)

    latent = pl.pallas_call(
        functools.partial(attend_kernel, reqs, drafts, heads),
        out_shape=jax.ShapeDtypeStruct((owners, reqs * hd, LATENT), bf16),
        in_specs=[smem_spec()] * 2 + [vmem_spec()] * 4,
        out_specs=vmem_spec(),
        compiler_params=params,
        name="attend",
    )(cache_len, draft_count, arrived, frequency, new_kv, jnp.swapaxes(latent_cache, 1, 2))
    returned = lax.all_to_all(latent, "tensor", split_axis=0, concat_axis=0, tiled=True)
    returned, w_other = lax.optimization_barrier((returned, w_other))

    values = pl.pallas_call(
        functools.partial(value_kernel, drafts, heads),
        out_shape=jax.ShapeDtypeStruct((owners * rows_dev, heads * VDIM), bf16),
        in_specs=[vmem_spec()] * 2,
        out_specs=vmem_spec(),
        compiler_params=params,
        name="values",
    )(returned, w_uv)
    nearest = step(values, "replica", replicas, 1)
    own = [values, nearest] + [step(values, "replica", replicas, k) for k in range(2, replicas)]
    w_own, w_other = fetch_halves(place, (w_own, w_other), half)
    other = [step(own[0], "tensor", owners, 1)]
    product = half_product(w_own, own[:1], params)
    product = output_rows((), 1, place, w_other, product, other, params)
    if replicas > 1:
        other = [step(own[1], "tensor", owners, 1)]
        other = other + [step(piece, "tensor", owners, 1) for piece in own[2:]]
        partial = half_product(w_own, own[1:], params)
        product = output_rows((product,), replicas, place, w_other, partial, other, params)
    product = product.reshape(replicas * owners, rows_dev, half)
    placed = lax.all_to_all(product, ("replica", "tensor"), split_axis=0, concat_axis=0, tiled=True)
    return pl.pallas_call(
        functools.partial(sum_kernel, replicas, owners // 2),
        out_shape=jax.ShapeDtypeStruct((rows_dev, replicas * 2 * half), bf16),
        in_specs=[vmem_spec()],
        out_specs=vmem_spec(),
        compiler_params=params,
        name="combine",
    )(placed)


def solution(mesh):
    rows = ("groups", "tensor", "replica")
    return jax.shard_map(
        local_step,
        mesh=mesh,
        in_specs=(
            P(rows, None),
            P(),
            P(None, "tensor"),
            P("tensor", None, None),
            P("tensor", None, None),
            P("tensor", "replica"),
            P(rows, None),
            P(rows, None, None),
            P(rows),
            P(rows),
        ),
        out_specs=P(rows, None),
        check_vma=False,
    )
```

```python
import functools
import math

import jax
import jax.numpy as jnp
from jax import lax
from jax.experimental import pallas as pl
from jax.experimental.pallas import tpu as pltpu
from jax.sharding import PartitionSpec as P


LATENT = 512
ROPE = 64
NOPE = 128
VDIM = 128
QKD = NOPE + ROPE
LANES = 128

FETCH_VMEM = 53_700_000
HALVES_VMEM = 51_000_000

rms_eps = 1e-06
rope_base = 50000.0

VMEM = pltpu.MemorySpace.VMEM
SMEM = pltpu.MemorySpace.SMEM
bf16 = jnp.bfloat16
f32 = jnp.float32


def vmem_spec():
    return pl.BlockSpec(memory_space=VMEM)


def smem_spec():
    return pl.BlockSpec(memory_space=SMEM)


def over(x, n):
    return x >> (n.bit_length() - 1) if n & (n - 1) == 0 else x // n


def rest(x, n):
    return x & (n - 1) if n & (n - 1) == 0 else x % n


def mm(a, b):
    return jnp.dot(a, b, preferred_element_type=f32)


def mm_nt(a, b):
    return lax.dot_general(a, b, (((1,), (1,)), ((), ())), preferred_element_type=f32)


def fetch_kernel(*refs):
    count = len(refs) // 2
    copies = [pltpu.make_async_copy(refs[i], refs[count + i], refs[-1].at[i]) for i in range(count)]
    for copy in copies:
        copy.start()
    for copy in copies:
        copy.wait()


def fetch(arrays, limit):
    return pl.pallas_call(
        fetch_kernel,
        out_shape=[pltpu.VMEM(x.shape, x.dtype) for x in arrays],
        in_specs=[pl.BlockSpec(memory_space=pl.ANY)] * len(arrays),
        out_specs=[vmem_spec()] * len(arrays),
        scratch_shapes=[pltpu.SemaphoreType.DMA((len(arrays),))],
        compiler_params=pltpu.CompilerParams(vmem_limit_bytes=limit),
        cost_estimate=pl.CostEstimate(
            flops=0, bytes_accessed=sum(4 * x.size for x in arrays), transcendentals=0
        ),
    )(*arrays)


def halves_kernel(place_ref, *refs):
    *sources, first, second, sems = refs
    copies = []
    for i, target in enumerate((first, second)):
        source, width = sources[i], target.shape[1]
        if source.shape[1] != width:
            source = source.at[:, pl.ds(pl.multiple_of(place_ref[0] * width, LANES), width)]
        copies.append(pltpu.make_async_copy(source, target, sems.at[i]))
        copies[i].start()
    for copy in copies:
        copy.wait()


def fetch_halves(place, arrays, width):
    depth = arrays[0].shape[0]
    return pl.pallas_call(
        halves_kernel,
        out_shape=[pltpu.VMEM((depth, width), bf16)] * 2,
        in_specs=[smem_spec()] + [pl.BlockSpec(memory_space=pl.ANY)] * 2,
        out_specs=[vmem_spec()] * 2,
        scratch_shapes=[pltpu.SemaphoreType.DMA((2,))],
        compiler_params=pltpu.CompilerParams(vmem_limit_bytes=HALVES_VMEM),
        cost_estimate=pl.CostEstimate(flops=0, bytes_accessed=8 * depth * width, transcendentals=0),
        name="near_output",
    )(place, *arrays)


def regroup(pieces, groups, size):
    assert groups == 2 and len(pieces) % 2 == 0
    rows = lax.broadcasted_iota(jnp.int32, pieces[0].shape, 0)
    low = rest(over(rows, size), 2) == 0
    total = pieces[0].shape[0]
    width = pieces[0].shape[1]
    firsts, seconds = [], []
    for h in range(0, len(pieces), 2):
        a, b = pieces[h], pieces[h + 1]
        firsts.append(jnp.where(low, a, pltpu.roll(b, size, 0)))
        seconds.append(jnp.where(low, pltpu.roll(a, total - size, 0), b))

    def stack(parts):
        parts = [part.reshape(total // (2 * size), 2 * size, width) for part in parts]
        return jnp.concatenate(parts, axis=1).reshape(total * len(parts), width)

    return [stack(firsts), stack(seconds)]


def query_kernel(reqs, drafts, heads, *refs):
    *x_refs, gain_ref, up_ref, uk_ref, out_ref = refs
    owners = out_ref.shape[0]
    me = lax.axis_index("tensor")
    hd = heads * drafts
    x = jnp.concatenate([x_ref[...] for x_ref in x_refs], axis=0).astype(f32)
    scaled = x * lax.rsqrt(jnp.mean(x * x, axis=-1, keepdims=True) + rms_eps)
    normed = (scaled * gain_ref[...][None, :]).astype(bf16)
    full = mm(normed, up_ref[...]).astype(bf16)
    absorbed = [mm(full[:, h * QKD : h * QKD + NOPE], uk_ref[h * NOPE : (h + 1) * NOPE]) for h in range(heads)]
    rope = [full[:, h * QKD + NOPE : (h + 1) * QKD].astype(f32) for h in range(heads)]
    absorbed = regroup(absorbed, reqs, drafts)
    rope = regroup(rope, reqs, drafts)
    chunks = LATENT // LANES
    per = LANES // ROPE
    absorbed = [x.reshape(owners, hd, LATENT).astype(bf16) for x in absorbed]
    rope = [
        jnp.concatenate(rope[b * per : (b + 1) * per], axis=-1).reshape(owners, hd, LANES).astype(bf16)
        for b in range(reqs // per)
    ]
    for k in range(owners):
        distance = int(format(k, f"0{owners.bit_length() - 1}b")[::-1], 2)
        target = me ^ distance
        for q in range(reqs):
            for c in range(chunks):
                at = (q * chunks + c) * hd
                out_ref[target, at : at + hd, :] = absorbed[q][k, :, c * LANES : (c + 1) * LANES]
        for b in range(reqs // per):
            at = (reqs * chunks + b) * hd
            out_ref[target, at : at + hd, :] = rope[b][k]


def attend_kernel(reqs, drafts, heads, len_ref, count_ref, q_ref, frequency_ref, new_ref, cache_ref, out_ref):
    owners = q_ref.shape[0]
    hd = heads * drafts
    count = owners * hd
    chunks = LATENT // LANES
    per = LANES // ROPE
    slots = cache_ref.shape[2]
    scale = QKD ** (-0.5) * math.log2(math.e)
    rotated = []
    for b in range(reqs // per):
        at = (reqs * chunks + b) * hd
        x = q_ref[:, at : at + hd, :].astype(f32).reshape(count, LANES)
        half = ROPE // 2
        low = rest(lax.broadcasted_iota(jnp.int32, x.shape, 1), ROPE) < half
        other = jnp.where(low, pltpu.roll(x, LANES - half, 1), pltpu.roll(x, half, 1))
        lane = lax.broadcasted_iota(jnp.int32, (hd, LANES), 1)
        length = jnp.zeros_like(lane)
        for i in range(per):
            length = jnp.where(over(lane, ROPE) == i, len_ref[b * per + i], length)
        position = length + rest(lax.broadcasted_iota(jnp.int32, (hd, LANES), 0), drafts)
        angle = position.astype(f32) * frequency_ref[...]
        sine = jnp.sin(angle)
        sine = jnp.where(rest(lane, ROPE) < half, -sine, sine)
        x = x.reshape(owners, hd, LANES) * jnp.cos(angle) + other.reshape(owners, hd, LANES) * sine
        x = x.astype(bf16).reshape(count, LANES)
        rotated += [x[:, i * ROPE : (i + 1) * ROPE] for i in range(per)]
    draft = rest(lax.broadcasted_iota(jnp.int32, (count, 1), 0), drafts)
    new_at = lax.broadcasted_iota(jnp.int32, (count, new_ref.shape[0]), 1)
    slot = lax.broadcasted_iota(jnp.int32, (1, slots), 1)
    for q in range(reqs):
        absorbed = jnp.concatenate(
            [
                q_ref[:, (q * chunks + c) * hd : (q * chunks + c + 1) * hd, :].reshape(count, LANES)
                for c in range(chunks)
            ],
            axis=-1,
        )
        keys = cache_ref[q]
        rows = new_ref[...]
        score = mm(absorbed, keys[:LATENT]) + mm(rotated[q], keys[LATENT:])
        fresh = mm_nt(absorbed, rows[:, :LATENT]) + mm_nt(rotated[q], rows[:, LATENT:])
        score = jnp.where(slot < len_ref[q], score, -jnp.inf)
        seen = (new_at >= q * drafts) & (new_at - q * drafts <= draft)
        fresh = jnp.where(seen, fresh, -jnp.inf)
        peak = jnp.maximum(
            jnp.max(score, axis=1, keepdims=True), jnp.max(fresh, axis=1, keepdims=True)
        )
        score = jnp.exp2((score - peak) * scale)
        fresh = jnp.exp2((fresh - peak) * scale)
        total = jnp.sum(score, axis=1, keepdims=True) + jnp.sum(fresh, axis=1, keepdims=True)
        mix = mm_nt(score.astype(bf16), keys[:LATENT]) + mm(fresh.astype(bf16), rows[:, :LATENT])
        mix = jnp.where(draft < count_ref[q], mix * (1.0 / total), 0.0).astype(bf16)
        out_ref[:, q * hd : (q + 1) * hd, :] = mix.reshape(owners, hd, LATENT)


def value_kernel(drafts, heads, latent_ref, uv_ref, out_ref):
    owners = latent_ref.shape[0]
    hd = heads * drafts
    pair = 2 * drafts
    rows = owners * pair
    low = rest(over(lax.broadcasted_iota(jnp.int32, (rows, LATENT), 0), drafts), 2) == 0
    for h in range(0, heads, 2):
        a = latent_ref[:, h * drafts : h * drafts + pair, :].astype(f32).reshape(rows, LATENT)
        b = latent_ref[:, hd + h * drafts : hd + h * drafts + pair, :].astype(f32).reshape(rows, LATENT)
        first = jnp.where(low, a, pltpu.roll(b, drafts, 0)).astype(bf16)
        second = jnp.where(low, pltpu.roll(a, rows - drafts, 0), b).astype(bf16)
        out_ref[:, h * VDIM : (h + 1) * VDIM] = mm(first, uv_ref[h]).astype(bf16)
        out_ref[:, (h + 1) * VDIM : (h + 2) * VDIM] = mm(second, uv_ref[h + 1]).astype(bf16)


def tile_of(width):
    return 256 if width % 256 == 0 else width


def half_product_kernel(count, *refs):
    w_ref, *value_refs, out_ref = refs
    rows = jnp.concatenate([ref[...] for ref in value_refs[:count]], axis=0)
    tile = tile_of(w_ref.shape[1])
    for at in range(0, w_ref.shape[1], tile):
        out_ref[:, at : at + tile] = mm(rows, w_ref[:, at : at + tile])


def half_product(weights, pieces, params):
    return pl.pallas_call(
        functools.partial(half_product_kernel, len(pieces)),
        out_shape=jax.ShapeDtypeStruct((len(pieces) * pieces[0].shape[0], weights.shape[1]), f32),
        in_specs=[vmem_spec()] * (1 + len(pieces)),
        out_specs=vmem_spec(),
        compiler_params=params,
        name="half_product",
    )(weights, *pieces)


def output_kernel(done, w_ref, partial_ref, *refs):
    ready_refs, value_refs, out_ref = refs[:done], refs[done:-1], refs[-1]
    rows = out_ref.shape[1]
    other = jnp.concatenate([ref[...] for ref in value_refs], axis=0)
    base = lax.axis_index("replica") if done else 0
    for k in range(done):
        out_ref[base ^ k] = ready_refs[k][0]
    part = (partial_ref[...] + mm(other, w_ref[...])).astype(bf16)
    for k in range(len(value_refs)):
        out_ref[base ^ (done + k)] = part[k * rows : (k + 1) * rows]


def output_rows(ready, blocks, weights, partial, other, params):
    operands = [weights, partial, *ready, *other]
    shape = (blocks, other[0].shape[0], weights.shape[1])
    return pl.pallas_call(
        functools.partial(output_kernel, len(ready)),
        out_shape=jax.ShapeDtypeStruct(shape, bf16),
        in_specs=[vmem_spec()] * len(operands),
        out_specs=vmem_spec(),
        compiler_params=params,
        name="output",
    )(*operands)


def sum_kernel(replicas, pairs, x_ref, out_ref):
    width = x_ref.shape[-1]
    for r in range(replicas):
        for c in range(2):
            total = None
            for p in range(pairs):
                part = x_ref[(r * pairs + p) * 2 + c].astype(f32)
                total = part if total is None else total + part
            at = (r * 2 + c) * width
            out_ref[:, at : at + width] = total.astype(bf16)


def step(x, axis, size, k):
    return lax.ppermute(x, axis, [(i, i ^ k) for i in range(size)])


def local_step(q_latent, q_gain, q_up, w_uk, w_uv, w_o, new_kv, latent_cache, cache_len, draft_count):
    rows_dev, _ = q_latent.shape
    owners = lax.axis_size("tensor")
    replicas = lax.axis_size("replica")
    heads = w_uk.shape[0]
    reqs = cache_len.shape[0]
    drafts = rows_dev // reqs
    hd = heads * drafts
    me = lax.axis_index("tensor")
    core = me % 2

    place = core[None].astype(jnp.int32)
    w_uk = w_uk.reshape(heads * NOPE, LATENT)
    near = fetch((q_up, w_uk, q_gain, q_latent), FETCH_VMEM)

    lane_pair = jnp.arange(LANES) % (ROPE // 2)
    frequency = (rope_base ** (-(lane_pair.astype(f32) * 2.0 / ROPE)))[None, :]

    first = step(q_latent, "tensor", owners, owners // 2)
    first, q_up, w_uk, gain, rows, frequency = lax.optimization_barrier((first, *near, frequency))
    rows = jnp.concatenate([rows, first], axis=0)
    bit = owners // 4
    while bit > 4:
        rows = jnp.concatenate([rows, step(rows, "tensor", owners, bit)], axis=0)
        bit //= 2
    parts = [rows]
    if bit == 4:
        parts = parts + [step(rows, "tensor", owners, k) for k in (4, 2, 6)]
        bit = 1
    while bit:
        parts = parts + [step(part, "tensor", owners, bit) for part in parts]
        bit //= 2

    chunks = LATENT // LANES
    packed = (reqs * chunks + reqs * ROPE // LANES) * hd
    params = pltpu.CompilerParams(vmem_limit_bytes=24 * 1024 * 1024)
    queries = pl.pallas_call(
        functools.partial(query_kernel, reqs, drafts, heads),
        out_shape=jax.ShapeDtypeStruct((owners, packed, LANES), bf16),
        in_specs=[vmem_spec()] * (len(parts) + 3),
        out_specs=vmem_spec(),
        compiler_params=params,
        name="query",
    )(*parts, gain, q_up, w_uk)
    arrived = lax.all_to_all(queries, "tensor", split_axis=0, concat_axis=0, tiled=True)

    arrived, w_late = lax.optimization_barrier((arrived, w_o))

    half = w_o.shape[1] // 2
    aligned = half % LANES == 0
    w_own = w_o if aligned else lax.dynamic_slice_in_dim(w_o, core * half, half, axis=1)
    w_away = w_late if aligned else lax.dynamic_slice_in_dim(w_late, (1 - core) * half, half, axis=1)
    w_other = step(w_away, "tensor", owners, 1)

    latent = pl.pallas_call(
        functools.partial(attend_kernel, reqs, drafts, heads),
        out_shape=jax.ShapeDtypeStruct((owners, reqs * hd, LATENT), bf16),
        in_specs=[smem_spec()] * 2 + [vmem_spec()] * 4,
        out_specs=vmem_spec(),
        compiler_params=params,
        name="attend",
    )(cache_len, draft_count, arrived, frequency, new_kv, jnp.swapaxes(latent_cache, 1, 2))
    returned = lax.all_to_all(latent, "tensor", split_axis=0, concat_axis=0, tiled=True)
    returned, w_other = lax.optimization_barrier((returned, w_other))

    values = pl.pallas_call(
        functools.partial(value_kernel, drafts, heads),
        out_shape=jax.ShapeDtypeStruct((owners * rows_dev, heads * VDIM), bf16),
        in_specs=[vmem_spec()] * 2,
        out_specs=vmem_spec(),
        compiler_params=params,
        name="values",
    )(returned, w_uv)
    nearest = step(values, "replica", replicas, 1)
    own = [values, nearest] + [step(values, "replica", replicas, k) for k in range(2, replicas)]
    w_own, w_other = fetch_halves(place, (w_own, w_other), half)
    other = [step(own[0], "tensor", owners, 1)]
    product = half_product(w_own, own[:1], params)
    product = output_rows((), 1, w_other, product, other, params)
    if replicas > 1:
        other = [step(own[1], "tensor", owners, 1)]
        other = other + [step(piece, "tensor", owners, 1) for piece in own[2:]]
        partial = half_product(w_own, own[1:], params)
        product = output_rows((product,), replicas, w_other, partial, other, params)
    product = product.reshape(replicas * owners, rows_dev, half)
    placed = lax.all_to_all(product, ("replica", "tensor"), split_axis=0, concat_axis=0, tiled=True)
    return pl.pallas_call(
        functools.partial(sum_kernel, replicas, owners // 2),
        out_shape=jax.ShapeDtypeStruct((rows_dev, replicas * 2 * half), bf16),
        in_specs=[vmem_spec()],
        out_specs=vmem_spec(),
        compiler_params=params,
        name="combine",
    )(placed)


def solution(mesh):
    rows = ("groups", "tensor", "replica")
    return jax.shard_map(
        local_step,
        mesh=mesh,
        in_specs=(
            P(rows, None),
            P(),
            P(None, "tensor"),
            P("tensor", None, None),
            P("tensor", None, None),
            P("tensor", "replica"),
            P(rows, None),
            P(rows, None, None),
            P(rows),
            P(rows),
        ),
        out_specs=P(rows, None),
        check_vma=False,
    )
```
